32 devices in a mesh: level: 4 (over y, x), blk: 8 (over z, core).
Axes of the slice: x: 2, y: 2, z: 4, core: 2. Of those that a mesh axis runs over, the one named last changes fastest.
Arguments:
- right_sides: float32 [4, 512, 2048], P('level', None, 'blk'), may hold values from -6 to 6
- leaf_gen: float32 [4, 2048, 256], P('level', 'blk'), may hold values from -1 to 1, as said below
- leaf_inverse: float32 [4, 1024, 128], P('level', 'blk'), may hold values from -0.5 to 0.5
- leaf_lower: float32 [4, 1024, 128], P('level', 'blk'), may hold values from -0.5 to 0.5
- node_gen: float32 [4, 8, 3, 256, 256], P('level', 'blk'), may hold values from -1 to 1, as said below
- node_inverse: float32 [4, 8, 3, 128, 128], P('level', 'blk'), may hold values from -1 to 1, as said below
- node_lower: float32 [4, 8, 3, 128, 128], P('level', 'blk'), may hold values from -1 to 1, as said below
- coupling: float32 [4, 128, 256], P('level'), may hold values from -0.5 to 0.5
- child_leaf: int32 [4], P('level'), may hold values from 0 to 7
Outputs:
- leaf_solution: float32 [4, 512, 1024], P('level', None, 'blk')
- node_solution: float32 [4, 8, 3, 512, 128], P('level', 'blk')
- root_skeleton: float32 [4, 512, 128], P('level')
The draws below stay inside these ranges and needn't reach their ends.
Inputs may be any that keep to these rules, and one draw needn't show every extreme that they name: `leaf_gen`: each leaf's 256 x 256 block is orthogonal. node_gen[p, i, h] is orthogonal and equal for all leaves i with the same i >> (h + 1). node_inverse[p, i, h] is equal for all leaves i with the same i >> (h + 1). node_lower[p, i, h] is equal for all leaves i with the same i >> (h + 1).
All inputs are finite; a program needn't handle non-finite values.
Results may differ from the reference program's by a relative error of at most 0.0003.
Values sent between devices are 32-bit elements; how exact they have to be, the bound alone decides.
No kernel may reach another device: no remote copies, remote signals or barrier semaphores. Data moves between devices by JAX's collectives and lax.ppermute only.
A program may use at most 64 MiB of HBM per device.

```python
import jax
import jax.numpy as jnp
from jax import lax

LEAF = 256
R = 128
NRHS = 512
RED = 128
LEAVES = 8
LEVELS = 4
FRONT = 2048
HEIGHT = 3


def orthogonal_stack(key, array_shape):
    values = jax.random.normal(key, array_shape, jnp.float32)
    factor, upper_part = jnp.linalg.qr(values)
    return factor


def node_draw(key, row_count, col_count, draw_kind, spread_factor):
    layers = []
    for tier_index in range(HEIGHT):
        group_span = 2 ** (tier_index + 1)
        array_shape = (LEVELS, LEAVES // group_span, row_count, col_count)
        subkey = jax.random.fold_in(key, 17 + tier_index)
        if draw_kind == 0:
            values = orthogonal_stack(subkey, array_shape)
        else:
            values = jax.random.truncated_normal(subkey, -4.0, 4.0, array_shape, jnp.float32) * spread_factor
        layers.append(jnp.repeat(values, group_span, axis=1))
    return jnp.stack(layers, axis=2)


def draw_leaf_gen(key, part):
    values = orthogonal_stack(jax.random.fold_in(key, 3), (LEVELS, LEAVES, LEAF, LEAF))
    return values.reshape(LEVELS, LEAVES * LEAF, LEAF)


def draw_node_gen(key, part):
    return node_draw(jax.random.fold_in(key, 5), 2 * R, 2 * R, 0, 1.0)


def draw_node_inverse(key, part):
    return node_draw(jax.random.fold_in(key, 7), R, R, 1, R ** (-0.5))


def draw_node_lower(key, part):
    return node_draw(jax.random.fold_in(key, 11), R, R, 1, 0.5 * R ** (-0.5))


def plant(entries, rng, smallest, high):
    spot = [jax.random.randint(jax.random.fold_in(rng, axis), (), 0, length) for axis, length in enumerate(entries.shape)]
    main_axis = entries.shape.index(max(entries.shape))
    beside = spot[:main_axis] + [(spot[main_axis] + 1) % entries.shape[main_axis]] + spot[main_axis + 1:]
    return entries.at[tuple(spot)].set(smallest).at[tuple(beside)].set(high)


def block_levels(own_key, shape, cuts, least, high):
    loudness, own = 1.0, jax.random.fold_in(own_key, 6)
    for position, shards_of in cuts:
        steps = jnp.exp(jax.random.uniform(jax.random.fold_in(own, position), (shards_of,), jnp.float32, least / len(cuts), high / len(cuts)))
        loudness = loudness * jnp.repeat(steps, shape[position] // shards_of).reshape([-1 if axis == position else 1 for axis in range(len(shape))])
    return loudness


def gaussian(key, extent, deviation, limit, cuts=(), dtype=jnp.bfloat16):
    array = deviation * jax.random.normal(key, extent, jnp.float32)
    if cuts:
        array = array * block_levels(key, extent, cuts, -0.22, 0.18)
    return jnp.clip(array, -limit, limit).astype(dtype)


def setup_inputs(seed: int = 0) -> dict:
    arg_keys = jax.random.split(jax.random.key(seed), 10)
    return {
        "right_sides": gaussian(arg_keys[0], (LEVELS, NRHS, FRONT), 1.0, 6.0, ((0, 4), (2, 8)), jnp.float32),
        "leaf_gen": draw_leaf_gen(jax.random.fold_in(arg_keys[9], 71), 0),
        "leaf_inverse": gaussian(arg_keys[2], (LEVELS, LEAVES * RED, RED), RED ** -0.5, 0.5, ((0, 4), (1, 8)), jnp.float32),
        "leaf_lower": gaussian(arg_keys[3], (LEVELS, LEAVES * RED, R), RED ** -0.5, 0.5, ((0, 4), (1, 8)), jnp.float32),
        "node_gen": draw_node_gen(jax.random.fold_in(arg_keys[9], 71), 0),
        "node_inverse": draw_node_inverse(jax.random.fold_in(arg_keys[9], 71), 0),
        "node_lower": draw_node_lower(jax.random.fold_in(arg_keys[9], 71), 0),
        "coupling": gaussian(arg_keys[7], (LEVELS, R, LEAF), R ** -0.5, 0.5, ((0, 4),), jnp.float32),
        "child_leaf": plant(jax.random.randint(arg_keys[8], (LEVELS,), 0, LEAVES), jax.random.fold_in(arg_keys[8], 1), 0, LEAVES - 1).astype(jnp.int32),
    }


exact_mode = lax.Precision.HIGHEST

def product(left, right):
    return jnp.matmul(left.astype(jnp.float32), right.astype(jnp.float32), precision=exact_mode)

def reference(right_sides, leaf_gen, leaf_inverse, leaf_lower, node_gen, node_inverse, node_lower, coupling, child_leaf):
    leaf_list = []
    node_list = []
    root_list = []
    incoming = jnp.zeros((NRHS, R), jnp.float32)
    for depth_index in range(LEVELS):
        update = product(incoming, coupling[depth_index])
        row_start = (child_leaf[depth_index] * LEAF).astype(jnp.int32)
        front_rhs = right_sides[depth_index]
        leaf_block = lax.dynamic_slice_in_dim(front_rhs, row_start, LEAF, 1)
        front_rhs = lax.dynamic_update_slice_in_dim(front_rhs, leaf_block + update, row_start, 1)
        pieces = front_rhs.reshape(NRHS, LEAVES, LEAF).transpose(1, 0, 2)
        turned = product(pieces, leaf_gen[depth_index].reshape(LEAVES, LEAF, LEAF))
        solved = product(turned[:, :, :RED], leaf_inverse[depth_index].reshape(LEAVES, RED, RED))
        skeleton = turned[:, :, RED:] - product(solved, leaf_lower[depth_index].reshape(LEAVES, RED, R))
        leaf_list.append(solved.transpose(1, 0, 2).reshape(NRHS, LEAVES * RED))
        per_tier = []
        for tier_index in range(HEIGHT):
            group_span = 2 ** (tier_index + 1)
            joined = jnp.concatenate([skeleton[0::2], skeleton[1::2]], axis=2)
            turned = product(joined, node_gen[depth_index, ::group_span, tier_index])
            solved = product(turned[:, :, :R], node_inverse[depth_index, ::group_span, tier_index])
            skeleton = turned[:, :, R:] - product(solved, node_lower[depth_index, ::group_span, tier_index])
            per_tier.append(jnp.repeat(solved, group_span, axis=0))
        node_list.append(jnp.stack(per_tier, axis=1))
        incoming = skeleton[0]
        root_list.append(incoming)
    return (jnp.stack(leaf_list), jnp.stack(node_list), jnp.stack(root_list))
```

```python
import functools

import jax
import jax.numpy as jnp
from jax import lax
from jax.experimental import pallas as pl
from jax.experimental.pallas import tpu as pltpu
from jax.sharding import PartitionSpec as P


f32 = jnp.float32
bf16 = jnp.bfloat16
VMEM = pltpu.VMEM
SMEM = pltpu.SMEM


def split(value):
    high = value.astype(bf16)
    return high, (value - high.astype(f32)).astype(bf16)


def narrow_dot(left, right):
    return jnp.dot(left, right, preferred_element_type=f32)


def split_dot(left, right):
    left_high, left_low = left
    right_high, right_low = right
    return narrow_dot(left_high, right_high) + (
        narrow_dot(left_high, right_low) + narrow_dot(left_low, right_high)
    )


def product(left, right):
    return split_dot(split(left), split(right))


def call(kernel, out_shape, args, flops, name, in_specs=None, scratch_shapes=(), out_specs=None):
    size = lambda s: s.size * s.dtype.itemsize
    outs = jax.tree.leaves(out_shape)
    specs = dict(in_specs=in_specs or [pl.BlockSpec(memory_space=VMEM)] * len(args))
    if out_specs is not None:
        specs["out_specs"] = out_specs
    else:
        specs["out_specs"] = jax.tree.map(lambda _: pl.BlockSpec(memory_space=VMEM), out_shape)
    return pl.pallas_call(
        kernel,
        out_shape=out_shape,
        scratch_shapes=scratch_shapes,
        name=name,
        cost_estimate=pl.CostEstimate(
            flops=flops,
            bytes_accessed=sum(size(a) for a in args) + sum(size(o) for o in outs),
            transcendentals=0,
        ),
        **specs,
    )(*args)


def fold(generator, inverse, lower):
    size = inverse.shape[0]
    solve_map = product(generator[:, :size], inverse)
    return solve_map, generator[:, size:] - product(solve_map, lower)


def leaf_kernel(flag, right, generator, inverse, lower, coupling, away, home, solve_map):
    core = flag[1]
    half, k_half = right.shape[0] // 2, coupling.shape[0] // 2
    solved, skeleton = fold(generator[...], inverse[...], lower[...])
    solve_map[...] = solved
    parts = split(skeleton)
    on_target = flag[0] == 1

    def one(which, out):
        rows = pl.ds(pl.multiple_of(which * half, 8), half)
        k_rows = pl.ds(pl.multiple_of(which * k_half, 8), k_half)
        out[:half, :] = split_dot(split(right[rows, :]), parts)
        lifted = jnp.where(on_target, coupling[k_rows, :], 0.0)
        out[half:, :] = split_dot(split(lifted), parts)

    one(1 - core, away)
    one(core, home)


def leaf_solve_kernel(flag, right, coupling, solve_map, solved, leaf_map):
    parts = split(solve_map[...])
    solved[...] = split_dot(split(right[...]), parts)
    leaf_map[...] = split_dot(split(jnp.where(flag[0] == 1, coupling[...], 0.0)), parts)


def fold_kernel(generator, inverse, lower, solve_map, skeleton_map):
    for tier in range(generator.shape[0]):
        solve_map[tier], skeleton_map[tier] = fold(generator[tier], inverse[tier], lower[tier])


def merge_kernel(tier, flag, home, away, tier_map, out):
    size = home.shape[1]
    upper = (flag[2] >> tier) & 1
    mine = tier_map[pl.ds(pl.multiple_of(upper * size, 8), size), :]
    other = tier_map[pl.ds(pl.multiple_of((1 - upper) * size, 8), size), :]
    out[...] = product(home[...], mine) + product(away[...], other)


def final_kernel(
    fronts, height, flag, solved, leaf_map, *refs
):
    nodes, refs = refs[: 2 * height], refs[2 * height :]
    roots, refs = refs[: 2 * fronts], refs[2 * fronts :]
    leaf_out, node_out, root_out, maps, root_maps, incoming = refs
    core, level = flag[1], flag[3]
    half = solved.shape[0] // 2
    size = solved.shape[1]
    k_half = leaf_map.shape[0] // 2
    mine = pl.ds(pl.multiple_of(core * k_half, 8), k_half)
    other = pl.ds(pl.multiple_of((1 - core) * k_half, 8), k_half)
    maps[:, :size] = leaf_map[...]
    for tier in range(height):
        columns = slice((tier + 1) * size, (tier + 2) * size)
        maps[mine, columns] = nodes[2 * tier][half:, :]
        maps[other, columns] = nodes[2 * tier + 1][half:, :]
    for front in range(fronts):
        root_maps[front, mine, :] = roots[2 * front][half:, :]
        root_maps[front, other, :] = roots[2 * front + 1][half:, :]
    maps[:, (height + 1) * size :] = root_maps[0]

    @pl.when(level == 0)
    def _():
        incoming[...] = jnp.zeros_like(incoming)

    for here in range(1, fronts):

        @pl.when(level == here)
        def _():
            for part in range(2):
                value = roots[2 * here + part][:half, :]
                for front in range(1, here):
                    value = roots[2 * (here ^ front) + part][:half, :] + product(
                        value, root_maps[here ^ front]
                    )
                incoming[part] = value

    map_parts = split(maps[...])
    for part, which in ((0, core), (1, 1 - core)):
        rows = pl.ds(pl.multiple_of(which * half, 8), half)
        change = split_dot(split(incoming[part]), map_parts)
        leaf_out[rows, :] = solved[rows, :] + change[:, :size]
        for tier in range(height):
            columns = slice((tier + 1) * size, (tier + 2) * size)
            node_out[tier, rows, :] = nodes[2 * tier + part][:half, :] + change[:, columns]
        root_out[rows, :] = roots[part][:half, :] + change[:, (height + 1) * size :]


def shards(
    right_sides,
    leaf_gen,
    leaf_inverse,
    leaf_lower,
    node_gen,
    node_inverse,
    node_lower,
    coupling,
    child_leaf,
):
    rows, leaf_size = right_sides.shape[1:]
    size = leaf_lower.shape[2]
    k_rows = coupling.shape[1]
    height = node_gen.shape[2]
    fronts = lax.axis_size("level")
    leaves = lax.axis_size("blk")
    level = lax.axis_index("level")
    position = lax.axis_index("blk")
    part = rows // 2 + k_rows // 2
    flag = jnp.stack(
        [(position == child_leaf[0]).astype(jnp.int32), position & 1, position, level]
    )
    flag_spec = [pl.BlockSpec(memory_space=SMEM)]
    vmem = pl.BlockSpec(memory_space=VMEM)
    array = lambda *shape: jax.ShapeDtypeStruct(shape, f32)

    def blk_swap(value, tier):
        return lax.ppermute(value, "blk", [(i, i ^ (1 << tier)) for i in range(leaves)])

    def level_swap(value, mask):
        return lax.ppermute(value, "level", [(i, i ^ mask) for i in range(fronts)])

    away, home, leaf_solve = call(
        leaf_kernel,
        (array(part, size), array(part, size), array(leaf_size, size)),
        (flag, right_sides[0], leaf_gen[0], leaf_inverse[0], leaf_lower[0], coupling[0]),
        6 * (rows + k_rows + leaf_size) * leaf_size * size,
        "leaf",
        in_specs=flag_spec + [vmem] * 5,
    )
    fold_flops = 6 * 2 * (2 * size) * size * size

    def folds(first, last):
        return call(
            fold_kernel,
            (array(last - first, 2 * size, size),) * 2,
            (
                node_gen[0, 0, first:last],
                node_inverse[0, 0, first:last],
                node_lower[0, 0, first:last],
            ),
            (last - first) * fold_flops,
            "fold",
        )

    first_maps, rest_maps = folds(0, 1), folds(1, height)

    def merge(tier, home, away, tier_map, name):
        return call(
            functools.partial(merge_kernel, tier),
            array(part, size),
            (flag, home, away, tier_map),
            6 * part * 2 * size * size,
            name,
            in_specs=flag_spec + [vmem] * 3,
        )

    nodes = []
    away = blk_swap(away, 0)
    for tier in range(height):
        solve_map, skeleton_map = (
            [m[0] for m in first_maps] if tier == 0 else [m[tier - 1] for m in rest_maps]
        )
        skeleton = merge(tier, home, away, skeleton_map, "skeleton")
        received = (
            blk_swap(skeleton, tier + 1)
            if tier + 1 < height
            else [level_swap(skeleton, mask) for mask in range(1, fronts)]
        )
        node = merge(tier, home, away, solve_map, "node")
        nodes += [node, blk_swap(node, 0)]
        home, away = skeleton, received
    solved, leaf_map = call(
        leaf_solve_kernel,
        (array(rows, size), array(k_rows, size)),
        (flag, right_sides[0], coupling[0], leaf_solve),
        6 * (rows + k_rows) * leaf_size * size,
        "leaf_solve",
        in_specs=flag_spec + [vmem] * 3,
    )
    roots = []
    for value in [home] + away:
        roots += [value, blk_swap(value, 0)]
    args = (flag, solved, leaf_map, *nodes, *roots)
    leaf_out, node_out, root_out = call(
        functools.partial(final_kernel, fronts, height),
        (array(rows, size), array(height, rows, size), array(rows, size)),
        args,
        6 * rows * size * size * (height + 2),
        "final",
        in_specs=flag_spec + [vmem] * (len(args) - 1),
        scratch_shapes=[
            pltpu.VMEM((k_rows, size * (height + 2)), f32),
            pltpu.VMEM((fronts, k_rows, size), f32),
            pltpu.VMEM((2, rows // 2, size), f32),
        ],
    )
    return (leaf_out[None], node_out[None, None], root_out[None])


def solution(mesh):
    in_specs = (
        P("level", None, "blk"),
        P("level", "blk", None),
        P("level", "blk", None),
        P("level", "blk", None),
        P("level", "blk", None, None, None),
        P("level", "blk", None, None, None),
        P("level", "blk", None, None, None),
        P("level", None, None),
        P("level"),
    )
    out_specs = (
        P("level", None, "blk"),
        P("level", "blk", None, None, None),
        P("level", None, None),
    )
    return jax.shard_map(shards, mesh=mesh, in_specs=in_specs, out_specs=out_specs, check_vma=False)
```

```python
import functools

import jax
import jax.numpy as jnp
from jax import lax
from jax.experimental import pallas as pl
from jax.experimental.pallas import tpu as pltpu
from jax.sharding import PartitionSpec as P


f32 = jnp.float32
bf16 = jnp.bfloat16
VMEM_LIMIT = 12 << 20


def split(value):
    high = value.astype(bf16)
    return high, (value - high.astype(f32)).astype(bf16)


def narrow_dot(left, right):
    return jnp.dot(left, right, preferred_element_type=f32)


def split_dot(left, right):
    left_high, left_low = left
    right_high, right_low = right
    return narrow_dot(left_high, right_high) + (
        narrow_dot(left_high, right_low) + narrow_dot(left_low, right_high)
    )


def product(left, right):
    return split_dot(split(left), split(right))


def call(kernel, out_shape, args, flops, name, in_specs=None, out_specs=None, scratch_shapes=()):
    size = lambda s: s.size * s.dtype.itemsize
    vmem = pl.BlockSpec(memory_space=pltpu.VMEM)
    moved = sum(size(a) for a in args) + sum(size(o) for o in jax.tree.leaves(out_shape))
    return pl.pallas_call(
        kernel,
        out_shape=out_shape,
        in_specs=in_specs or [vmem] * len(args),
        out_specs=out_specs or jax.tree.map(lambda _: vmem, out_shape),
        scratch_shapes=scratch_shapes,
        name=name,
        compiler_params=pltpu.CompilerParams(vmem_limit_bytes=VMEM_LIMIT),
        cost_estimate=pl.CostEstimate(flops=flops, bytes_accessed=moved, transcendentals=0),
    )(*args)


def span(index, length):
    return pl.ds(pl.multiple_of(index * length, 8), length)


def fold(generator, inverse, lower):
    size = inverse.shape[0]
    solve_map = product(generator[:, :size], inverse)
    return solve_map, generator[:, size:] - product(solve_map, lower)


def leaf_kernel(
    child, right, generator, inverse, lower, coupling,
    away, home, solve_map,
    right_here, generator_here, inverse_here, lower_here, coupling_here, sems,
):
    position = lax.axis_index("blk")
    core = position & 1
    half, k_half = right.shape[0] // 2, coupling.shape[0] // 2
    copies = [
        pltpu.make_async_copy(source, target, sems.at[i])
        for i, (source, target) in enumerate(
            [
                (generator, generator_here),
                (inverse, inverse_here),
                (lower, lower_here),
                (coupling, coupling_here),
                (right.at[span(1 - core, half)], right_here.at[0]),
                (right.at[span(core, half)], right_here.at[1]),
            ]
        )
    ]
    for copy in copies:
        copy.start()
    for copy in copies[:3]:
        copy.wait()
    solved, skeleton = fold(generator_here[...], inverse_here[...], lower_here[...])
    solve_map[...] = solved
    parts = split(skeleton)
    on_target = position == child[0]
    copies[3].wait()
    for i, (which, out) in enumerate([(1 - core, away), (core, home)]):
        lifted = jnp.where(on_target, coupling_here[span(which, k_half), :], 0.0)
        out[half:, :] = split_dot(split(lifted), parts)
        copies[4 + i].wait()
        out[:half, :] = split_dot(split(right_here[i]), parts)


def leaf_solve_kernel(child, right, coupling, solve_map, solved, leaf_map):
    parts = split(solve_map[...])
    on_target = lax.axis_index("blk") == child[0]
    solved[...] = split_dot(split(right[...]), parts)
    leaf_map[...] = split_dot(split(jnp.where(on_target, coupling[...], 0.0)), parts)


def fold_kernel(first, last, generator, inverse, lower, solve_map, skeleton_map):
    for tier in range(first, last):
        solve_map[tier - first], skeleton_map[tier - first] = fold(
            generator[tier], inverse[tier], lower[tier]
        )


def merge_kernel(tier, index, home, away, tier_map, *refs):
    out = refs[-1]
    size = home.shape[1]
    upper = (lax.axis_index("blk") >> tier) & 1
    mine = tier_map[index, span(upper, size), :]
    other = tier_map[index, span(1 - upper, size), :]
    out[...] = product(home[...], mine) + product(away[...], other)


def maps_kernel(half, leaf_map, *refs):
    pairs, (high, low, maps) = refs[:-3], refs[-3:]
    k_half, size = leaf_map.shape[0] // 2, leaf_map.shape[1]
    core = lax.axis_index("blk") & 1
    maps[:, :size] = leaf_map[...]
    for i in range(len(pairs) // 2):
        columns = slice((i + 1) * size, (i + 2) * size)
        maps[span(core, k_half), columns] = pairs[2 * i][half:, :]
        maps[span(1 - core, k_half), columns] = pairs[2 * i + 1][half:, :]
    high[...], low[...] = split(maps[...])


def final_kernel(fronts, height, solved, high, low, *refs):
    nodes, refs = refs[: 2 * height], refs[2 * height :]
    roots, refs = refs[: 2 * fronts], refs[2 * fronts :]
    leaf_out, node_out, root_out, root_maps, incoming, result, sems = refs
    core, level = lax.axis_index("blk") & 1, lax.axis_index("level")
    half, size = solved.shape[0] // 2, solved.shape[1]
    k_half = high.shape[0] // 2
    for front in range(1, fronts):
        root_maps[front, span(core, k_half), :] = roots[2 * front][half:, :]
        root_maps[front, span(1 - core, k_half), :] = roots[2 * front + 1][half:, :]

    @pl.when(level == 0)
    def _():
        incoming[...] = jnp.zeros_like(incoming)

    for here in range(1, fronts):

        @pl.when(level == here)
        def _():
            for part in range(2):
                value = roots[2 * here + part][:half, :]
                for front in range(1, here):
                    value = roots[2 * (here ^ front) + part][:half, :] + product(
                        value, root_maps[here ^ front]
                    )
                incoming[part] = value

    copies = []
    for part, which in ((0, core), (1, 1 - core)):
        rows = span(which, half)
        change = split_dot(split(incoming[part]), (high[...], low[...]))
        bases = (
            [solved[rows, :]]
            + [nodes[2 * tier + part][:half, :] for tier in range(height)]
            + [roots[part][:half, :]]
        )
        targets = (
            [leaf_out.at[rows]] + [node_out.at[tier, rows] for tier in range(height)] + [root_out.at[rows]]
        )
        for i, (base, target) in enumerate(zip(bases, targets)):
            result[part, i] = base + change[:, i * size : (i + 1) * size]
            copies.append(pltpu.make_async_copy(result.at[part, i], target, sems.at[part, i]))
            copies[-1].start()
    for copy in copies:
        copy.wait()


def shards(
    right_sides,
    leaf_gen,
    leaf_inverse,
    leaf_lower,
    node_gen,
    node_inverse,
    node_lower,
    coupling,
    child_leaf,
):
    rows, leaf_size = right_sides.shape[1:]
    size = leaf_lower.shape[2]
    k_rows = coupling.shape[1]
    height = node_gen.shape[2]
    fronts = lax.axis_size("level")
    leaves = lax.axis_size("blk")
    half = rows // 2
    part = half + k_rows // 2
    smem = pl.BlockSpec(memory_space=pltpu.SMEM)
    vmem = pl.BlockSpec(memory_space=pltpu.VMEM)
    hbm = pl.BlockSpec(memory_space=pltpu.HBM)
    anywhere = pl.BlockSpec(memory_space=pl.ANY)
    array = lambda *shape: jax.ShapeDtypeStruct(shape, f32)

    def blk_swap(value, tier):
        return lax.ppermute(value, "blk", [(i, i ^ (1 << tier)) for i in range(leaves)])

    def level_swap(value, mask):
        return lax.ppermute(value, "level", [(i, i ^ mask) for i in range(fronts)])

    away, home, leaf_solve = call(
        leaf_kernel,
        (array(part, size), array(part, size), array(leaf_size, size)),
        (child_leaf, right_sides[0], leaf_gen[0], leaf_inverse[0], leaf_lower[0], coupling[0]),
        6 * (rows + k_rows + leaf_size) * leaf_size * size,
        "leaf",
        in_specs=[smem] + [hbm] * 5,
        scratch_shapes=[
            pltpu.VMEM((2, half, leaf_size), f32),
            pltpu.VMEM((leaf_size, leaf_size), f32),
            pltpu.VMEM((size, size), f32),
            pltpu.VMEM((size, size), f32),
            pltpu.VMEM((k_rows, leaf_size), f32),
            pltpu.SemaphoreType.DMA((6,)),
        ],
    )

    def folds(first, last):
        return call(
            functools.partial(fold_kernel, first, last),
            (array(last - first, 2 * size, size),) * 2,
            (node_gen[0, 0], node_inverse[0, 0], node_lower[0, 0]),
            (last - first) * 6 * 4 * size * size * size,
            "fold",
        )

    def merge(tier, maps, home, away, after, name):
        return call(
            functools.partial(merge_kernel, tier, max(tier - 1, 0)),
            array(part, size),
            (home, away, maps, *after),
            6 * part * 2 * size * size,
            name,
            in_specs=[vmem] * 3 + [anywhere] * len(after),
        )

    first_maps = folds(0, 1)
    away = blk_swap(away, 0)
    nodes, after = [], []
    for tier in range(height):
        solve_maps, skeleton_maps = first_maps if tier == 0 else rest_maps
        skeleton = merge(tier, skeleton_maps, home, away, after, "skeleton")
        if tier + 1 < height:
            received = blk_swap(skeleton, tier + 1)
        else:
            received = [level_swap(skeleton, mask) for mask in range(1, fronts)]
        node = merge(tier, solve_maps, home, away, (), "node")
        after = [node]
        if tier == 0:
            rest_maps = folds(1, height)
            solved, leaf_map = call(
                leaf_solve_kernel,
                (array(rows, size), array(k_rows, size)),
                (child_leaf, right_sides[0], coupling[0], leaf_solve),
                6 * (rows + k_rows) * leaf_size * size,
                "leaf_solve",
                in_specs=[smem] + [vmem] * 3,
            )
            after.append(solved)
        nodes += [node, blk_swap(node, 0)]
        home, away = skeleton, received
    roots = []
    for value in [home] + away:
        roots += [value, blk_swap(value, 0)]
    high, low = call(
        functools.partial(maps_kernel, half),
        (jax.ShapeDtypeStruct((k_rows, size * (height + 2)), bf16),) * 2,
        (leaf_map, *nodes, *roots[:2]),
        k_rows * size * (height + 2) * 4,
        "maps",
        scratch_shapes=[pltpu.VMEM((k_rows, size * (height + 2)), f32)],
    )
    leaf_out, node_out, root_out = call(
        functools.partial(final_kernel, fronts, height),
        (array(rows, size), array(height, rows, size), array(rows, size)),
        (solved, high, low, *nodes, *roots),
        6 * rows * size * size * (height + 2),
        "final",
        out_specs=(hbm,) * 3,
        scratch_shapes=[
            pltpu.VMEM((fronts, k_rows, size), f32),
            pltpu.VMEM((2, half, size), f32),
            pltpu.VMEM((2, height + 2, half, size), f32),
            pltpu.SemaphoreType.DMA((2, height + 2)),
        ],
    )
    return (leaf_out[None], node_out[None, None], root_out[None])


def solution(mesh):
    in_specs = (
        P("level", None, "blk"),
        P("level", "blk", None),
        P("level", "blk", None),
        P("level", "blk", None),
        P("level", "blk", None, None, None),
        P("level", "blk", None, None, None),
        P("level", "blk", None, None, None),
        P("level", None, None),
        P("level"),
    )
    out_specs = (
        P("level", None, "blk"),
        P("level", "blk", None, None, None),
        P("level", None, None),
    )
    return jax.shard_map(shards, mesh=mesh, in_specs=in_specs, out_specs=out_specs, check_vma=False)
```

```python
import functools

import jax
import jax.numpy as jnp
from jax import lax
from jax.experimental import pallas as pl
from jax.experimental.pallas import tpu as pltpu
from jax.sharding import PartitionSpec as P


f32 = jnp.float32
bf16 = jnp.bfloat16
VMEM_LIMIT = 12 << 20


def split(value):
    high = value.astype(bf16)
    return high, (value - high.astype(f32)).astype(bf16)


def narrow_dot(left, right):
    return jnp.dot(left, right, preferred_element_type=f32)


def split_dot(left, right):
    left_high, left_low = left
    right_high, right_low = right
    return narrow_dot(left_high, right_high) + (
        narrow_dot(left_high, right_low) + narrow_dot(left_low, right_high)
    )


def product(left, right):
    return split_dot(split(left), split(right))


def call(kernel, out_shape, args, flops, name, in_specs=None, out_specs=None, scratch_shapes=()):
    size = lambda s: s.size * s.dtype.itemsize
    vmem = pl.BlockSpec(memory_space=pltpu.VMEM)
    moved = sum(size(a) for a in args) + sum(size(o) for o in jax.tree.leaves(out_shape))
    return pl.pallas_call(
        kernel,
        out_shape=out_shape,
        in_specs=in_specs or [vmem] * len(args),
        out_specs=out_specs or jax.tree.map(lambda _: vmem, out_shape),
        scratch_shapes=scratch_shapes,
        name=name,
        compiler_params=pltpu.CompilerParams(vmem_limit_bytes=VMEM_LIMIT),
        cost_estimate=pl.CostEstimate(flops=flops, bytes_accessed=moved, transcendentals=0),
    )(*args)


def span(index, length):
    return pl.ds(pl.multiple_of(index * length, 8), length)


def fold(generator, inverse, lower):
    size = inverse.shape[0]
    solve_map = product(generator[:, :size], inverse)
    return solve_map, generator[:, size:] - product(solve_map, lower)


def leaf_kernel(
    right, generator, inverse, lower, coupling, *refs
):
    later, (away, home, solve_map), refs = refs[:3], refs[3:6], refs[6:]
    (right_here, coupling_here, *later_here), refs = refs[:5], refs[5:]
    generator_here, inverse_here, lower_here, sems = refs
    core = lax.axis_index("blk") & 1
    half, k_half = right.shape[0] // 2, coupling.shape[0] // 2
    copies = [
        pltpu.make_async_copy(source, target, sems.at[i])
        for i, (source, target) in enumerate(
            [
                (generator, generator_here),
                (inverse, inverse_here),
                (lower, lower_here),
                (right.at[span(1 - core, half)], right_here.at[0]),
                (coupling, coupling_here),
                (right.at[span(core, half)], right_here.at[1]),
                *zip(later, later_here),
            ]
        )
    ]
    for copy in copies[:6]:
        copy.start()
    for copy in copies[:2]:
        copy.wait()
    for copy in copies[6:]:
        copy.start()
    solved = product(generator_here[:, : inverse.shape[0]], inverse_here[...])
    solve_map[...] = solved
    copies[2].wait()
    parts = split(generator_here[:, inverse.shape[0] :] - product(solved, lower_here[...]))
    copies[3].wait()
    away[:half, :] = split_dot(split(right_here[0]), parts)
    copies[4].wait()
    away[half:, :] = split_dot(split(coupling_here[span(1 - core, k_half), :]), parts)
    home[half:, :] = split_dot(split(coupling_here[span(core, k_half), :]), parts)
    copies[5].wait()
    home[:half, :] = split_dot(split(right_here[1]), parts)
    for copy in copies[6:]:
        copy.wait()


def leaf_solve_kernel(child, right, coupling, solve_map, solved, leaf_map):
    parts = split(solve_map[...])
    for part in range(2):
        solved[part] = split_dot(split(right[1 - part]), parts)
    on_target = lax.axis_index("blk") == child[0]
    leaf_map[...] = jnp.where(on_target, split_dot(split(coupling[...]), parts), 0.0)


def fold_kernel(first, last, generator, inverse, lower, solve_map, skeleton_map):
    for tier in range(first, last):
        solve_map[tier - first], skeleton_map[tier - first] = fold(
            generator[tier], inverse[tier], lower[tier]
        )


def merge_kernel(half, tier, index, home, away, tier_map, *refs):
    out = refs[-1]
    size = home.shape[1]
    position = lax.axis_index("blk")
    upper = (position >> tier) & 1
    mine = split(tier_map[index, span(upper, size), :])
    other = split(tier_map[index, span(1 - upper, size), :])
    if tier > 0:
        out[...] = split_dot(split(home[...]), mine) + split_dot(split(away[...]), other)
        return
    child = refs[0][0]
    out[:half, :] = split_dot(split(home[:half, :]), mine) + split_dot(split(away[:half, :]), other)
    out[half:, :] = jnp.where(
        position == child, split_dot(split(home[half:, :]), mine), 0.0
    ) + jnp.where(position ^ 1 == child, split_dot(split(away[half:, :]), other), 0.0)


def maps_kernel(half, leaf_map, *refs):
    pairs, (high, low, maps) = refs[:-3], refs[-3:]
    k_half, size = leaf_map.shape[0] // 2, leaf_map.shape[1]
    core = lax.axis_index("blk") & 1
    maps[:, :size] = leaf_map[...]
    for i in range(len(pairs) // 2):
        columns = slice((i + 1) * size, (i + 2) * size)
        maps[span(core, k_half), columns] = pairs[2 * i][half:, :]
        maps[span(1 - core, k_half), columns] = pairs[2 * i + 1][half:, :]
    high[...], low[...] = split(maps[...])


def final_kernel(fronts, height, solved, high, low, *refs):
    nodes, refs = refs[: 2 * height], refs[2 * height :]
    roots, refs = refs[: 2 * fronts], refs[2 * fronts :]
    leaf_out, node_out, root_out, root_maps, incoming, result, sems = refs
    core, level = lax.axis_index("blk") & 1, lax.axis_index("level")
    half, size = solved.shape[1:]
    k_half = high.shape[0] // 2
    for front in range(1, fronts):
        root_maps[front, span(core, k_half), :] = roots[2 * front][half:, :]
        root_maps[front, span(1 - core, k_half), :] = roots[2 * front + 1][half:, :]

    @pl.when(level == 0)
    def _():
        incoming[...] = jnp.zeros_like(incoming)

    for here in range(1, fronts):

        @pl.when(level == here)
        def _():
            for part in range(2):
                value = roots[2 * here + part][:half, :]
                for front in range(1, here):
                    value = roots[2 * (here ^ front) + part][:half, :] + product(
                        value, root_maps[here ^ front]
                    )
                incoming[part] = value

    copies = []
    for part, which in ((0, core), (1, 1 - core)):
        rows = span(which, half)
        change = split_dot(split(incoming[part]), (high[...], low[...]))
        bases = (
            [solved[part]]
            + [nodes[2 * tier + part][:half, :] for tier in range(height)]
            + [roots[part][:half, :]]
        )
        targets = (
            [leaf_out.at[rows]] + [node_out.at[tier, rows] for tier in range(height)] + [root_out.at[rows]]
        )
        for i, (base, target) in enumerate(zip(bases, targets)):
            result[part, i] = base + change[:, i * size : (i + 1) * size]
            copies.append(pltpu.make_async_copy(result.at[part, i], target, sems.at[part, i]))
            copies[-1].start()
    for copy in copies:
        copy.wait()


def shards(
    right_sides,
    leaf_gen,
    leaf_inverse,
    leaf_lower,
    node_gen,
    node_inverse,
    node_lower,
    coupling,
    child_leaf,
):
    rows, leaf_size = right_sides.shape[1:]
    size = leaf_lower.shape[2]
    k_rows = coupling.shape[1]
    height = node_gen.shape[2]
    fronts = lax.axis_size("level")
    leaves = lax.axis_size("blk")
    half = rows // 2
    part = half + k_rows // 2
    smem = pl.BlockSpec(memory_space=pltpu.SMEM)
    vmem = pl.BlockSpec(memory_space=pltpu.VMEM)
    hbm = pl.BlockSpec(memory_space=pltpu.HBM)
    anywhere = pl.BlockSpec(memory_space=pl.ANY)
    array = lambda *shape: jax.ShapeDtypeStruct(shape, f32)

    def blk_swap(value, tier):
        return lax.ppermute(value, "blk", [(i, i ^ (1 << tier)) for i in range(leaves)])

    def level_swap(value, mask):
        return lax.ppermute(value, "level", [(i, i ^ mask) for i in range(fronts)])

    away, home, leaf_solve, right_here, coupling_here, *node_params = call(
        leaf_kernel,
        (
            array(part, size),
            array(part, size),
            array(leaf_size, size),
            array(2, half, leaf_size),
            array(k_rows, leaf_size),
            array(*node_gen.shape[2:]),
            array(*node_inverse.shape[2:]),
            array(*node_lower.shape[2:]),
        ),
        tuple(
            pltpu.with_memory_space_constraint(value, pltpu.HBM)
            for value in (
                right_sides[0],
                leaf_gen[0],
                leaf_inverse[0],
                leaf_lower[0],
                coupling[0],
                node_gen[0, 0],
                node_inverse[0, 0],
                node_lower[0, 0],
            )
        ),
        6 * (rows + k_rows + leaf_size) * leaf_size * size,
        "leaf",
        in_specs=[hbm] * 8,
        scratch_shapes=[
            pltpu.VMEM((leaf_size, leaf_size), f32),
            pltpu.VMEM((size, size), f32),
            pltpu.VMEM((size, size), f32),
            pltpu.SemaphoreType.DMA((9,)),
        ],
    )

    def folds(first, last):
        return call(
            functools.partial(fold_kernel, first, last),
            (array(last - first, 2 * size, size),) * 2,
            tuple(node_params),
            (last - first) * 6 * 4 * size * size * size,
            "fold",
        )

    def merge(tier, maps, home, away, after, name):
        return call(
            functools.partial(merge_kernel, half, tier, max(tier - 1, 0)),
            array(part, size),
            (home, away, maps) + ((child_leaf,) if tier == 0 else after),
            6 * part * 2 * size * size,
            name,
            in_specs=[vmem] * 3 + ([smem] if tier == 0 else [anywhere] * len(after)),
        )

    home, child_leaf = lax.optimization_barrier((home, child_leaf))
    first_maps = folds(0, 1)
    away = blk_swap(away, 0)
    nodes, after = [], ()
    for tier in range(height):
        solve_maps, skeleton_maps = first_maps if tier == 0 else rest_maps
        skeleton = merge(tier, skeleton_maps, home, away, after, "skeleton")
        if tier + 1 < height:
            received = blk_swap(skeleton, tier + 1)
        else:
            received = [level_swap(skeleton, mask) for mask in range(1, fronts)]
        node = merge(tier, solve_maps, home, away, (), "node")
        after = (node,)
        if tier == 0:
            rest_maps = folds(1, height)
            solved, leaf_map = call(
                leaf_solve_kernel,
                (array(2, half, size), array(k_rows, size)),
                (child_leaf, right_here, coupling_here, leaf_solve),
                6 * (rows + k_rows) * leaf_size * size,
                "leaf_solve",
                in_specs=[smem] + [vmem] * 3,
            )
            after += (solved,)
        nodes += [node, blk_swap(node, 0)]
        home, away = skeleton, received
    roots = []
    for value in [home] + away:
        roots += [value, blk_swap(value, 0)]
    high, low = call(
        functools.partial(maps_kernel, half),
        (jax.ShapeDtypeStruct((k_rows, size * (height + 2)), bf16),) * 2,
        (leaf_map, *nodes, *roots[:2]),
        k_rows * size * (height + 2) * 4,
        "maps",
        scratch_shapes=[pltpu.VMEM((k_rows, size * (height + 2)), f32)],
    )
    leaf_out, node_out, root_out = call(
        functools.partial(final_kernel, fronts, height),
        (array(rows, size), array(height, rows, size), array(rows, size)),
        (solved, high, low, *nodes, *roots),
        6 * rows * size * size * (height + 2),
        "final",
        out_specs=(hbm,) * 3,
        scratch_shapes=[
            pltpu.VMEM((fronts, k_rows, size), f32),
            pltpu.VMEM((2, half, size), f32),
            pltpu.VMEM((2, height + 2, half, size), f32),
            pltpu.SemaphoreType.DMA((2, height + 2)),
        ],
    )
    return (leaf_out[None], node_out[None, None], root_out[None])


def solution(mesh):
    in_specs = (
        P("level", None, "blk"),
        P("level", "blk", None),
        P("level", "blk", None),
        P("level", "blk", None),
        P("level", "blk", None, None, None),
        P("level", "blk", None, None, None),
        P("level", "blk", None, None, None),
        P("level", None, None),
        P("level"),
    )
    out_specs = (
        P("level", None, "blk"),
        P("level", "blk", None, None, None),
        P("level", None, None),
    )
    return jax.shard_map(shards, mesh=mesh, in_specs=in_specs, out_specs=out_specs, check_vma=False)
```

```python
import functools

import jax
import jax.numpy as jnp
from jax import lax
from jax.experimental import pallas as pl
from jax.experimental.pallas import tpu as pltpu
from jax.sharding import PartitionSpec as P


f32 = jnp.float32
bf16 = jnp.bfloat16
VMEM_LIMIT = 12 << 20


def split(value):
    high = value.astype(bf16)
    return high, (value - high.astype(f32)).astype(bf16)


def wide_left(value):
    high, low = split(value)
    return jnp.concatenate([high, low, high], axis=1)


def wide_right(value):
    high, low = split(value)
    return jnp.concatenate([high, high, low], axis=0)


def wide_dot(left, right):
    return jnp.dot(left, right, preferred_element_type=f32)


def product(left, right):
    return wide_dot(wide_left(left), wide_right(right))


def call(kernel, out_shape, args, flops, name, in_specs=None, out_specs=None, scratch_shapes=()):
    size = lambda s: s.size * s.dtype.itemsize
    vmem = pl.BlockSpec(memory_space=pltpu.VMEM)
    moved = sum(size(a) for a in args) + sum(size(o) for o in jax.tree.leaves(out_shape))
    return pl.pallas_call(
        kernel,
        out_shape=out_shape,
        in_specs=in_specs or [vmem] * len(args),
        out_specs=out_specs or jax.tree.map(lambda _: vmem, out_shape),
        scratch_shapes=scratch_shapes,
        name=name,
        compiler_params=pltpu.CompilerParams(vmem_limit_bytes=VMEM_LIMIT),
        cost_estimate=pl.CostEstimate(flops=flops, bytes_accessed=moved, transcendentals=0),
    )(*args)


def span(index, length):
    return pl.ds(pl.multiple_of(index * length, 8), length)


def leaf_kernel(
    right, generator, inverse, lower, coupling, *refs
):
    later, (away, home, solve_map), refs = refs[:3], refs[3:6], refs[6:]
    (right_here, coupling_here, *later_here), refs = refs[:5], refs[5:]
    generator_here, inverse_here, lower_here, sems = refs
    core = lax.axis_index("blk") & 1
    half, k_half = right.shape[0] // 2, coupling.shape[0] // 2
    copies = [
        pltpu.make_async_copy(source, target, sems.at[i])
        for i, (source, target) in enumerate(
            [
                (generator, generator_here),
                (inverse, inverse_here),
                (lower, lower_here),
                (right.at[span(1 - core, half)], right_here.at[0]),
                (coupling, coupling_here),
                (right.at[span(core, half)], right_here.at[1]),
                *zip(later, later_here),
            ]
        )
    ]
    for copy in copies[:6]:
        copy.start()
    for copy in copies[:2]:
        copy.wait()
    for copy in copies[6:]:
        copy.start()
    solved = product(generator_here[:, : inverse.shape[0]], inverse_here[...])
    solve_map[...] = solved
    copies[2].wait()
    parts = wide_right(generator_here[:, inverse.shape[0] :] - product(solved, lower_here[...]))
    copies[3].wait()
    away[:half, :] = wide_dot(wide_left(right_here[0]), parts)
    copies[4].wait()
    away[half:, :] = wide_dot(wide_left(coupling_here[span(1 - core, k_half), :]), parts)
    home[half:, :] = wide_dot(wide_left(coupling_here[span(core, k_half), :]), parts)
    copies[5].wait()
    home[:half, :] = wide_dot(wide_left(right_here[1]), parts)
    for copy in copies[6:]:
        copy.wait()


def leaf_solve_kernel(child, right, coupling, solve_map, solved, leaf_map):
    parts = wide_right(solve_map[...])
    for part in range(2):
        solved[part] = wide_dot(wide_left(right[1 - part]), parts)
    on_target = lax.axis_index("blk") == child[0]
    leaf_map[...] = jnp.where(on_target, wide_dot(wide_left(coupling[...]), parts), 0.0)


def fold_kernel(first, last, generator, inverse, lower, *refs):
    if first == 0:
        home, other_maps, base, both, mine_maps = refs
    else:
        mine_maps, other_maps, both = refs
    size = inverse.shape[1]
    for tier in range(first, last):
        solve_map = product(generator[tier, :, :size], inverse[tier])
        both[:, :size] = solve_map
        both[:, size:] = generator[tier, :, size:] - product(solve_map, lower[tier])
        upper = (lax.axis_index("blk") >> tier) & 1
        mine_maps[tier - first] = wide_right(both[span(upper, size), :])
        other_maps[tier - first] = wide_right(both[span(1 - upper, size), :])
    if first == 0:
        base[...] = wide_dot(wide_left(home[...]), mine_maps[0])


def base_kernel(index, home, mine_maps, base):
    base[...] = wide_dot(wide_left(home[...]), mine_maps[index])


def merge_kernel(index, base, away, other_maps, *refs):
    node, skeleton = refs[-2:]
    size = away.shape[1]
    both = base[...] + wide_dot(wide_left(away[...]), other_maps[index])
    skeleton[...] = both[:, size:]
    node[...] = both[:, :size]


def first_merge_kernel(half, child, base, away, other_maps, node, skeleton):
    size = away.shape[1]
    position = lax.axis_index("blk")
    both = base[:half, :] + wide_dot(wide_left(away[:half, :]), other_maps[0])
    skeleton[:half, :] = both[:, size:]
    node[:half, :] = both[:, :size]
    both = jnp.where(position == child[0], base[half:, :], 0.0) + jnp.where(
        position ^ 1 == child[0], wide_dot(wide_left(away[half:, :]), other_maps[0]), 0.0
    )
    skeleton[half:, :] = both[:, size:]
    node[half:, :] = both[:, :size]


def maps_kernel(half, leaf_map, *refs):
    pairs, (wide_maps, maps) = refs[:-2], refs[-2:]
    k_half, size = leaf_map.shape[0] // 2, leaf_map.shape[1]
    core = lax.axis_index("blk") & 1
    maps[:, :size] = leaf_map[...]
    for i in range(len(pairs) // 2):
        columns = slice((i + 1) * size, (i + 2) * size)
        maps[span(core, k_half), columns] = pairs[2 * i][half:, :]
        maps[span(1 - core, k_half), columns] = pairs[2 * i + 1][half:, :]
    wide_maps[...] = wide_right(maps[...])


def final_kernel(fronts, height, solved, wide_maps, *refs):
    nodes, refs = refs[: 2 * height], refs[2 * height :]
    roots, refs = refs[: 2 * fronts], refs[2 * fronts :]
    leaf_out, node_out, root_out, root_maps, incoming, result, sems = refs
    core, level = lax.axis_index("blk") & 1, lax.axis_index("level")
    half, size = solved.shape[1:]
    k_half = root_maps.shape[1] // 2
    for front in range(1, fronts):
        root_maps[front, span(core, k_half), :] = roots[2 * front][half:, :]
        root_maps[front, span(1 - core, k_half), :] = roots[2 * front + 1][half:, :]

    @pl.when(level == 0)
    def _():
        incoming[...] = jnp.zeros_like(incoming)

    for here in range(1, fronts):

        @pl.when(level == here)
        def _():
            for part in range(2):
                value = roots[2 * here + part][:half, :]
                for front in range(1, here):
                    value = roots[2 * (here ^ front) + part][:half, :] + product(
                        value, root_maps[here ^ front]
                    )
                incoming[part] = value

    copies = []
    for part, which in ((0, core), (1, 1 - core)):
        rows = span(which, half)
        change = wide_dot(wide_left(incoming[part]), wide_maps[...])
        bases = (
            [solved[part]]
            + [nodes[2 * tier + part][:half, :] for tier in range(height)]
            + [roots[part][:half, :]]
        )
        targets = (
            [leaf_out.at[rows]] + [node_out.at[tier, rows] for tier in range(height)] + [root_out.at[rows]]
        )
        for i, (base, target) in enumerate(zip(bases, targets)):
            result[part, i] = base + change[:, i * size : (i + 1) * size]
            copies.append(pltpu.make_async_copy(result.at[part, i], target, sems.at[part, i]))
            copies[-1].start()
    for copy in copies:
        copy.wait()


def shards(
    right_sides,
    leaf_gen,
    leaf_inverse,
    leaf_lower,
    node_gen,
    node_inverse,
    node_lower,
    coupling,
    child_leaf,
):
    rows, leaf_size = right_sides.shape[1:]
    size = leaf_lower.shape[2]
    k_rows = coupling.shape[1]
    height = node_gen.shape[2]
    fronts = lax.axis_size("level")
    leaves = lax.axis_size("blk")
    half = rows // 2
    part = half + k_rows // 2
    smem = pl.BlockSpec(memory_space=pltpu.SMEM)
    vmem = pl.BlockSpec(memory_space=pltpu.VMEM)
    hbm = pl.BlockSpec(memory_space=pltpu.HBM)
    anywhere = pl.BlockSpec(memory_space=pl.ANY)
    array = lambda *shape: jax.ShapeDtypeStruct(shape, f32)

    def blk_swap(value, tier):
        return lax.ppermute(value, "blk", [(i, i ^ (1 << tier)) for i in range(leaves)])

    def level_swap(value, mask):
        return lax.ppermute(value, "level", [(i, i ^ mask) for i in range(fronts)])

    away, home, leaf_solve, right_here, coupling_here, *node_params = call(
        leaf_kernel,
        (
            array(part, size),
            array(part, size),
            array(leaf_size, size),
            array(2, half, leaf_size),
            array(k_rows, leaf_size),
            array(*node_gen.shape[2:]),
            array(*node_inverse.shape[2:]),
            array(*node_lower.shape[2:]),
        ),
        tuple(
            pltpu.with_memory_space_constraint(value, pltpu.HBM)
            for value in (
                right_sides[0],
                leaf_gen[0],
                leaf_inverse[0],
                leaf_lower[0],
                coupling[0],
                node_gen[0, 0],
                node_inverse[0, 0],
                node_lower[0, 0],
            )
        ),
        6 * (rows + k_rows + leaf_size) * leaf_size * size,
        "leaf",
        in_specs=[hbm] * 8,
        scratch_shapes=[
            pltpu.VMEM((leaf_size, leaf_size), f32),
            pltpu.VMEM((size, size), f32),
            pltpu.VMEM((size, size), f32),
            pltpu.SemaphoreType.DMA((9,)),
        ],
    )

    def folds(first, last, *home):
        maps = jax.ShapeDtypeStruct((last - first, 3 * size, 2 * size), bf16)
        return call(
            functools.partial(fold_kernel, first, last),
            (maps, array(part, 2 * size)) if home else (maps, maps),
            (*node_params, *home),
            (last - first) * 6 * 4 * size * size * size,
            "fold",
            scratch_shapes=[pltpu.VMEM((2 * size, 2 * size), f32)]
            + [pltpu.VMEM(maps.shape, bf16)] * len(home),
        )

    home, child_leaf = lax.optimization_barrier((home, child_leaf))
    other_maps, base = folds(0, 1, home)
    away = blk_swap(away, 0)
    merge_flops = 6 * part * 2 * size * size
    node, skeleton = call(
        functools.partial(first_merge_kernel, half),
        (array(part, size),) * 2,
        (child_leaf, base, away, other_maps),
        merge_flops,
        "merge",
        in_specs=[smem] + [vmem] * 3,
    )
    nodes = [node, blk_swap(node, 0)]
    for tier in range(1, height):
        away = blk_swap(skeleton, tier)
        after = tuple(nodes[1::2]) if tier > 1 else ()
        if tier == 1:
            mine_maps, other_maps = folds(1, height)
            solved, leaf_map = call(
                leaf_solve_kernel,
                (array(2, half, size), array(k_rows, size)),
                (child_leaf, right_here, coupling_here, leaf_solve),
                6 * (rows + k_rows) * leaf_size * size,
                "leaf_solve",
                in_specs=[smem] + [vmem] * 3,
            )
            after = (solved,)
        base = call(
            functools.partial(base_kernel, tier - 1),
            array(part, 2 * size),
            (skeleton, mine_maps),
            merge_flops,
            "base",
        )
        node, skeleton = call(
            functools.partial(merge_kernel, tier - 1),
            (array(part, size),) * 2,
            (base, away, other_maps, *after),
            merge_flops,
            "merge",
            in_specs=[vmem] * 3 + [anywhere] * len(after),
        )
        nodes += [node, blk_swap(node, 0)]
    home, away = skeleton, [level_swap(skeleton, mask) for mask in range(1, fronts)]
    roots = []
    for value in [home] + away:
        roots += [value, blk_swap(value, 0)]
    wide_maps = call(
        functools.partial(maps_kernel, half),
        jax.ShapeDtypeStruct((3 * k_rows, size * (height + 2)), bf16),
        (leaf_map, *nodes, *roots[:2]),
        k_rows * size * (height + 2) * 4,
        "maps",
        scratch_shapes=[pltpu.VMEM((k_rows, size * (height + 2)), f32)],
    )
    leaf_out, node_out, root_out = call(
        functools.partial(final_kernel, fronts, height),
        (array(rows, size), array(height, rows, size), array(rows, size)),
        (solved, wide_maps, *nodes, *roots),
        6 * rows * size * size * (height + 2),
        "final",
        out_specs=(hbm,) * 3,
        scratch_shapes=[
            pltpu.VMEM((fronts, k_rows, size), f32),
            pltpu.VMEM((2, half, size), f32),
            pltpu.VMEM((2, height + 2, half, size), f32),
            pltpu.SemaphoreType.DMA((2, height + 2)),
        ],
    )
    return (leaf_out[None], node_out[None, None], root_out[None])


def solution(mesh):
    in_specs = (
        P("level", None, "blk"),
        P("level", "blk", None),
        P("level", "blk", None),
        P("level", "blk", None),
        P("level", "blk", None, None, None),
        P("level", "blk", None, None, None),
        P("level", "blk", None, None, None),
        P("level", None, None),
        P("level"),
    )
    out_specs = (
        P("level", None, "blk"),
        P("level", "blk", None, None, None),
        P("level", None, None),
    )
    return jax.shard_map(shards, mesh=mesh, in_specs=in_specs, out_specs=out_specs, check_vma=False)
```

```python
import functools

import jax
import jax.numpy as jnp
from jax import lax
from jax.experimental import pallas as pl
from jax.experimental.pallas import tpu as pltpu
from jax.sharding import PartitionSpec as P


f32 = jnp.float32
bf16 = jnp.bfloat16
VMEM_LIMIT = 12 << 20


def split(value):
    high = value.astype(bf16)
    return high, (value - high.astype(f32)).astype(bf16)


def wide_left(value):
    high, low = split(value)
    return jnp.concatenate([high, low, high], axis=1)


def wide_right(value):
    high, low = split(value)
    return jnp.concatenate([high, high, low], axis=0)


def wide_dot(left, right):
    return jnp.dot(left, right, preferred_element_type=f32)


def product(left, right):
    return wide_dot(wide_left(left), wide_right(right))


def call(kernel, out_shape, args, flops, name, in_specs=None, out_specs=None, scratch_shapes=()):
    size = lambda s: s.size * s.dtype.itemsize
    vmem = pl.BlockSpec(memory_space=pltpu.VMEM)
    moved = sum(size(a) for a in args) + sum(size(o) for o in jax.tree.leaves(out_shape))
    return pl.pallas_call(
        kernel,
        out_shape=out_shape,
        in_specs=in_specs or [vmem] * len(args),
        out_specs=out_specs or jax.tree.map(lambda _: vmem, out_shape),
        scratch_shapes=scratch_shapes,
        name=name,
        compiler_params=pltpu.CompilerParams(vmem_limit_bytes=VMEM_LIMIT),
        cost_estimate=pl.CostEstimate(flops=flops, bytes_accessed=moved, transcendentals=0),
    )(*args)


def span(index, length):
    return pl.ds(pl.multiple_of(index * length, 8), length)


def leaf_kernel(
    right, generator, inverse, lower, coupling, *refs
):
    later, (away, home, solve_map), refs = refs[:3], refs[3:6], refs[6:]
    (right_here, coupling_here, *later_here), refs = refs[:5], refs[5:]
    generator_here, inverse_here, lower_here, sems = refs
    core = lax.axis_index("blk") & 1
    half, k_half = right.shape[0] // 2, coupling.shape[0] // 2
    copies = [
        pltpu.make_async_copy(source, target, sems.at[i])
        for i, (source, target) in enumerate(
            [
                (generator, generator_here),
                (inverse, inverse_here),
                (lower, lower_here),
                (right.at[span(1 - core, half)], right_here.at[0]),
                (coupling, coupling_here),
                (right.at[span(core, half)], right_here.at[1]),
                *zip(later, later_here),
            ]
        )
    ]
    for copy in copies[:6]:
        copy.start()
    for copy in copies[:2]:
        copy.wait()
    for copy in copies[6:]:
        copy.start()
    solved = product(generator_here[:, : inverse.shape[0]], inverse_here[...])
    solve_map[...] = solved
    copies[2].wait()
    parts = wide_right(generator_here[:, inverse.shape[0] :] - product(solved, lower_here[...]))
    copies[3].wait()
    away[:half, :] = wide_dot(wide_left(right_here[0]), parts)
    copies[4].wait()
    away[half:, :] = wide_dot(wide_left(coupling_here[span(1 - core, k_half), :]), parts)
    home[half:, :] = wide_dot(wide_left(coupling_here[span(core, k_half), :]), parts)
    copies[5].wait()
    home[:half, :] = wide_dot(wide_left(right_here[1]), parts)
    for copy in copies[6:]:
        copy.wait()


def leaf_solve_kernel(child, right, coupling, solve_map, solved, leaf_map):
    parts = wide_right(solve_map[...])
    for part in range(2):
        solved[part] = wide_dot(wide_left(right[1 - part]), parts)
    on_target = lax.axis_index("blk") == child[0]
    leaf_map[...] = jnp.where(on_target, wide_dot(wide_left(coupling[...]), parts), 0.0)


def fold_kernel(first, last, generator, inverse, lower, *refs):
    if first == 0:
        home, other_maps, base, both, mine_maps = refs
    else:
        mine_maps, other_maps, both = refs[-3:]
    size = inverse.shape[1]
    for tier in range(first, last):
        solve_map = product(generator[tier, :, :size], inverse[tier])
        both[:, :size] = solve_map
        both[:, size:] = generator[tier, :, size:] - product(solve_map, lower[tier])
        upper = (lax.axis_index("blk") >> tier) & 1
        mine_maps[tier - first] = wide_right(both[span(upper, size), :])
        other_maps[tier - first] = wide_right(both[span(1 - upper, size), :])
    if first == 0:
        base[...] = wide_dot(wide_left(home[...]), mine_maps[0])


def base_kernel(index, home, mine_maps, base):
    base[...] = wide_dot(wide_left(home[...]), mine_maps[index])


def merge_kernel(index, base, away, other_maps, *refs):
    node, skeleton = refs[-2:]
    size = away.shape[1]
    both = base[...] + wide_dot(wide_left(away[...]), other_maps[index])
    skeleton[...] = both[:, size:]
    node[...] = both[:, :size]


def first_merge_kernel(half, child, base, away, other_maps, node, skeleton, carried):
    size = away.shape[1]
    position = lax.axis_index("blk")
    both = base[:half, :] + wide_dot(wide_left(away[:half, :]), other_maps[0])
    skeleton[...] = both[:, size:]
    node[...] = both[:, :size]
    carried[...] = jnp.where(position == child[0], base[half:, :], 0.0) + jnp.where(
        position ^ 1 == child[0], wide_dot(wide_left(away[half:, :]), other_maps[0]), 0.0
    )


def climb_kernel(index, carried, mine_maps, near):
    k_half, size = carried.shape
    near[:k_half, :] = carried[...]
    near[k_half:, :] = wide_dot(wide_left(carried[...]), mine_maps[index, :, size:])


def pair_kernel(index, home, away, mine_maps, other_maps, out):
    out[...] = wide_dot(wide_left(home[...]), mine_maps[index]) + wide_dot(
        wide_left(away[...]), other_maps[index]
    )


def top_kernel(index, tails, near_home, near_away, far, far_other, mine_maps, other_maps, _, out):
    k_half, size = far.shape
    count = tails.shape[0]
    out[:count] = tails[...]
    out[count] = wide_dot(wide_left(near_home[:k_half, :]), mine_maps[index, :, :size]) + wide_dot(
        wide_left(near_away[:k_half, :]), other_maps[index, :, :size]
    )
    home = near_home[k_half:, :] + near_away[k_half:, :]
    both = wide_dot(wide_left(home), mine_maps[index + 1]) + wide_dot(
        wide_left(far[...] + far_other[...]), other_maps[index + 1]
    )
    out[count + 1] = both[:, :size]
    out[count + 2] = both[:, size:]


def maps_kernel(leaf_map, home, away, wide_maps, root_map, maps):
    k_half, size = home.shape[1:]
    core = lax.axis_index("blk") & 1
    maps[:, :size] = leaf_map[...]
    for i in range(home.shape[0]):
        columns = slice((i + 1) * size, (i + 2) * size)
        maps[span(core, k_half), columns] = home[i]
        maps[span(1 - core, k_half), columns] = away[i]
    wide_maps[...] = wide_right(maps[...])
    root_map[...] = maps[:, home.shape[0] * size :]


def incoming_kernel(fronts, *refs):
    roots, root_maps, out = refs[: fronts - 1], refs[fronts - 1 : -1], refs[-1]
    level = lax.axis_index("level")

    @pl.when(level == 0)
    def _():
        out[...] = jnp.zeros_like(out)

    for here in range(1, fronts):

        @pl.when(level == here)
        def _():
            value = roots[here - 1][...]
            for front in range(1, here):
                mask = here ^ front
                value = roots[mask - 1][...] + product(value, root_maps[mask - 1][...])
            out[...] = value


def final_kernel(height, solved, wide_maps, *refs):
    nodes, refs = refs[: 2 * height], refs[2 * height :]
    roots, incoming, refs = refs[:2], refs[2:4], refs[4:]
    leaf_out, node_out, root_out, result, sems = refs
    core = lax.axis_index("blk") & 1
    half, size = solved.shape[1:]
    copies = []
    for part, which in ((0, core), (1, 1 - core)):
        rows = span(which, half)
        change = wide_dot(wide_left(incoming[part][...]), wide_maps[...])
        bases = [solved[part]] + [nodes[2 * tier + part][...] for tier in range(height)] + [roots[part][...]]
        targets = (
            [leaf_out.at[rows]] + [node_out.at[tier, rows] for tier in range(height)] + [root_out.at[rows]]
        )
        for i, (base, target) in enumerate(zip(bases, targets)):
            result[part, i] = base + change[:, i * size : (i + 1) * size]
            copies.append(pltpu.make_async_copy(result.at[part, i], target, sems.at[part, i]))
            copies[-1].start()
    for copy in copies:
        copy.wait()


def shards(
    right_sides,
    leaf_gen,
    leaf_inverse,
    leaf_lower,
    node_gen,
    node_inverse,
    node_lower,
    coupling,
    child_leaf,
):
    rows, leaf_size = right_sides.shape[1:]
    size = leaf_lower.shape[2]
    k_rows = coupling.shape[1]
    height = node_gen.shape[2]
    fronts = lax.axis_size("level")
    leaves = lax.axis_size("blk")
    half = rows // 2
    part = half + k_rows // 2
    smem = pl.BlockSpec(memory_space=pltpu.SMEM)
    vmem = pl.BlockSpec(memory_space=pltpu.VMEM)
    hbm = pl.BlockSpec(memory_space=pltpu.HBM)
    anywhere = pl.BlockSpec(memory_space=pl.ANY)
    array = lambda *shape: jax.ShapeDtypeStruct(shape, f32)

    def blk_swap(value, mask):
        return lax.ppermute(value, "blk", [(i, i ^ mask) for i in range(leaves)])

    def level_swap(value, mask):
        return lax.ppermute(value, "level", [(i, i ^ mask) for i in range(fronts)])

    away, home, leaf_solve, right_here, coupling_here, *node_params = call(
        leaf_kernel,
        (
            array(part, size),
            array(part, size),
            array(leaf_size, size),
            array(2, half, leaf_size),
            array(k_rows, leaf_size),
            array(*node_gen.shape[2:]),
            array(*node_inverse.shape[2:]),
            array(*node_lower.shape[2:]),
        ),
        tuple(
            pltpu.with_memory_space_constraint(value, pltpu.HBM)
            for value in (
                right_sides[0],
                leaf_gen[0],
                leaf_inverse[0],
                leaf_lower[0],
                coupling[0],
                node_gen[0, 0],
                node_inverse[0, 0],
                node_lower[0, 0],
            )
        ),
        6 * (rows + k_rows + leaf_size) * leaf_size * size,
        "leaf",
        in_specs=[hbm] * 8,
        scratch_shapes=[
            pltpu.VMEM((leaf_size, leaf_size), f32),
            pltpu.VMEM((size, size), f32),
            pltpu.VMEM((size, size), f32),
            pltpu.SemaphoreType.DMA((9,)),
        ],
    )

    def folds(first, last, *home, after=()):
        maps = jax.ShapeDtypeStruct((last - first, 3 * size, 2 * size), bf16)
        return call(
            functools.partial(fold_kernel, first, last),
            (maps, array(part, 2 * size)) if home else (maps, maps),
            (*node_params, *home, *after),
            (last - first) * 6 * 4 * size * size * size,
            "fold",
            in_specs=[vmem] * (3 + len(home)) + [anywhere] * len(after),
            scratch_shapes=[pltpu.VMEM((2 * size, 2 * size), f32)]
            + [pltpu.VMEM(maps.shape, bf16)] * len(home),
        )

    home, child_leaf = lax.optimization_barrier((home, child_leaf))
    other_maps, base = folds(0, 1, home)
    away = blk_swap(away, 1)
    k_half = k_rows // 2
    merge_flops = 6 * half * 2 * size * size
    node, skeleton, carried = call(
        functools.partial(first_merge_kernel, half),
        (array(half, size), array(half, size), array(k_half, 2 * size)),
        (child_leaf, base, away, other_maps),
        merge_flops,
        "merge",
        in_specs=[smem] + [vmem] * 3,
    )
    nodes, tails, carried = [node], [carried[:, :size]], carried[:, size:]
    for tier in range(1, height):
        with jax.named_scope(f"main_{tier}"):
            away = blk_swap(skeleton, 1 << tier)
        after = ()
        if tier == 1:
            mine_maps, other_maps = folds(1, height, after=(skeleton,))
        if tier < height - 2:
            both = call(
                functools.partial(pair_kernel, tier - 1),
                array(k_half, 2 * size),
                (carried, blk_swap(carried, 1 << tier), mine_maps, other_maps),
                6 * k_half * 4 * size * size,
                "pair",
            )
            tails.append(both[:, :size])
            carried = both[:, size:]
        if tier == height - 2:
            near = call(
                functools.partial(climb_kernel, tier - 1),
                array(2 * k_half, size),
                (carried, mine_maps),
                6 * k_half * size * size,
                "climb",
            )
            near_away = blk_swap(near, 1 << tier)
            far = near[k_half:]
            far_away = [blk_swap(far, 2 << tier), blk_swap(far, 3 << tier)]
            after = (near,)
        if tier == height - 1:
            home = call(
                functools.partial(top_kernel, tier - 2),
                array(height + 1, k_half, size),
                (jnp.stack(tails), near, near_away, *far_away, mine_maps, other_maps, skeleton),
                6 * k_half * 6 * size * size,
                "top",
                in_specs=[vmem] * 7 + [anywhere],
            )
            solved, leaf_map = call(
                leaf_solve_kernel,
                (array(2, half, size), array(k_rows, size)),
                (child_leaf, right_here, coupling_here, leaf_solve),
                6 * (rows + k_rows) * leaf_size * size,
                "leaf_solve",
                in_specs=[smem] + [vmem] * 3,
            )
            wide_maps, root_map = call(
                maps_kernel,
                (
                    jax.ShapeDtypeStruct((3 * k_rows, size * (height + 2)), bf16),
                    array(k_rows, size),
                ),
                (leaf_map, home, blk_swap(home, 1)),
                k_rows * size * (height + 2) * 4,
                "maps",
                scratch_shapes=[pltpu.VMEM((k_rows, size * (height + 2)), f32)],
            )
            with jax.named_scope("root_map"):
                root_maps = [level_swap(root_map, mask) for mask in range(1, fronts)]
            after = (root_map,)
        base = call(
            functools.partial(base_kernel, tier - 1),
            array(half, 2 * size),
            (skeleton, mine_maps),
            merge_flops,
            "base",
        )
        node, skeleton = call(
            functools.partial(merge_kernel, tier - 1),
            (array(half, size),) * 2,
            (base, away, other_maps, *after),
            merge_flops,
            "merge",
            in_specs=[vmem] * 3 + [anywhere] * len(after),
        )
        nodes.append(node)
    roots = [level_swap(skeleton, mask) for mask in range(1, fronts)]
    incoming = call(
        functools.partial(incoming_kernel, fronts),
        array(half, size),
        (*roots, *root_maps),
        6 * (fronts - 1) * half * size * size,
        "incoming",
    )
    pairs = []
    for value in nodes + [skeleton, incoming]:
        pairs += [value, blk_swap(value, 1)]
    leaf_out, node_out, root_out = call(
        functools.partial(final_kernel, height),
        (array(rows, size), array(height, rows, size), array(rows, size)),
        (solved, wide_maps, *pairs),
        6 * rows * size * size * (height + 2),
        "final",
        out_specs=(hbm,) * 3,
        scratch_shapes=[
            pltpu.VMEM((2, height + 2, half, size), f32),
            pltpu.SemaphoreType.DMA((2, height + 2)),
        ],
    )
    return (leaf_out[None], node_out[None, None], root_out[None])


def solution(mesh):
    in_specs = (
        P("level", None, "blk"),
        P("level", "blk", None),
        P("level", "blk", None),
        P("level", "blk", None),
        P("level", "blk", None, None, None),
        P("level", "blk", None, None, None),
        P("level", "blk", None, None, None),
        P("level", None, None),
        P("level"),
    )
    out_specs = (
        P("level", None, "blk"),
        P("level", "blk", None, None, None),
        P("level", None, None),
    )
    return jax.shard_map(shards, mesh=mesh, in_specs=in_specs, out_specs=out_specs, check_vma=False)
```

```python
import functools

import jax
import jax.numpy as jnp
from jax import lax
from jax.experimental import pallas as pl
from jax.experimental.pallas import tpu as pltpu
from jax.sharding import PartitionSpec as P


f32 = jnp.float32
bf16 = jnp.bfloat16
VMEM_LIMIT = 12 << 20


def split(value):
    high = value.astype(bf16)
    return high, (value - high.astype(f32)).astype(bf16)


def wide_left(value):
    high, low = split(value)
    return jnp.concatenate([high, low, high], axis=1)


def wide_right(value):
    high, low = split(value)
    return jnp.concatenate([high, high, low], axis=0)


def wide_dot(left, right):
    return jnp.dot(left, right, preferred_element_type=f32)


def product(left, right):
    return wide_dot(wide_left(left), wide_right(right))


def call(kernel, out_shape, args, flops, in_specs=None, out_specs=None, scratch_shapes=()):
    size = lambda s: s.size * s.dtype.itemsize
    vmem = pl.BlockSpec(memory_space=pltpu.VMEM)
    moved = sum(size(a) for a in args) + sum(size(o) for o in jax.tree.leaves(out_shape))
    return pl.pallas_call(
        kernel,
        out_shape=out_shape,
        in_specs=in_specs or [vmem] * len(args),
        out_specs=out_specs or jax.tree.map(lambda _: vmem, out_shape),
        scratch_shapes=scratch_shapes,
        compiler_params=pltpu.CompilerParams(vmem_limit_bytes=VMEM_LIMIT),
        cost_estimate=pl.CostEstimate(flops=flops, bytes_accessed=moved, transcendentals=0),
    )(*args)


def span(index, length):
    return pl.ds(pl.multiple_of(index * length, 8), length)


def leaf_kernel(
    right, generator, inverse, lower, coupling, *refs
):
    later, (away, home, solve_map), refs = refs[:3], refs[3:6], refs[6:]
    (right_here, coupling_here, *later_here), refs = refs[:5], refs[5:]
    generator_here, inverse_here, lower_here, sems = refs
    core = lax.axis_index("blk") & 1
    half, k_half = right.shape[0] // 2, coupling.shape[0] // 2
    copies = [
        pltpu.make_async_copy(source, target, sems.at[i])
        for i, (source, target) in enumerate(
            [
                (generator, generator_here),
                (inverse, inverse_here),
                (lower, lower_here),
                (right.at[span(1 - core, half)], right_here.at[0]),
                (coupling, coupling_here),
                (right.at[span(core, half)], right_here.at[1]),
                *zip(later, later_here),
            ]
        )
    ]
    for copy in copies[:6]:
        copy.start()
    for copy in copies[:2]:
        copy.wait()
    for copy in copies[6:]:
        copy.start()
    solved = product(generator_here[:, : inverse.shape[0]], inverse_here[...])
    solve_map[...] = solved
    copies[2].wait()
    parts = wide_right(generator_here[:, inverse.shape[0] :] - product(solved, lower_here[...]))
    copies[3].wait()
    away[:half, :] = wide_dot(wide_left(right_here[0]), parts)
    copies[4].wait()
    away[half:, :] = wide_dot(wide_left(coupling_here[span(1 - core, k_half), :]), parts)
    home[half:, :] = wide_dot(wide_left(coupling_here[span(core, k_half), :]), parts)
    copies[5].wait()
    home[:half, :] = wide_dot(wide_left(right_here[1]), parts)
    for copy in copies[6:]:
        copy.wait()


def leaf_solve_kernel(child, right, coupling, solve_map, solved, leaf_map):
    parts = wide_right(solve_map[...])
    for part in range(2):
        solved[part] = wide_dot(wide_left(right[1 - part]), parts)
    on_target = lax.axis_index("blk") == child[0]
    leaf_map[...] = jnp.where(on_target, wide_dot(wide_left(coupling[...]), parts), 0.0)


def fold_kernel(first, last, generator, inverse, lower, *refs):
    if first == 0:
        home, other_maps, base, both, mine_maps = refs
    else:
        mine_maps, other_maps, both = refs[-3:]
    size = inverse.shape[1]
    for tier in range(first, last):
        solve_map = product(generator[tier, :, :size], inverse[tier])
        both[:, :size] = solve_map
        both[:, size:] = generator[tier, :, size:] - product(solve_map, lower[tier])
        upper = (lax.axis_index("blk") >> tier) & 1
        mine_maps[tier - first] = wide_right(both[span(upper, size), :])
        other_maps[tier - first] = wide_right(both[span(1 - upper, size), :])
    if first == 0:
        base[...] = wide_dot(wide_left(home[...]), mine_maps[0])


def base_kernel(index, home, mine_maps, base):
    base[...] = wide_dot(wide_left(home[...]), mine_maps[index])


def merge_kernel(index, base, away, other_maps, *refs):
    node, skeleton = refs[-2:]
    size = away.shape[1]
    both = base[...] + wide_dot(wide_left(away[...]), other_maps[index])
    skeleton[...] = both[:, size:]
    node[...] = both[:, :size]


def first_merge_kernel(half, child, base, away, other_maps, node, skeleton, carried):
    size = away.shape[1]
    position = lax.axis_index("blk")
    both = base[:half, :] + wide_dot(wide_left(away[:half, :]), other_maps[0])
    skeleton[...] = both[:, size:]
    node[...] = both[:, :size]
    carried[...] = jnp.where(position == child[0], base[half:, :], 0.0) + jnp.where(
        position ^ 1 == child[0], wide_dot(wide_left(away[half:, :]), other_maps[0]), 0.0
    )


def climb_kernel(index, carried, mine_maps, near):
    k_half, size = carried.shape
    near[:k_half, :] = carried[...]
    near[k_half:, :] = wide_dot(wide_left(carried[...]), mine_maps[index, :, size:])


def pair_kernel(index, home, away, mine_maps, other_maps, out):
    out[...] = wide_dot(wide_left(home[...]), mine_maps[index]) + wide_dot(
        wide_left(away[...]), other_maps[index]
    )


def top_kernel(index, tails, near_home, near_away, far, far_other, mine_maps, other_maps, out):
    k_half, size = far.shape
    count = tails.shape[0]
    out[:count] = tails[...]
    out[count] = wide_dot(wide_left(near_home[:k_half, :]), mine_maps[index, :, :size]) + wide_dot(
        wide_left(near_away[:k_half, :]), other_maps[index, :, :size]
    )
    home = near_home[k_half:, :] + near_away[k_half:, :]
    both = wide_dot(wide_left(home), mine_maps[index + 1]) + wide_dot(
        wide_left(far[...] + far_other[...]), other_maps[index + 1]
    )
    out[count + 1] = both[:, :size]
    out[count + 2] = both[:, size:]


def maps_kernel(leaf_map, home, away, wide_maps, root_map, maps):
    k_half, size = home.shape[1:]
    core = lax.axis_index("blk") & 1
    maps[:, :size] = leaf_map[...]
    for i in range(home.shape[0]):
        columns = slice((i + 1) * size, (i + 2) * size)
        maps[span(core, k_half), columns] = home[i]
        maps[span(1 - core, k_half), columns] = away[i]
    wide_maps[...] = wide_right(maps[...])
    root_map[...] = maps[:, home.shape[0] * size :]


def incoming_kernel(fronts, *refs):
    roots, root_maps, out = refs[: fronts - 1], refs[fronts - 1 : -1], refs[-1]
    level = lax.axis_index("level")

    @pl.when(level == 0)
    def _():
        out[...] = jnp.zeros_like(out)

    for here in range(1, fronts):

        @pl.when(level == here)
        def _():
            value = roots[here - 1][...]
            for front in range(1, here):
                mask = here ^ front
                value = roots[mask - 1][...] + product(value, root_maps[mask - 1][...])
            out[...] = value


def final_kernel(height, solved, wide_maps, *refs):
    nodes, refs = refs[: 2 * height], refs[2 * height :]
    roots, incoming, refs = refs[:2], refs[2:4], refs[4:]
    leaf_out, node_out, root_out, result, sems = refs
    core = lax.axis_index("blk") & 1
    half, size = solved.shape[1:]
    copies = []
    for part, which in ((0, core), (1, 1 - core)):
        rows = span(which, half)
        change = wide_dot(wide_left(incoming[part][...]), wide_maps[...])
        bases = [solved[part]] + [nodes[2 * tier + part][...] for tier in range(height)] + [roots[part][...]]
        targets = (
            [leaf_out.at[rows]] + [node_out.at[tier, rows] for tier in range(height)] + [root_out.at[rows]]
        )
        for i, (base, target) in enumerate(zip(bases, targets)):
            result[part, i] = base + change[:, i * size : (i + 1) * size]
            copies.append(pltpu.make_async_copy(result.at[part, i], target, sems.at[part, i]))
            copies[-1].start()
    for copy in copies:
        copy.wait()


def shards(
    right_sides,
    leaf_gen,
    leaf_inverse,
    leaf_lower,
    node_gen,
    node_inverse,
    node_lower,
    coupling,
    child_leaf,
):
    rows, leaf_size = right_sides.shape[1:]
    size = leaf_lower.shape[2]
    k_rows = coupling.shape[1]
    height = node_gen.shape[2]
    fronts = lax.axis_size("level")
    leaves = lax.axis_size("blk")
    half = rows // 2
    part = half + k_rows // 2
    smem = pl.BlockSpec(memory_space=pltpu.SMEM)
    vmem = pl.BlockSpec(memory_space=pltpu.VMEM)
    hbm = pl.BlockSpec(memory_space=pltpu.HBM)
    anywhere = pl.BlockSpec(memory_space=pl.ANY)
    array = lambda *shape: jax.ShapeDtypeStruct(shape, f32)

    def blk_swap(value, mask):
        return lax.ppermute(value, "blk", [(i, i ^ mask) for i in range(leaves)])

    def level_swap(value, mask):
        return lax.ppermute(value, "level", [(i, i ^ mask) for i in range(fronts)])

    away, home, leaf_solve, right_here, coupling_here, *node_params = call(
        leaf_kernel,
        (
            array(part, size),
            array(part, size),
            array(leaf_size, size),
            array(2, half, leaf_size),
            array(k_rows, leaf_size),
            array(*node_gen.shape[2:]),
            array(*node_inverse.shape[2:]),
            array(*node_lower.shape[2:]),
        ),
        tuple(
            pltpu.with_memory_space_constraint(value, pltpu.HBM)
            for value in (
                right_sides[0],
                leaf_gen[0],
                leaf_inverse[0],
                leaf_lower[0],
                coupling[0],
                node_gen[0, 0],
                node_inverse[0, 0],
                node_lower[0, 0],
            )
        ),
        6 * (rows + k_rows + leaf_size) * leaf_size * size,
        in_specs=[hbm] * 8,
        scratch_shapes=[
            pltpu.VMEM((leaf_size, leaf_size), f32),
            pltpu.VMEM((size, size), f32),
            pltpu.VMEM((size, size), f32),
            pltpu.SemaphoreType.DMA((9,)),
        ],
    )

    def folds(first, last, *home, after=()):
        maps = jax.ShapeDtypeStruct((last - first, 3 * size, 2 * size), bf16)
        return call(
            functools.partial(fold_kernel, first, last),
            (maps, array(part, 2 * size)) if home else (maps, maps),
            (*node_params, *home, *after),
            (last - first) * 6 * 4 * size * size * size,
            in_specs=[vmem] * (3 + len(home)) + [anywhere] * len(after),
            scratch_shapes=[pltpu.VMEM((2 * size, 2 * size), f32)]
            + [pltpu.VMEM(maps.shape, bf16)] * len(home),
        )

    home, child_leaf = lax.optimization_barrier((home, child_leaf))
    other_maps, base = folds(0, 1, home)
    away = blk_swap(away, 1)
    k_half = k_rows // 2
    merge_flops = 6 * half * 2 * size * size
    node, skeleton, carried = call(
        functools.partial(first_merge_kernel, half),
        (array(half, size), array(half, size), array(k_half, 2 * size)),
        (child_leaf, base, away, other_maps),
        merge_flops,
        in_specs=[smem] + [vmem] * 3,
    )
    nodes, tails, carried = [node], [carried[:, :size]], carried[:, size:]
    for tier in range(1, height):
        away = blk_swap(skeleton, 1 << tier)
        after = ()
        if tier == 1:
            mine_maps, other_maps = folds(1, height, after=(skeleton,))
        if tier < height - 2:
            both = call(
                functools.partial(pair_kernel, tier - 1),
                array(k_half, 2 * size),
                (carried, blk_swap(carried, 1 << tier), mine_maps, other_maps),
                6 * k_half * 4 * size * size,
            )
            tails.append(both[:, :size])
            carried = both[:, size:]
        if tier == height - 2:
            near = call(
                functools.partial(climb_kernel, tier - 1),
                array(2 * k_half, size),
                (carried, mine_maps),
                6 * k_half * size * size,
            )
            near_away = blk_swap(near, 1 << tier)
            far = near[k_half:]
            far_away = [blk_swap(far, 2 << tier)]
            far_away.append(blk_swap(far, 3 << tier))
            after = (near,)
        if tier == height - 1:
            home = call(
                functools.partial(top_kernel, tier - 2),
                array(height + 1, k_half, size),
                (jnp.stack(tails), near, near_away, *far_away, mine_maps, other_maps),
                6 * k_half * 6 * size * size,
            )
            solved, leaf_map = call(
                leaf_solve_kernel,
                (array(2, half, size), array(k_rows, size)),
                (child_leaf, right_here, coupling_here, leaf_solve),
                6 * (rows + k_rows) * leaf_size * size,
                in_specs=[smem] + [vmem] * 3,
            )
            wide_maps, root_map = call(
                maps_kernel,
                (
                    jax.ShapeDtypeStruct((3 * k_rows, size * (height + 2)), bf16),
                    array(k_rows, size),
                ),
                (leaf_map, home, blk_swap(home, 1)),
                k_rows * size * (height + 2) * 4,
                scratch_shapes=[pltpu.VMEM((k_rows, size * (height + 2)), f32)],
            )
            root_maps = [level_swap(root_map, mask) for mask in range(1, fronts)]
            after = (root_map,)
        base = call(
            functools.partial(base_kernel, tier - 1),
            array(half, 2 * size),
            (skeleton, mine_maps),
            merge_flops,
        )
        node, skeleton = call(
            functools.partial(merge_kernel, tier - 1),
            (array(half, size),) * 2,
            (base, away, other_maps, *after),
            merge_flops,
            in_specs=[vmem] * 3 + [anywhere] * len(after),
        )
        nodes.append(node)
    roots = [level_swap(skeleton, mask) for mask in range(1, fronts)]
    incoming = call(
        functools.partial(incoming_kernel, fronts),
        array(half, size),
        (*roots, *root_maps),
        6 * (fronts - 1) * half * size * size,
    )
    pairs = []
    for value in nodes + [skeleton, incoming]:
        pairs += [value, blk_swap(value, 1)]
    leaf_out, node_out, root_out = call(
        functools.partial(final_kernel, height),
        (array(rows, size), array(height, rows, size), array(rows, size)),
        (solved, wide_maps, *pairs),
        6 * rows * size * size * (height + 2),
        out_specs=(hbm,) * 3,
        scratch_shapes=[
            pltpu.VMEM((2, height + 2, half, size), f32),
            pltpu.SemaphoreType.DMA((2, height + 2)),
        ],
    )
    return (leaf_out[None], node_out[None, None], root_out[None])


def solution(mesh):
    in_specs = (
        P("level", None, "blk"),
        P("level", "blk", None),
        P("level", "blk", None),
        P("level", "blk", None),
        P("level", "blk", None, None, None),
        P("level", "blk", None, None, None),
        P("level", "blk", None, None, None),
        P("level", None, None),
        P("level"),
    )
    out_specs = (
        P("level", None, "blk"),
        P("level", "blk", None, None, None),
        P("level", None, None),
    )

    return jax.shard_map(shards, mesh=mesh, in_specs=in_specs, out_specs=out_specs, check_vma=False)
```

```python
import functools

import jax
import jax.numpy as jnp
from jax import lax
from jax.experimental import pallas as pl
from jax.experimental.pallas import tpu as pltpu
from jax.sharding import PartitionSpec as P


f32 = jnp.float32
bf16 = jnp.bfloat16
VMEM_LIMIT = 12 << 20


def split(value):
    high = value.astype(bf16)
    return high, (value - high.astype(f32)).astype(bf16)


def wide_left(value):
    high, low = split(value)
    return jnp.concatenate([high, low, high], axis=1)


def wide_right(value):
    high, low = split(value)
    return jnp.concatenate([high, high, low], axis=0)


def wide_dot(left, right):
    return jnp.dot(left, right, preferred_element_type=f32)


def product(left, right):
    return wide_dot(wide_left(left), wide_right(right))


def call(kernel, out_shape, args, flops, in_specs=None, out_specs=None, scratch_shapes=()):
    size = lambda s: s.size * s.dtype.itemsize
    vmem = pl.BlockSpec(memory_space=pltpu.VMEM)
    moved = sum(size(a) for a in args) + sum(size(o) for o in jax.tree.leaves(out_shape))
    return pl.pallas_call(
        kernel,
        out_shape=out_shape,
        in_specs=in_specs or [vmem] * len(args),
        out_specs=out_specs or jax.tree.map(lambda _: vmem, out_shape),
        scratch_shapes=scratch_shapes,
        compiler_params=pltpu.CompilerParams(vmem_limit_bytes=VMEM_LIMIT),
        cost_estimate=pl.CostEstimate(flops=flops, bytes_accessed=moved, transcendentals=0),
    )(*args)


def span(index, length):
    return pl.ds(pl.multiple_of(index * length, 8), length)


def leaf_kernel(
    right, generator, inverse, lower, coupling, *refs
):
    later, (away, home, solve_map), refs = refs[:3], refs[3:6], refs[6:]
    (right_here, coupling_here, *later_here), refs = refs[:5], refs[5:]
    generator_here, inverse_here, lower_here, sems = refs
    core = lax.axis_index("blk") & 1
    half, k_half = right.shape[0] // 2, coupling.shape[0] // 2
    copies = [
        pltpu.make_async_copy(source, target, sems.at[i])
        for i, (source, target) in enumerate(
            [
                (generator, generator_here),
                (inverse, inverse_here),
                (lower, lower_here),
                (right.at[span(1 - core, half)], right_here.at[0]),
                (coupling, coupling_here),
                (right.at[span(core, half)], right_here.at[1]),
                *zip(later, later_here),
            ]
        )
    ]
    for copy in copies[:6]:
        copy.start()
    for copy in copies[:2]:
        copy.wait()
    for copy in copies[6:]:
        copy.start()
    solved = product(generator_here[:, : inverse.shape[0]], inverse_here[...])
    solve_map[...] = solved
    copies[2].wait()
    parts = wide_right(generator_here[:, inverse.shape[0] :] - product(solved, lower_here[...]))
    copies[3].wait()
    away[:half, :] = wide_dot(wide_left(right_here[0]), parts)
    copies[4].wait()
    away[half:, :] = wide_dot(wide_left(coupling_here[span(1 - core, k_half), :]), parts)
    home[half:, :] = wide_dot(wide_left(coupling_here[span(core, k_half), :]), parts)
    copies[5].wait()
    home[:half, :] = wide_dot(wide_left(right_here[1]), parts)
    for copy in copies[6:]:
        copy.wait()


def leaf_solve_kernel(child, right, coupling, solve_map, solved, leaf_map):
    parts = wide_right(solve_map[...])
    for part in range(2):
        solved[part] = wide_dot(wide_left(right[1 - part]), parts)
    on_target = lax.axis_index("blk") == child[0]
    leaf_map[...] = jnp.where(on_target, wide_dot(wide_left(coupling[...]), parts), 0.0)


def fold_kernel(first, last, generator, inverse, lower, *refs):
    if first == 0:
        home, other_maps, base, both, mine_maps = refs
    else:
        mine_maps, other_maps, both = refs[-3:]
    size = inverse.shape[1]
    for tier in range(first, last):
        solve_map = product(generator[tier, :, :size], inverse[tier])
        both[:, :size] = solve_map
        both[:, size:] = generator[tier, :, size:] - product(solve_map, lower[tier])
        upper = (lax.axis_index("blk") >> tier) & 1
        mine_maps[tier - first] = wide_right(both[span(upper, size), :])
        other_maps[tier - first] = wide_right(both[span(1 - upper, size), :])
    if first == 0:
        base[...] = wide_dot(wide_left(home[...]), mine_maps[0])


def base_kernel(index, home, mine_maps, base):
    base[...] = wide_dot(wide_left(home[...]), mine_maps[index])


def merge_kernel(index, base, away, other_maps, *refs):
    node, skeleton = refs[-2:]
    size = away.shape[1]
    both = base[...] + wide_dot(wide_left(away[...]), other_maps[index])
    skeleton[...] = both[:, size:]
    node[...] = both[:, :size]


def first_merge_kernel(half, child, base, away, other_maps, node, skeleton, carried):
    size = away.shape[1]
    position = lax.axis_index("blk")
    both = base[:half, :] + wide_dot(wide_left(away[:half, :]), other_maps[0])
    skeleton[...] = both[:, size:]
    node[...] = both[:, :size]
    carried[...] = jnp.where(position == child[0], base[half:, :], 0.0) + jnp.where(
        position ^ 1 == child[0], wide_dot(wide_left(away[half:, :]), other_maps[0]), 0.0
    )


def climb_kernel(index, carried, mine_maps, climb):
    size = carried.shape[1]
    climb[...] = wide_dot(wide_left(carried[...]), mine_maps[index, :, size:])


def relay_kernel(carried, climb, far, out):
    for i, value in enumerate((carried, climb, far)):
        out[i] = value[...]


def pair_kernel(index, home, away, mine_maps, other_maps, out):
    out[...] = wide_dot(wide_left(home[...]), mine_maps[index]) + wide_dot(
        wide_left(away[...]), other_maps[index]
    )


def top_kernel(index, tails, home, away, mine_maps, other_maps, out):
    size = tails.shape[2]
    count = tails.shape[0]
    out[:count] = tails[...]
    out[count] = wide_dot(wide_left(home[0]), mine_maps[index, :, :size]) + wide_dot(
        wide_left(away[0]), other_maps[index, :, :size]
    )
    both = wide_dot(wide_left(home[1] + away[1]), mine_maps[index + 1]) + wide_dot(
        wide_left(home[2] + away[2]), other_maps[index + 1]
    )
    out[count + 1] = both[:, :size]
    out[count + 2] = both[:, size:]


def last_merge_kernel(index, base, away, other_maps, tails, *refs):
    node, root = refs[-2:]
    half, size = away.shape
    both = base[...] + wide_dot(wide_left(away[...]), other_maps[index])
    root[:half, :] = both[:, size:]
    root[half:, :] = tails[tails.shape[0] - 1]
    node[...] = both[:, :size]


def maps_kernel(leaf_map, home, away, *refs):
    wide_maps, maps = refs[-2:]
    k_half, size = home.shape[1:]
    core = lax.axis_index("blk") & 1
    maps[:, :size] = leaf_map[...]
    for i in range(home.shape[0]):
        columns = slice((i + 1) * size, (i + 2) * size)
        maps[span(core, k_half), columns] = home[i]
        maps[span(1 - core, k_half), columns] = away[i]
    wide_maps[...] = wide_right(maps[...])


def final_kernel(fronts, height, solved, wide_maps, *refs):
    nodes, refs = refs[: 2 * height], refs[2 * height :]
    roots, refs = refs[: 2 * fronts], refs[2 * fronts :]
    leaf_out, node_out, root_out, root_maps, incoming, result, sems = refs
    core, level = lax.axis_index("blk") & 1, lax.axis_index("level")
    half, size = solved.shape[1:]
    k_half = root_maps.shape[1] // 2
    for front in range(1, fronts):
        root_maps[front, span(core, k_half), :] = roots[2 * front][half:, :]
        root_maps[front, span(1 - core, k_half), :] = roots[2 * front + 1][half:, :]

    @pl.when(level == 0)
    def _():
        incoming[...] = jnp.zeros_like(incoming)

    for here in range(1, fronts):

        @pl.when(level == here)
        def _():
            for part in range(2):
                value = roots[2 * here + part][:half, :]
                for front in range(1, here):
                    value = roots[2 * (here ^ front) + part][:half, :] + product(
                        value, root_maps[here ^ front]
                    )
                incoming[part] = value

    copies = []
    for part, which in ((0, core), (1, 1 - core)):
        rows = span(which, half)
        change = wide_dot(wide_left(incoming[part]), wide_maps[...])
        bases = (
            [solved[part]]
            + [nodes[2 * tier + part][...] for tier in range(height)]
            + [roots[part][:half, :]]
        )
        targets = (
            [leaf_out.at[rows]] + [node_out.at[tier, rows] for tier in range(height)] + [root_out.at[rows]]
        )
        for i, (base, target) in enumerate(zip(bases, targets)):
            result[part, i] = base + change[:, i * size : (i + 1) * size]
            copies.append(pltpu.make_async_copy(result.at[part, i], target, sems.at[part, i]))
            copies[-1].start()
    for copy in copies:
        copy.wait()


def shards(
    right_sides,
    leaf_gen,
    leaf_inverse,
    leaf_lower,
    node_gen,
    node_inverse,
    node_lower,
    coupling,
    child_leaf,
):
    rows, leaf_size = right_sides.shape[1:]
    size = leaf_lower.shape[2]
    k_rows = coupling.shape[1]
    height = node_gen.shape[2]
    fronts = lax.axis_size("level")
    leaves = lax.axis_size("blk")
    half = rows // 2
    part = half + k_rows // 2
    smem = pl.BlockSpec(memory_space=pltpu.SMEM)
    vmem = pl.BlockSpec(memory_space=pltpu.VMEM)
    hbm = pl.BlockSpec(memory_space=pltpu.HBM)
    anywhere = pl.BlockSpec(memory_space=pl.ANY)
    array = lambda *shape: jax.ShapeDtypeStruct(shape, f32)

    def blk_swap(value, mask):
        return lax.ppermute(value, "blk", [(i, i ^ mask) for i in range(leaves)])

    def level_swap(value, mask):
        return lax.ppermute(value, "level", [(i, i ^ mask) for i in range(fronts)])

    away, home, leaf_solve, right_here, coupling_here, *node_params = call(
        leaf_kernel,
        (
            array(part, size),
            array(part, size),
            array(leaf_size, size),
            array(2, half, leaf_size),
            array(k_rows, leaf_size),
            array(*node_gen.shape[2:]),
            array(*node_inverse.shape[2:]),
            array(*node_lower.shape[2:]),
        ),
        tuple(
            pltpu.with_memory_space_constraint(value, pltpu.HBM)
            for value in (
                right_sides[0],
                leaf_gen[0],
                leaf_inverse[0],
                leaf_lower[0],
                coupling[0],
                node_gen[0, 0],
                node_inverse[0, 0],
                node_lower[0, 0],
            )
        ),
        6 * (rows + k_rows + leaf_size) * leaf_size * size,
        in_specs=[hbm] * 8,
        scratch_shapes=[
            pltpu.VMEM((leaf_size, leaf_size), f32),
            pltpu.VMEM((size, size), f32),
            pltpu.VMEM((size, size), f32),
            pltpu.SemaphoreType.DMA((9,)),
        ],
    )

    def folds(first, last, *home):
        maps = jax.ShapeDtypeStruct((last - first, 3 * size, 2 * size), bf16)
        return call(
            functools.partial(fold_kernel, first, last),
            (maps, array(part, 2 * size)) if home else (maps, maps),
            (*node_params, *home),
            (last - first) * 6 * 4 * size * size * size,
            scratch_shapes=[pltpu.VMEM((2 * size, 2 * size), f32)]
            + [pltpu.VMEM(maps.shape, bf16)] * len(home),
        )

    home, child_leaf = lax.optimization_barrier((home, child_leaf))
    other_maps, base = folds(0, 1, home)
    away = blk_swap(away, 1)
    k_half = k_rows // 2
    merge_flops = 6 * half * 2 * size * size
    node, skeleton, carried = call(
        functools.partial(first_merge_kernel, half),
        (array(half, size), array(half, size), array(k_half, 2 * size)),
        (child_leaf, base, away, other_maps),
        merge_flops,
        in_specs=[smem] + [vmem] * 3,
    )
    nodes, tails, carried = [node], [carried[:, :size]], carried[:, size:]
    for tier in range(1, height):
        away = blk_swap(skeleton, 1 << tier)
        after = ()
        if tier == 1:
            mine_maps, other_maps = folds(1, height)
        if tier < height - 2:
            both = call(
                functools.partial(pair_kernel, tier - 1),
                array(k_half, 2 * size),
                (carried, blk_swap(carried, 1 << tier), mine_maps, other_maps),
                6 * k_half * 4 * size * size,
            )
            tails.append(both[:, :size])
            carried = both[:, size:]
        if tier == height - 2:
            climb = call(
                functools.partial(climb_kernel, tier - 1),
                array(k_half, size),
                (carried, mine_maps),
                6 * k_half * size * size,
            )
            far = blk_swap(climb, 2 << tier)
            after = (climb,)
        if tier == height - 1:
            relay = call(relay_kernel, array(3, k_half, size), (carried, climb, far), k_half * size)
            relayed = blk_swap(relay, 1 << (tier - 1))
            tails = call(
                functools.partial(top_kernel, tier - 2),
                array(height + 1, k_half, size),
                (jnp.stack(tails), relay, relayed, mine_maps, other_maps),
                6 * k_half * 6 * size * size,
            )
            solved, leaf_map = call(
                leaf_solve_kernel,
                (array(2, half, size), array(k_rows, size)),
                (child_leaf, right_here, coupling_here, leaf_solve),
                6 * (rows + k_rows) * leaf_size * size,
                in_specs=[smem] + [vmem] * 3,
            )
            after = (solved,)
        base = call(
            functools.partial(base_kernel, tier - 1),
            array(half, 2 * size),
            (skeleton, mine_maps),
            merge_flops,
        )
        last = tier == height - 1
        node, skeleton = call(
            functools.partial(last_merge_kernel if last else merge_kernel, tier - 1),
            (array(half, size), array(part if last else half, size)),
            (base, away, other_maps) + ((tails,) if last else ()) + after,
            merge_flops,
            in_specs=[vmem] * (4 if last else 3) + [anywhere] * len(after),
        )
        nodes.append(node)
    received = [level_swap(skeleton, mask) for mask in range(1, fronts)]
    roots = [skeleton, blk_swap(skeleton, 1)]
    for value in received:
        roots += [value, blk_swap(value, 1)]
    pairs = []
    for value in nodes:
        pairs += [value, blk_swap(value, 1)]
    after = (*pairs[1::2], roots[1])
    wide_maps = call(
        maps_kernel,
        jax.ShapeDtypeStruct((3 * k_rows, size * (height + 2)), bf16),
        (leaf_map, tails, blk_swap(tails, 1), *after),
        k_rows * size * (height + 2) * 4,
        in_specs=[vmem] * 3 + [anywhere] * len(after),
        scratch_shapes=[pltpu.VMEM((k_rows, size * (height + 2)), f32)],
    )
    leaf_out, node_out, root_out = call(
        functools.partial(final_kernel, fronts, height),
        (array(rows, size), array(height, rows, size), array(rows, size)),
        (solved, wide_maps, *pairs, *roots),
        6 * rows * size * size * (height + 2),
        out_specs=(hbm,) * 3,
        scratch_shapes=[
            pltpu.VMEM((fronts, k_rows, size), f32),
            pltpu.VMEM((2, half, size), f32),
            pltpu.VMEM((2, height + 2, half, size), f32),
            pltpu.SemaphoreType.DMA((2, height + 2)),
        ],
    )
    return (leaf_out[None], node_out[None, None], root_out[None])


def solution(mesh):
    in_specs = (
        P("level", None, "blk"),
        P("level", "blk", None),
        P("level", "blk", None),
        P("level", "blk", None),
        P("level", "blk", None, None, None),
        P("level", "blk", None, None, None),
        P("level", "blk", None, None, None),
        P("level", None, None),
        P("level"),
    )
    out_specs = (
        P("level", None, "blk"),
        P("level", "blk", None, None, None),
        P("level", None, None),
    )

    return jax.shard_map(shards, mesh=mesh, in_specs=in_specs, out_specs=out_specs, check_vma=False)
```

```python
import functools

import jax
import jax.numpy as jnp
from jax import lax
from jax.experimental import pallas as pl
from jax.experimental.pallas import tpu as pltpu
from jax.sharding import PartitionSpec as P


f32 = jnp.float32
bf16 = jnp.bfloat16
VMEM_LIMIT = 12 << 20


def split(value):
    high = value.astype(bf16)
    return high, (value - high.astype(f32)).astype(bf16)


def wide_left(value):
    high, low = split(value)
    return jnp.concatenate([high, low, high], axis=1)


def wide_right(value):
    high, low = split(value)
    return jnp.concatenate([high, high, low], axis=0)


def wide_dot(left, right):
    return jnp.dot(left, right, preferred_element_type=f32)


def product(left, right):
    return wide_dot(wide_left(left), wide_right(right))


def call(kernel, out_shape, args, flops, in_specs=None, out_specs=None, scratch_shapes=()):
    size = lambda s: s.size * s.dtype.itemsize
    vmem = pl.BlockSpec(memory_space=pltpu.VMEM)
    moved = sum(size(a) for a in args) + sum(size(o) for o in jax.tree.leaves(out_shape))
    return pl.pallas_call(
        kernel,
        out_shape=out_shape,
        in_specs=in_specs or [vmem] * len(args),
        out_specs=out_specs or jax.tree.map(lambda _: vmem, out_shape),
        scratch_shapes=scratch_shapes,
        compiler_params=pltpu.CompilerParams(vmem_limit_bytes=VMEM_LIMIT),
        cost_estimate=pl.CostEstimate(flops=flops, bytes_accessed=moved, transcendentals=0),
    )(*args)


def span(index, length):
    return pl.ds(pl.multiple_of(index * length, 8), length)


def leaf_kernel(right, generator, inverse, lower, coupling, *refs):
    later, (away, solve_map, skeleton_map), refs = refs[:3], refs[3:6], refs[6:]
    (right_here, coupling_here, *later_here), refs = refs[:5], refs[5:]
    generator_here, inverse_here, lower_here, sems = refs
    core = lax.axis_index("blk") & 1
    half, k_half = right.shape[0] // 2, coupling.shape[0] // 2
    size = inverse.shape[0]
    copies = [
        pltpu.make_async_copy(source, target, sems.at[i])
        for i, (source, target) in enumerate(
            [
                (generator, generator_here),
                (inverse, inverse_here),
                (lower, lower_here),
                (right.at[span(1 - core, half)], right_here.at[0]),
                (coupling, coupling_here),
                (right.at[span(core, half)], right_here.at[1]),
                *((source.at[0], target) for source, target in zip(later, later_here)),
            ]
        )
    ]
    for copy in copies:
        copy.start()
    for copy in copies[:2]:
        copy.wait()
    solved = product(generator_here[:, :size], inverse_here[...])
    solve_map[...] = solved
    copies[2].wait()
    parts = wide_right(generator_here[:, size:] - product(solved, lower_here[...]))
    skeleton_map[...] = parts
    copies[3].wait()
    away[:half, :] = wide_dot(wide_left(right_here[0]), parts)
    copies[4].wait()
    away[half:, :] = wide_dot(wide_left(coupling_here[span(1 - core, k_half), :]), parts)
    for copy in copies[5:]:
        copy.wait()


def leaf_solve_kernel(child, right, coupling, solve_map, solved, leaf_map):
    parts = wide_right(solve_map[...])
    for part in range(2):
        solved[part] = wide_dot(wide_left(right[1 - part]), parts)
    on_target = lax.axis_index("blk") == child[0]
    leaf_map[...] = jnp.where(on_target, wide_dot(wide_left(coupling[...]), parts), 0.0)


def fold(tier, generator, inverse, lower, both):
    size = inverse.shape[0]
    solve_map = product(generator[:, :size], inverse)
    both[:, :size] = solve_map
    both[:, size:] = generator[:, size:] - product(solve_map, lower)
    upper = (lax.axis_index("blk") >> tier) & 1
    return wide_right(both[span(upper, size), :]), wide_right(both[span(1 - upper, size), :])


def first_fold_kernel(
    generator, inverse, lower, right, coupling, skeleton_map, mine_maps, other_maps, base, home, both
):
    core = lax.axis_index("blk") & 1
    k_half = home.shape[0]
    value = wide_dot(wide_left(right[1]), skeleton_map[...])
    home[...] = wide_dot(wide_left(coupling[span(core, k_half), :]), skeleton_map[...])
    mine_maps[0], other_maps[0] = fold(0, generator[...], inverse[...], lower[...], both)
    base[...] = wide_dot(wide_left(value), mine_maps[0])


def fold_kernel(generator, inverse, lower, mine_maps, other_maps, both):
    for tier in range(1, generator.shape[0]):
        mine_maps[tier - 1], other_maps[tier - 1] = fold(
            tier, generator[tier], inverse[tier], lower[tier], both
        )


def base_kernel(index, home, mine_maps, base):
    base[...] = wide_dot(wide_left(home[...]), mine_maps[index])


def merge_kernel(index, base, away, other_maps, *refs):
    node, skeleton = refs[-2:]
    size = away.shape[1]
    both = base[...] + wide_dot(wide_left(away[...]), other_maps[index])
    skeleton[...] = both[:, size:]
    node[...] = both[:, :size]


def first_merge_kernel(base, away, other_maps, node, skeleton):
    half, size = node.shape
    both = base[...] + wide_dot(wide_left(away[:half, :]), other_maps[0])
    skeleton[...] = both[:, size:]
    node[...] = both[:, :size]


def carry_kernel(child, home, away, mine_maps, other_maps, tail, carried):
    k_half, size = home.shape
    position = lax.axis_index("blk")
    mine = wide_dot(wide_left(home[...]), mine_maps[0])
    other = wide_dot(wide_left(away[away.shape[0] - k_half :, :]), other_maps[0])
    both = jnp.where(position == child[0], mine, 0.0) + jnp.where(position ^ 1 == child[0], other, 0.0)
    tail[...] = both[:, :size]
    carried[...] = both[:, size:]


def climb_kernel(index, carried, mine_maps, climb):
    size = carried.shape[1]
    climb[...] = wide_dot(wide_left(carried[...]), mine_maps[index, :, size:])


def relay_kernel(carried, climb, far, out):
    for i, value in enumerate((carried, climb, far)):
        out[i] = value[...]


def pair_kernel(index, home, away, mine_maps, other_maps, out):
    out[...] = wide_dot(wide_left(home[...]), mine_maps[index]) + wide_dot(
        wide_left(away[...]), other_maps[index]
    )


def top_kernel(index, tails, home, away, mine_maps, other_maps, out):
    size = tails.shape[2]
    count = tails.shape[0]
    out[:count] = tails[...]
    out[count] = wide_dot(wide_left(home[0]), mine_maps[index, :, :size]) + wide_dot(
        wide_left(away[0]), other_maps[index, :, :size]
    )
    both = wide_dot(wide_left(home[1] + away[1]), mine_maps[index + 1]) + wide_dot(
        wide_left(home[2] + away[2]), other_maps[index + 1]
    )
    out[count + 1] = both[:, :size]
    out[count + 2] = both[:, size:]


def last_merge_kernel(index, base, away, other_maps, tails, *refs):
    node, root = refs[-2:]
    half, size = away.shape
    both = base[...] + wide_dot(wide_left(away[...]), other_maps[index])
    root[:half, :] = both[:, size:]
    root[half:, :] = tails[tails.shape[0] - 1]
    node[...] = both[:, :size]


def maps_kernel(leaf_map, home, away, *refs):
    wide_maps, maps = refs[-2:]
    k_half, size = home.shape[1:]
    core = lax.axis_index("blk") & 1
    maps[:, :size] = leaf_map[...]
    for i in range(home.shape[0]):
        columns = slice((i + 1) * size, (i + 2) * size)
        maps[span(core, k_half), columns] = home[i]
        maps[span(1 - core, k_half), columns] = away[i]
    wide_maps[...] = wide_right(maps[...])


def final_kernel(fronts, height, solved, wide_maps, *refs):
    nodes, refs = refs[: 2 * height], refs[2 * height :]
    roots, refs = refs[: 2 * fronts], refs[2 * fronts :]
    leaf_out, node_out, root_out, root_maps, incoming, result, sems = refs
    core, level = lax.axis_index("blk") & 1, lax.axis_index("level")
    half, size = solved.shape[1:]
    k_half = root_maps.shape[1] // 2
    for front in range(1, fronts):
        root_maps[front, span(core, k_half), :] = roots[2 * front][half:, :]
        root_maps[front, span(1 - core, k_half), :] = roots[2 * front + 1][half:, :]

    def both_rows(mask):
        return jnp.concatenate([roots[2 * mask][:half, :], roots[2 * mask + 1][:half, :]], axis=0)

    @pl.when(level == 0)
    def _():
        incoming[...] = jnp.zeros_like(incoming)

    for here in range(1, fronts):

        @pl.when(level == here)
        def _():
            value = both_rows(here)
            for front in range(1, here):
                value = both_rows(here ^ front) + product(value, root_maps[here ^ front])
            incoming[...] = value

    copies = []
    step = half // 2
    for chunk in range(4):
        part, first = chunk // 2, chunk % 2 * step
        inner = slice(first, first + step)
        rows = pl.ds(pl.multiple_of((core if part == 0 else 1 - core) * half + first, 8), step)
        change = wide_dot(wide_left(incoming[chunk * step : (chunk + 1) * step, :]), wide_maps[...])
        bases = (
            [solved[part, inner, :]]
            + [nodes[2 * tier + part][inner, :] for tier in range(height)]
            + [roots[part][inner, :]]
        )
        targets = (
            [leaf_out.at[rows]] + [node_out.at[tier, rows] for tier in range(height)] + [root_out.at[rows]]
        )
        for i, (base, target) in enumerate(zip(bases, targets)):
            result[chunk, i] = base + change[:, i * size : (i + 1) * size]
            copies.append(pltpu.make_async_copy(result.at[chunk, i], target, sems.at[chunk, i]))
            copies[-1].start()
    for copy in copies:
        copy.wait()


def shards(
    right_sides,
    leaf_gen,
    leaf_inverse,
    leaf_lower,
    node_gen,
    node_inverse,
    node_lower,
    coupling,
    child_leaf,
):
    rows, leaf_size = right_sides.shape[1:]
    size = leaf_lower.shape[2]
    k_rows = coupling.shape[1]
    height = node_gen.shape[2]
    fronts = lax.axis_size("level")
    leaves = lax.axis_size("blk")
    half = rows // 2
    part = half + k_rows // 2
    smem = pl.BlockSpec(memory_space=pltpu.SMEM)
    vmem = pl.BlockSpec(memory_space=pltpu.VMEM)
    hbm = pl.BlockSpec(memory_space=pltpu.HBM)
    anywhere = pl.BlockSpec(memory_space=pl.ANY)
    array = lambda *shape: jax.ShapeDtypeStruct(shape, f32)

    def blk_swap(value, mask):
        return lax.ppermute(value, "blk", [(i, i ^ mask) for i in range(leaves)])

    def level_swap(value, mask):
        return lax.ppermute(value, "level", [(i, i ^ mask) for i in range(fronts)])

    k_half = k_rows // 2
    node_params = (node_gen[0, 0], node_inverse[0, 0], node_lower[0, 0])
    away, leaf_solve, leaf_skeleton, right_here, coupling_here, *first_params = call(
        leaf_kernel,
        (
            array(part, size),
            array(leaf_size, size),
            jax.ShapeDtypeStruct((3 * leaf_size, size), bf16),
            array(2, half, leaf_size),
            array(k_rows, leaf_size),
            *(array(*value.shape[1:]) for value in node_params),
        ),
        tuple(
            pltpu.with_memory_space_constraint(value, pltpu.HBM)
            for value in (
                right_sides[0],
                leaf_gen[0],
                leaf_inverse[0],
                leaf_lower[0],
                coupling[0],
                *node_params,
            )
        ),
        6 * (part + leaf_size) * leaf_size * size,
        in_specs=[hbm] * 8,
        scratch_shapes=[
            pltpu.VMEM((leaf_size, leaf_size), f32),
            pltpu.VMEM((size, size), f32),
            pltpu.VMEM((size, size), f32),
            pltpu.SemaphoreType.DMA((9,)),
        ],
    )
    merge_flops = 6 * half * 2 * size * size
    fold_flops = 6 * 4 * size * size * size
    wide = lambda count: jax.ShapeDtypeStruct((count, 3 * size, 2 * size), bf16)
    both = pltpu.VMEM((2 * size, 2 * size), f32)
    first_mine, first_other, base, home = call(
        first_fold_kernel,
        (wide(1), wide(1), array(half, 2 * size), array(k_half, size)),
        (*first_params, right_here, coupling_here, leaf_skeleton),
        fold_flops + 6 * part * (leaf_size + 2 * size) * size,
        scratch_shapes=[both],
    )
    *node_params, away = lax.optimization_barrier((*node_params, away))
    away = blk_swap(away, 1)
    node, skeleton = call(
        first_merge_kernel,
        (array(half, size), array(half, size)),
        (base, away, first_other),
        merge_flops,
    )
    nodes, away_first = [node], away
    child_leaf, skeleton = lax.optimization_barrier((child_leaf, skeleton))
    for tier in range(1, height):
        away = blk_swap(skeleton, 1 << tier)
        after = ()
        if tier == 1:
            mine_maps, other_maps = call(
                fold_kernel,
                (wide(height - 1),) * 2,
                tuple(node_params),
                (height - 1) * fold_flops,
                scratch_shapes=[both],
            )
            tail, carried = call(
                carry_kernel,
                (array(k_half, size),) * 2,
                (child_leaf, home, away_first, first_mine, first_other),
                6 * k_half * 4 * size * size,
                in_specs=[smem] + [vmem] * 4,
            )
            tails = [tail]
        if tier < height - 2:
            both = call(
                functools.partial(pair_kernel, tier - 1),
                array(k_half, 2 * size),
                (carried, blk_swap(carried, 1 << tier), mine_maps, other_maps),
                6 * k_half * 4 * size * size,
            )
            tails.append(both[:, :size])
            carried = both[:, size:]
        if tier == height - 2:
            climb = call(
                functools.partial(climb_kernel, tier - 1),
                array(k_half, size),
                (carried, mine_maps),
                6 * k_half * size * size,
            )
            far = blk_swap(climb, 2 << tier)
            after = (climb,)
        if tier == height - 1:
            relay = call(relay_kernel, array(3, k_half, size), (carried, climb, far), k_half * size)
            relayed = blk_swap(relay, 1 << (tier - 1))
            tails = call(
                functools.partial(top_kernel, tier - 2),
                array(height + 1, k_half, size),
                (jnp.stack(tails), relay, relayed, mine_maps, other_maps),
                6 * k_half * 6 * size * size,
            )
            solved, leaf_map = call(
                leaf_solve_kernel,
                (array(2, half, size), array(k_rows, size)),
                (child_leaf, right_here, coupling_here, leaf_solve),
                6 * (rows + k_rows) * leaf_size * size,
                in_specs=[smem] + [vmem] * 3,
            )
            after = (solved,)
        base = call(
            functools.partial(base_kernel, tier - 1),
            array(half, 2 * size),
            (skeleton, mine_maps),
            merge_flops,
        )
        last = tier == height - 1
        node, skeleton = call(
            functools.partial(last_merge_kernel if last else merge_kernel, tier - 1),
            (array(half, size), array(part if last else half, size)),
            (base, away, other_maps) + ((tails,) if last else ()) + after,
            merge_flops,
            in_specs=[vmem] * (4 if last else 3) + [anywhere] * len(after),
        )
        nodes.append(node)
    received = [level_swap(skeleton, mask) for mask in range(1, fronts)]
    roots = [skeleton, blk_swap(skeleton, 1)]
    for value in received:
        roots += [value, blk_swap(value, 1)]
    pairs = []
    for value in nodes:
        pairs += [value, blk_swap(value, 1)]
    after = (*pairs[1::2], roots[1])
    wide_maps = call(
        maps_kernel,
        jax.ShapeDtypeStruct((3 * k_rows, size * (height + 2)), bf16),
        (leaf_map, tails, blk_swap(tails, 1), *after),
        k_rows * size * (height + 2) * 4,
        in_specs=[vmem] * 3 + [anywhere] * len(after),
        scratch_shapes=[pltpu.VMEM((k_rows, size * (height + 2)), f32)],
    )
    leaf_out, node_out, root_out = call(
        functools.partial(final_kernel, fronts, height),
        (array(rows, size), array(height, rows, size), array(rows, size)),
        (solved, wide_maps, *pairs, *roots),
        6 * rows * size * size * (height + 2),
        out_specs=(hbm,) * 3,
        scratch_shapes=[
            pltpu.VMEM((fronts, k_rows, size), f32),
            pltpu.VMEM((rows, size), f32),
            pltpu.VMEM((4, height + 2, rows // 4, size), f32),
            pltpu.SemaphoreType.DMA((4, height + 2)),
        ],
    )
    return (leaf_out[None], node_out[None, None], root_out[None])


def solution(mesh):
    in_specs = (
        P("level", None, "blk"),
        P("level", "blk", None),
        P("level", "blk", None),
        P("level", "blk", None),
        P("level", "blk", None, None, None),
        P("level", "blk", None, None, None),
        P("level", "blk", None, None, None),
        P("level", None, None),
        P("level"),
    )
    out_specs = (
        P("level", None, "blk"),
        P("level", "blk", None, None, None),
        P("level", None, None),
    )

    return jax.shard_map(shards, mesh=mesh, in_specs=in_specs, out_specs=out_specs, check_vma=False)
```

```python
import functools

import jax
import jax.numpy as jnp
from jax import lax
from jax.experimental import pallas as pl
from jax.experimental.pallas import tpu as pltpu
from jax.sharding import PartitionSpec as P


f32 = jnp.float32
bf16 = jnp.bfloat16
VMEM_LIMIT = 12 << 20


def split(value):
    high = value.astype(bf16)
    return high, (value - high.astype(f32)).astype(bf16)


def wide_left(value):
    high, low = split(value)
    return jnp.concatenate([high, low, high], axis=1)


def wide_right(value):
    high, low = split(value)
    return jnp.concatenate([high, high, low], axis=0)


def wide_dot(left, right):
    return jnp.dot(left, right, preferred_element_type=f32)


def product(left, right):
    return wide_dot(wide_left(left), wide_right(right))


def call(kernel, out_shape, args, flops, in_specs=None, out_specs=None, scratch_shapes=()):
    size = lambda s: s.size * s.dtype.itemsize
    vmem = pl.BlockSpec(memory_space=pltpu.VMEM)
    moved = sum(size(a) for a in args) + sum(size(o) for o in jax.tree.leaves(out_shape))
    return pl.pallas_call(
        kernel,
        out_shape=out_shape,
        in_specs=in_specs or [vmem] * len(args),
        out_specs=out_specs or jax.tree.map(lambda _: vmem, out_shape),
        scratch_shapes=scratch_shapes,
        compiler_params=pltpu.CompilerParams(vmem_limit_bytes=VMEM_LIMIT),
        cost_estimate=pl.CostEstimate(flops=flops, bytes_accessed=moved, transcendentals=0),
    )(*args)


def span(index, length):
    return pl.ds(pl.multiple_of(index * length, 8), length)


def leaf_kernel(right, generator, inverse, lower, coupling, *refs):
    later, (away, solve_map, skeleton_map), refs = refs[:3], refs[3:6], refs[6:]
    (right_here, coupling_here, *later_here), refs = refs[:5], refs[5:]
    generator_here, inverse_here, lower_here, sems = refs
    core = lax.axis_index("blk") & 1
    half, k_half = right.shape[0] // 2, coupling.shape[0] // 2
    size = inverse.shape[0]
    copies = [
        pltpu.make_async_copy(source, target, sems.at[i])
        for i, (source, target) in enumerate(
            [
                (generator, generator_here),
                (inverse, inverse_here),
                (lower, lower_here),
                (right.at[span(1 - core, half)], right_here.at[0]),
                (coupling, coupling_here),
                (right.at[span(core, half)], right_here.at[1]),
                *((source.at[0], target) for source, target in zip(later, later_here)),
            ]
        )
    ]
    for copy in copies:
        copy.start()
    for copy in copies[:2]:
        copy.wait()
    solved = product(generator_here[:, :size], inverse_here[...])
    solve_map[...] = solved
    copies[2].wait()
    parts = wide_right(generator_here[:, size:] - product(solved, lower_here[...]))
    skeleton_map[...] = parts
    copies[3].wait()
    away[:half, :] = wide_dot(wide_left(right_here[0]), parts)
    copies[4].wait()
    away[half:, :] = wide_dot(wide_left(coupling_here[span(1 - core, k_half), :]), parts)
    for copy in copies[5:]:
        copy.wait()


def leaf_solve_kernel(child, right, coupling, solve_map, solved, leaf_map):
    parts = wide_right(solve_map[...])
    for part in range(2):
        solved[part] = wide_dot(wide_left(right[1 - part]), parts)
    on_target = lax.axis_index("blk") == child[0]
    leaf_map[...] = jnp.where(on_target, wide_dot(wide_left(coupling[...]), parts), 0.0)


def fold(tier, generator, inverse, lower, both):
    size = inverse.shape[0]
    solve_map = product(generator[:, :size], inverse)
    both[:, :size] = solve_map
    both[:, size:] = generator[:, size:] - product(solve_map, lower)
    upper = (lax.axis_index("blk") >> tier) & 1
    return wide_right(both[span(upper, size), :]), wide_right(both[span(1 - upper, size), :])


def first_fold_kernel(
    generator, inverse, lower, right, coupling, skeleton_map, mine_maps, other_maps, base, home, both
):
    core = lax.axis_index("blk") & 1
    k_half = home.shape[0]
    value = wide_dot(wide_left(right[1]), skeleton_map[...])
    home[...] = wide_dot(wide_left(coupling[span(core, k_half), :]), skeleton_map[...])
    mine_maps[0], other_maps[0] = fold(0, generator[...], inverse[...], lower[...], both)
    base[...] = wide_dot(wide_left(value), mine_maps[0])


def fold_kernel(generator, inverse, lower, mine_maps, other_maps, both):
    for tier in range(1, generator.shape[0]):
        mine_maps[tier - 1], other_maps[tier - 1] = fold(
            tier, generator[tier], inverse[tier], lower[tier], both
        )


def base_kernel(index, home, mine_maps, base):
    base[...] = wide_dot(wide_left(home[...]), mine_maps[index])


def merge_kernel(index, base, away, other_maps, *refs):
    node, skeleton = refs[-2:]
    size = away.shape[1]
    both = base[...] + wide_dot(wide_left(away[...]), other_maps[index])
    skeleton[...] = both[:, size:]
    node[...] = both[:, :size]


def first_merge_kernel(base, away, other_maps, node, skeleton):
    half, size = node.shape
    both = base[...] + wide_dot(wide_left(away[:half, :]), other_maps[0])
    skeleton[...] = both[:, size:]
    node[...] = both[:, :size]


def carry_kernel(child, home, away, mine_maps, other_maps, tail, carried):
    k_half, size = home.shape
    position = lax.axis_index("blk")
    mine = wide_dot(wide_left(home[...]), mine_maps[0])
    other = wide_dot(wide_left(away[away.shape[0] - k_half :, :]), other_maps[0])
    both = jnp.where(position == child[0], mine, 0.0) + jnp.where(position ^ 1 == child[0], other, 0.0)
    tail[...] = both[:, :size]
    carried[...] = both[:, size:]


def climb_kernel(index, carried, mine_maps, climb):
    size = carried.shape[1]
    climb[...] = wide_dot(wide_left(carried[...]), mine_maps[index, :, size:])


def relay_kernel(carried, far, out):
    out[0] = carried[...]
    out[1] = far[...]


def pair_kernel(index, home, away, mine_maps, other_maps, out):
    out[...] = wide_dot(wide_left(home[...]), mine_maps[index]) + wide_dot(
        wide_left(away[...]), other_maps[index]
    )


def top_kernel(index, tails, home, away, mine_maps, other_maps, out):
    size = tails.shape[2]
    count = tails.shape[0]
    out[:count] = tails[...]
    both = wide_dot(wide_left(home[0]), mine_maps[index]) + wide_dot(
        wide_left(away[0]), other_maps[index]
    )
    out[count] = both[:, :size]
    both = wide_dot(wide_left(both[:, size:]), mine_maps[index + 1]) + wide_dot(
        wide_left(home[1] + away[1]), other_maps[index + 1]
    )
    out[count + 1] = both[:, :size]
    out[count + 2] = both[:, size:]


def last_merge_kernel(index, base, away, other_maps, tails, *refs):
    node, root = refs[-2:]
    half, size = away.shape
    both = base[...] + wide_dot(wide_left(away[...]), other_maps[index])
    root[:half, :] = both[:, size:]
    root[half:, :] = tails[tails.shape[0] - 1]
    node[...] = both[:, :size]


def maps_kernel(leaf_map, home, away, *refs):
    wide_maps, maps = refs[-2:]
    k_half, size = home.shape[1:]
    core = lax.axis_index("blk") & 1
    maps[:, :size] = leaf_map[...]
    for i in range(home.shape[0]):
        columns = slice((i + 1) * size, (i + 2) * size)
        maps[span(core, k_half), columns] = home[i]
        maps[span(1 - core, k_half), columns] = away[i]
    wide_maps[...] = wide_right(maps[...])


def final_kernel(fronts, height, solved, wide_maps, *refs):
    nodes, refs = refs[: 2 * height], refs[2 * height :]
    roots, refs = refs[: 2 * fronts], refs[2 * fronts :]
    leaf_out, node_out, root_out, root_maps, incoming, result, sems = refs
    core, level = lax.axis_index("blk") & 1, lax.axis_index("level")
    half, size = solved.shape[1:]
    k_half = root_maps.shape[1] // 2
    for front in range(1, fronts):
        root_maps[front, span(core, k_half), :] = roots[2 * front][half:, :]
        root_maps[front, span(1 - core, k_half), :] = roots[2 * front + 1][half:, :]

    def both_rows(mask):
        return jnp.concatenate([roots[2 * mask][:half, :], roots[2 * mask + 1][:half, :]], axis=0)

    @pl.when(level == 0)
    def _():
        incoming[...] = jnp.zeros_like(incoming)

    for here in range(1, fronts):

        @pl.when(level == here)
        def _():
            value = both_rows(here)
            for front in range(1, here):
                value = both_rows(here ^ front) + product(value, root_maps[here ^ front])
            incoming[...] = value

    copies = []
    step = half // 2
    for chunk in range(4):
        part, first = chunk // 2, chunk % 2 * step
        inner = slice(first, first + step)
        rows = pl.ds(pl.multiple_of((core if part == 0 else 1 - core) * half + first, 8), step)
        change = wide_dot(wide_left(incoming[chunk * step : (chunk + 1) * step, :]), wide_maps[...])
        bases = (
            [solved[part, inner, :]]
            + [nodes[2 * tier + part][inner, :] for tier in range(height)]
            + [roots[part][inner, :]]
        )
        targets = (
            [leaf_out.at[rows]] + [node_out.at[tier, rows] for tier in range(height)] + [root_out.at[rows]]
        )
        for i, (base, target) in enumerate(zip(bases, targets)):
            result[chunk, i] = base + change[:, i * size : (i + 1) * size]
            copies.append(pltpu.make_async_copy(result.at[chunk, i], target, sems.at[chunk, i]))
            copies[-1].start()
    for copy in copies:
        copy.wait()


def shards(
    right_sides,
    leaf_gen,
    leaf_inverse,
    leaf_lower,
    node_gen,
    node_inverse,
    node_lower,
    coupling,
    child_leaf,
):
    rows, leaf_size = right_sides.shape[1:]
    size = leaf_lower.shape[2]
    k_rows = coupling.shape[1]
    height = node_gen.shape[2]
    fronts = lax.axis_size("level")
    leaves = lax.axis_size("blk")
    half = rows // 2
    part = half + k_rows // 2
    smem = pl.BlockSpec(memory_space=pltpu.SMEM)
    vmem = pl.BlockSpec(memory_space=pltpu.VMEM)
    hbm = pl.BlockSpec(memory_space=pltpu.HBM)
    anywhere = pl.BlockSpec(memory_space=pl.ANY)
    array = lambda *shape: jax.ShapeDtypeStruct(shape, f32)

    def blk_swap(value, mask):
        return lax.ppermute(value, "blk", [(i, i ^ mask) for i in range(leaves)])

    def level_swap(value, mask):
        return lax.ppermute(value, "level", [(i, i ^ mask) for i in range(fronts)])

    k_half = k_rows // 2
    node_params = (node_gen[0, 0], node_inverse[0, 0], node_lower[0, 0])
    away, leaf_solve, leaf_skeleton, right_here, coupling_here, *first_params = call(
        leaf_kernel,
        (
            array(part, size),
            array(leaf_size, size),
            jax.ShapeDtypeStruct((3 * leaf_size, size), bf16),
            array(2, half, leaf_size),
            array(k_rows, leaf_size),
            *(array(*value.shape[1:]) for value in node_params),
        ),
        tuple(
            pltpu.with_memory_space_constraint(value, pltpu.HBM)
            for value in (
                right_sides[0],
                leaf_gen[0],
                leaf_inverse[0],
                leaf_lower[0],
                coupling[0],
                *node_params,
            )
        ),
        6 * (part + leaf_size) * leaf_size * size,
        in_specs=[hbm] * 8,
        scratch_shapes=[
            pltpu.VMEM((leaf_size, leaf_size), f32),
            pltpu.VMEM((size, size), f32),
            pltpu.VMEM((size, size), f32),
            pltpu.SemaphoreType.DMA((9,)),
        ],
    )
    merge_flops = 6 * half * 2 * size * size
    fold_flops = 6 * 4 * size * size * size
    wide = lambda count: jax.ShapeDtypeStruct((count, 3 * size, 2 * size), bf16)
    both = pltpu.VMEM((2 * size, 2 * size), f32)
    first_mine, first_other, base, home = call(
        first_fold_kernel,
        (wide(1), wide(1), array(half, 2 * size), array(k_half, size)),
        (*first_params, right_here, coupling_here, leaf_skeleton),
        fold_flops + 6 * part * (leaf_size + 2 * size) * size,
        scratch_shapes=[both],
    )
    *node_params, away = lax.optimization_barrier((*node_params, away))
    away = blk_swap(away, 1)
    node, skeleton = call(
        first_merge_kernel,
        (array(half, size), array(half, size)),
        (base, away, first_other),
        merge_flops,
    )
    nodes, away_first = [node], away
    child_leaf, skeleton = lax.optimization_barrier((child_leaf, skeleton))
    for tier in range(1, height):
        away = blk_swap(skeleton, 1 << tier)
        after = ()
        if tier == 1:
            mine_maps, other_maps = call(
                fold_kernel,
                (wide(height - 1),) * 2,
                tuple(node_params),
                (height - 1) * fold_flops,
                scratch_shapes=[both],
            )
            tail, carried = call(
                carry_kernel,
                (array(k_half, size),) * 2,
                (child_leaf, home, away_first, first_mine, first_other),
                6 * k_half * 4 * size * size,
                in_specs=[smem] + [vmem] * 4,
            )
            tails = [tail]
        if tier < height - 2:
            both = call(
                functools.partial(pair_kernel, tier - 1),
                array(k_half, 2 * size),
                (carried, blk_swap(carried, 1 << tier), mine_maps, other_maps),
                6 * k_half * 4 * size * size,
            )
            tails.append(both[:, :size])
            carried = both[:, size:]
        if tier == height - 2:
            climb = call(
                functools.partial(climb_kernel, tier - 1),
                array(k_half, size),
                (carried, mine_maps),
                6 * k_half * size * size,
            )
            far = blk_swap(climb, 2 << tier)
            after = (climb,)
        if tier == height - 1:
            relay = call(relay_kernel, array(2, k_half, size), (carried, far), k_half * size)
            relayed = blk_swap(relay, 1 << (tier - 1))
            tails = call(
                functools.partial(top_kernel, tier - 2),
                array(height + 1, k_half, size),
                (jnp.stack(tails), relay, relayed, mine_maps, other_maps),
                6 * k_half * 6 * size * size,
            )
            solved, leaf_map = call(
                leaf_solve_kernel,
                (array(2, half, size), array(k_rows, size)),
                (child_leaf, right_here, coupling_here, leaf_solve),
                6 * (rows + k_rows) * leaf_size * size,
                in_specs=[smem] + [vmem] * 3,
            )
            after = (solved,)
        base = call(
            functools.partial(base_kernel, tier - 1),
            array(half, 2 * size),
            (skeleton, mine_maps),
            merge_flops,
        )
        last = tier == height - 1
        node, skeleton = call(
            functools.partial(last_merge_kernel if last else merge_kernel, tier - 1),
            (array(half, size), array(part if last else half, size)),
            (base, away, other_maps) + ((tails,) if last else ()) + after,
            merge_flops,
            in_specs=[vmem] * (4 if last else 3) + [anywhere] * len(after),
        )
        nodes.append(node)
    received = [level_swap(skeleton, mask) for mask in range(1, fronts)]
    roots = [skeleton, blk_swap(skeleton, 1)]
    for value in received:
        roots += [value, blk_swap(value, 1)]
    pairs = []
    for value in nodes:
        pairs += [value, blk_swap(value, 1)]
    after = (*pairs[1::2], roots[1])
    wide_maps = call(
        maps_kernel,
        jax.ShapeDtypeStruct((3 * k_rows, size * (height + 2)), bf16),
        (leaf_map, tails, blk_swap(tails, 1), *after),
        k_rows * size * (height + 2) * 4,
        in_specs=[vmem] * 3 + [anywhere] * len(after),
        scratch_shapes=[pltpu.VMEM((k_rows, size * (height + 2)), f32)],
    )
    leaf_out, node_out, root_out = call(
        functools.partial(final_kernel, fronts, height),
        (array(rows, size), array(height, rows, size), array(rows, size)),
        (solved, wide_maps, *pairs, *roots),
        6 * rows * size * size * (height + 2),
        out_specs=(hbm,) * 3,
        scratch_shapes=[
            pltpu.VMEM((fronts, k_rows, size), f32),
            pltpu.VMEM((rows, size), f32),
            pltpu.VMEM((4, height + 2, rows // 4, size), f32),
            pltpu.SemaphoreType.DMA((4, height + 2)),
        ],
    )
    return (leaf_out[None], node_out[None, None], root_out[None])


def solution(mesh):
    in_specs = (
        P("level", None, "blk"),
        P("level", "blk", None),
        P("level", "blk", None),
        P("level", "blk", None),
        P("level", "blk", None, None, None),
        P("level", "blk", None, None, None),
        P("level", "blk", None, None, None),
        P("level", None, None),
        P("level"),
    )
    out_specs = (
        P("level", None, "blk"),
        P("level", "blk", None, None, None),
        P("level", None, None),
    )

    return jax.shard_map(shards, mesh=mesh, in_specs=in_specs, out_specs=out_specs, check_vma=False)
```

```python
import functools

import jax
import jax.numpy as jnp
from jax import lax
from jax.experimental import pallas as pl
from jax.experimental.pallas import tpu as pltpu
from jax.sharding import PartitionSpec as P


f32 = jnp.float32
bf16 = jnp.bfloat16
VMEM_LIMIT = 12 << 20


def split(value):
    high = value.astype(bf16)
    return high, (value - high.astype(f32)).astype(bf16)


def wide_left(value):
    high, low = split(value)
    return jnp.concatenate([high, low, high], axis=1)


def wide_right(value):
    high, low = split(value)
    return jnp.concatenate([high, high, low], axis=0)


def wide_dot(left, right):
    return jnp.dot(left, right, preferred_element_type=f32)


def product(left, right):
    return wide_dot(wide_left(left), wide_right(right))


def call(kernel, out_shape, args, flops, in_specs=None, out_specs=None, scratch_shapes=()):
    size = lambda s: s.size * s.dtype.itemsize
    vmem = pl.BlockSpec(memory_space=pltpu.VMEM)
    moved = sum(size(a) for a in args) + sum(size(o) for o in jax.tree.leaves(out_shape))
    return pl.pallas_call(
        kernel,
        out_shape=out_shape,
        in_specs=in_specs or [vmem] * len(args),
        out_specs=out_specs or jax.tree.map(lambda _: vmem, out_shape),
        scratch_shapes=scratch_shapes,
        compiler_params=pltpu.CompilerParams(vmem_limit_bytes=VMEM_LIMIT),
        cost_estimate=pl.CostEstimate(flops=flops, bytes_accessed=moved, transcendentals=0),
    )(*args)


def span(index, length):
    return pl.ds(pl.multiple_of(index * length, 8), length)


def leaf_kernel(right, generator, inverse, lower, coupling, *refs):
    later, (away, solve_map, skeleton_map), refs = refs[:3], refs[3:6], refs[6:]
    (right_here, coupling_here, *later_here), refs = refs[:5], refs[5:]
    generator_here, inverse_here, lower_here, sems = refs
    core = lax.axis_index("blk") & 1
    half, k_half = right.shape[0] // 2, coupling.shape[0] // 2
    size = inverse.shape[0]
    copies = [
        pltpu.make_async_copy(source, target, sems.at[i])
        for i, (source, target) in enumerate(
            [
                (generator, generator_here),
                (inverse, inverse_here),
                (lower, lower_here),
                (right.at[span(1 - core, half)], right_here.at[0]),
                (coupling, coupling_here),
                (right.at[span(core, half)], right_here.at[1]),
                *((source.at[0], target) for source, target in zip(later, later_here)),
            ]
        )
    ]
    for copy in copies:
        copy.start()
    for copy in copies[:2]:
        copy.wait()
    solved = product(generator_here[:, :size], inverse_here[...])
    solve_map[...] = solved
    copies[2].wait()
    parts = wide_right(generator_here[:, size:] - product(solved, lower_here[...]))
    skeleton_map[...] = parts
    copies[3].wait()
    away[:half, :] = wide_dot(wide_left(right_here[0]), parts)
    copies[4].wait()
    away[half:, :] = wide_dot(wide_left(coupling_here[span(1 - core, k_half), :]), parts)
    for copy in copies[5:]:
        copy.wait()


def leaf_solve_kernel(child, right, coupling, solve_map, solved, leaf_map):
    parts = wide_right(solve_map[...])
    for part in range(2):
        solved[part] = wide_dot(wide_left(right[1 - part]), parts)
    on_target = lax.axis_index("blk") == child[0]
    leaf_map[...] = jnp.where(on_target, wide_dot(wide_left(coupling[...]), parts), 0.0)


def fold(tier, generator, inverse, lower, both):
    size = inverse.shape[0]
    solve_map = product(generator[:, :size], inverse)
    both[:, :size] = solve_map
    both[:, size:] = generator[:, size:] - product(solve_map, lower)
    upper = (lax.axis_index("blk") >> tier) & 1
    return wide_right(both[span(upper, size), :]), wide_right(both[span(1 - upper, size), :])


def first_fold_kernel(
    generator, inverse, lower, right, coupling, skeleton_map, mine_maps, other_maps, base, home, both
):
    core = lax.axis_index("blk") & 1
    k_half = home.shape[0]
    value = wide_dot(wide_left(right[1]), skeleton_map[...])
    home[...] = wide_dot(wide_left(coupling[span(core, k_half), :]), skeleton_map[...])
    mine_maps[0], other_maps[0] = fold(0, generator[...], inverse[...], lower[...], both)
    base[...] = wide_dot(wide_left(value), mine_maps[0])


def fold_kernel(first, generator, inverse, lower, *refs):
    mine_maps, other_maps, both = refs[-3:]
    for i in range(mine_maps.shape[0]):
        tier = first + i
        mine_maps[i], other_maps[i] = fold(tier, generator[tier], inverse[tier], lower[tier], both)


def base_kernel(index, home, mine_maps, base):
    base[...] = wide_dot(wide_left(home[...]), mine_maps[index])


def merge_kernel(index, base, away, other_maps, *refs):
    node, skeleton = refs[-2:]
    size = away.shape[1]
    both = base[...] + wide_dot(wide_left(away[...]), other_maps[index])
    skeleton[...] = both[:, size:]
    node[...] = both[:, :size]


def first_merge_kernel(base, away, other_maps, node, skeleton):
    half, size = node.shape
    both = base[...] + wide_dot(wide_left(away[:half, :]), other_maps[0])
    skeleton[...] = both[:, size:]
    node[...] = both[:, :size]


def carry_kernel(child, home, away, mine_maps, other_maps, next_maps, tail, carried, *climb):
    k_half, size = home.shape
    position = lax.axis_index("blk")
    mine = wide_dot(wide_left(home[...]), mine_maps[0])
    other = wide_dot(wide_left(away[away.shape[0] - k_half :, :]), other_maps[0])
    both = jnp.where(position == child[0], mine, 0.0) + jnp.where(position ^ 1 == child[0], other, 0.0)
    tail[...] = both[:, :size]
    carried[...] = both[:, size:]
    for out in climb:
        out[...] = wide_dot(wide_left(both[:, size:]), next_maps[0, :, size:])


def climb_kernel(index, carried, mine_maps, climb):
    size = carried.shape[1]
    climb[...] = wide_dot(wide_left(carried[...]), mine_maps[index, :, size:])


def relay_kernel(carried, far, out):
    out[0] = carried[...]
    out[1] = far[...]


def pair_kernel(index, home, away, mine_maps, other_maps, out):
    out[...] = wide_dot(wide_left(home[...]), mine_maps[index]) + wide_dot(
        wide_left(away[...]), other_maps[index]
    )


def top_kernel(index, tails, home, away, mine_maps, other_maps, top_mine, top_other, out):
    size = tails.shape[2]
    count = tails.shape[0]
    out[:count] = tails[...]
    both = wide_dot(wide_left(home[0]), mine_maps[index]) + wide_dot(
        wide_left(away[0]), other_maps[index]
    )
    out[count] = both[:, :size]
    both = wide_dot(wide_left(both[:, size:]), top_mine[0]) + wide_dot(
        wide_left(home[1] + away[1]), top_other[0]
    )
    out[count + 1] = both[:, :size]
    out[count + 2] = both[:, size:]


def last_merge_kernel(index, base, away, other_maps, tails, *refs):
    node, root = refs[-2:]
    half, size = away.shape
    both = base[...] + wide_dot(wide_left(away[...]), other_maps[index])
    root[:half, :] = both[:, size:]
    root[half:, :] = tails[tails.shape[0] - 1]
    node[...] = both[:, :size]


def maps_kernel(leaf_map, home, away, *refs):
    wide_maps, maps = refs[-2:]
    k_half, size = home.shape[1:]
    core = lax.axis_index("blk") & 1
    maps[:, :size] = leaf_map[...]
    for i in range(home.shape[0]):
        columns = slice((i + 1) * size, (i + 2) * size)
        maps[span(core, k_half), columns] = home[i]
        maps[span(1 - core, k_half), columns] = away[i]
    wide_maps[...] = wide_right(maps[...])


def final_kernel(fronts, height, solved, wide_maps, *refs):
    nodes, refs = refs[: 2 * height], refs[2 * height :]
    roots, refs = refs[: 2 * fronts], refs[2 * fronts :]
    leaf_out, node_out, root_out, root_maps, incoming, result, sems = refs
    core, level = lax.axis_index("blk") & 1, lax.axis_index("level")
    half, size = solved.shape[1:]
    k_half = root_maps.shape[1] // 2
    for front in range(1, fronts):
        root_maps[front, span(core, k_half), :] = roots[2 * front][half:, :]
        root_maps[front, span(1 - core, k_half), :] = roots[2 * front + 1][half:, :]

    def both_rows(mask):
        return jnp.concatenate([roots[2 * mask][:half, :], roots[2 * mask + 1][:half, :]], axis=0)

    @pl.when(level == 0)
    def _():
        incoming[...] = jnp.zeros_like(incoming)

    for here in range(1, fronts):

        @pl.when(level == here)
        def _():
            value = both_rows(here)
            for front in range(1, here):
                value = both_rows(here ^ front) + product(value, root_maps[here ^ front])
            incoming[...] = value

    copies = []
    step = half // 2
    for chunk in range(4):
        part, first = chunk // 2, chunk % 2 * step
        inner = slice(first, first + step)
        rows = pl.ds(pl.multiple_of((core if part == 0 else 1 - core) * half + first, 8), step)
        change = wide_dot(wide_left(incoming[chunk * step : (chunk + 1) * step, :]), wide_maps[...])
        bases = (
            [solved[part, inner, :]]
            + [nodes[2 * tier + part][inner, :] for tier in range(height)]
            + [roots[part][inner, :]]
        )
        targets = (
            [leaf_out.at[rows]] + [node_out.at[tier, rows] for tier in range(height)] + [root_out.at[rows]]
        )
        for i, (base, target) in enumerate(zip(bases, targets)):
            result[chunk, i] = base + change[:, i * size : (i + 1) * size]
            copies.append(pltpu.make_async_copy(result.at[chunk, i], target, sems.at[chunk, i]))
            copies[-1].start()
    for copy in copies:
        copy.wait()


def shards(
    right_sides,
    leaf_gen,
    leaf_inverse,
    leaf_lower,
    node_gen,
    node_inverse,
    node_lower,
    coupling,
    child_leaf,
):
    rows, leaf_size = right_sides.shape[1:]
    size = leaf_lower.shape[2]
    k_rows = coupling.shape[1]
    height = node_gen.shape[2]
    fronts = lax.axis_size("level")
    leaves = lax.axis_size("blk")
    half = rows // 2
    part = half + k_rows // 2
    smem = pl.BlockSpec(memory_space=pltpu.SMEM)
    vmem = pl.BlockSpec(memory_space=pltpu.VMEM)
    hbm = pl.BlockSpec(memory_space=pltpu.HBM)
    anywhere = pl.BlockSpec(memory_space=pl.ANY)
    array = lambda *shape: jax.ShapeDtypeStruct(shape, f32)

    def blk_swap(value, mask):
        return lax.ppermute(value, "blk", [(i, i ^ mask) for i in range(leaves)])

    def level_swap(value, mask):
        return lax.ppermute(value, "level", [(i, i ^ mask) for i in range(fronts)])

    k_half = k_rows // 2
    node_params = (node_gen[0, 0], node_inverse[0, 0], node_lower[0, 0])
    away, leaf_solve, leaf_skeleton, right_here, coupling_here, *first_params = call(
        leaf_kernel,
        (
            array(part, size),
            array(leaf_size, size),
            jax.ShapeDtypeStruct((3 * leaf_size, size), bf16),
            array(2, half, leaf_size),
            array(k_rows, leaf_size),
            *(array(*value.shape[1:]) for value in node_params),
        ),
        tuple(
            pltpu.with_memory_space_constraint(value, pltpu.HBM)
            for value in (
                right_sides[0],
                leaf_gen[0],
                leaf_inverse[0],
                leaf_lower[0],
                coupling[0],
                *node_params,
            )
        ),
        6 * (part + leaf_size) * leaf_size * size,
        in_specs=[hbm] * 8,
        scratch_shapes=[
            pltpu.VMEM((leaf_size, leaf_size), f32),
            pltpu.VMEM((size, size), f32),
            pltpu.VMEM((size, size), f32),
            pltpu.SemaphoreType.DMA((9,)),
        ],
    )
    merge_flops = 6 * half * 2 * size * size
    fold_flops = 6 * 4 * size * size * size
    wide = lambda count: jax.ShapeDtypeStruct((count, 3 * size, 2 * size), bf16)
    both = pltpu.VMEM((2 * size, 2 * size), f32)
    first_mine, first_other, base, home = call(
        first_fold_kernel,
        (wide(1), wide(1), array(half, 2 * size), array(k_half, size)),
        (*first_params, right_here, coupling_here, leaf_skeleton),
        fold_flops + 6 * part * (leaf_size + 2 * size) * size,
        scratch_shapes=[both],
    )
    *node_params, away = lax.optimization_barrier((*node_params, away))
    away = blk_swap(away, 1)
    node, skeleton = call(
        first_merge_kernel,
        (array(half, size), array(half, size)),
        (base, away, first_other),
        merge_flops,
    )
    nodes, away_first = [node], away

    def folds(first, last, *after):
        return call(
            functools.partial(fold_kernel, first),
            (wide(last - first),) * 2,
            (*node_params, *after),
            (last - first) * fold_flops,
            in_specs=[vmem] * 3 + [anywhere] * len(after),
            scratch_shapes=[both],
        )

    child_leaf, skeleton = lax.optimization_barrier((child_leaf, skeleton))
    for tier in range(1, height):
        away = blk_swap(skeleton, 1 << tier)
        after = ()
        if tier == 1:
            mine_maps, other_maps = folds(1, height - 1)
            tail, carried, *climb = call(
                carry_kernel,
                (array(k_half, size),) * (3 if height == 3 else 2),
                (child_leaf, home, away_first, first_mine, first_other, mine_maps),
                6 * k_half * 5 * size * size,
                in_specs=[smem] + [vmem] * 5,
            )
            tails = [tail]
        if tier < height - 2:
            pair = call(
                functools.partial(pair_kernel, tier - 1),
                array(k_half, 2 * size),
                (carried, blk_swap(carried, 1 << tier), mine_maps, other_maps),
                6 * k_half * 4 * size * size,
            )
            tails.append(pair[:, :size])
            carried = pair[:, size:]
        if tier == height - 2:
            if not climb:
                climb = [
                    call(
                        functools.partial(climb_kernel, tier - 1),
                        array(k_half, size),
                        (carried, mine_maps),
                        6 * k_half * size * size,
                    )
                ]
            far = blk_swap(climb[0], 2 << tier)
            after = (climb[0],)
        if tier == height - 1:
            top_mine, top_other = folds(height - 1, height)
            relay = call(relay_kernel, array(2, k_half, size), (carried, far), k_half * size)
            relayed = blk_swap(relay, 1 << (tier - 1))
            tails = call(
                functools.partial(top_kernel, tier - 2),
                array(height + 1, k_half, size),
                (jnp.stack(tails), relay, relayed, mine_maps, other_maps, top_mine, top_other),
                6 * k_half * 6 * size * size,
            )
            solved, leaf_map = call(
                leaf_solve_kernel,
                (array(2, half, size), array(k_rows, size)),
                (child_leaf, right_here, coupling_here, leaf_solve),
                6 * (rows + k_rows) * leaf_size * size,
                in_specs=[smem] + [vmem] * 3,
            )
            after = (solved,)
        last = tier == height - 1
        if last:
            mine_maps, other_maps = top_mine, top_other
        index = 0 if last else tier - 1
        base = call(
            functools.partial(base_kernel, index),
            array(half, 2 * size),
            (skeleton, mine_maps),
            merge_flops,
        )
        node, skeleton = call(
            functools.partial(last_merge_kernel if last else merge_kernel, index),
            (array(half, size), array(part if last else half, size)),
            (base, away, other_maps) + ((tails,) if last else ()) + after,
            merge_flops,
            in_specs=[vmem] * (4 if last else 3) + [anywhere] * len(after),
        )
        nodes.append(node)
    received = [level_swap(skeleton, mask) for mask in range(1, fronts)]
    roots = [skeleton, blk_swap(skeleton, 1)]
    for value in received:
        roots += [value, blk_swap(value, 1)]
    pairs = []
    for value in nodes:
        pairs += [value, blk_swap(value, 1)]
    after = (*pairs[1::2], roots[1])
    wide_maps = call(
        maps_kernel,
        jax.ShapeDtypeStruct((3 * k_rows, size * (height + 2)), bf16),
        (leaf_map, tails, blk_swap(tails, 1), *after),
        k_rows * size * (height + 2) * 4,
        in_specs=[vmem] * 3 + [anywhere] * len(after),
        scratch_shapes=[pltpu.VMEM((k_rows, size * (height + 2)), f32)],
    )
    leaf_out, node_out, root_out = call(
        functools.partial(final_kernel, fronts, height),
        (array(rows, size), array(height, rows, size), array(rows, size)),
        (solved, wide_maps, *pairs, *roots),
        6 * rows * size * size * (height + 2),
        out_specs=(hbm,) * 3,
        scratch_shapes=[
            pltpu.VMEM((fronts, k_rows, size), f32),
            pltpu.VMEM((rows, size), f32),
            pltpu.VMEM((4, height + 2, rows // 4, size), f32),
            pltpu.SemaphoreType.DMA((4, height + 2)),
        ],
    )
    return (leaf_out[None], node_out[None, None], root_out[None])


def solution(mesh):
    in_specs = (
        P("level", None, "blk"),
        P("level", "blk", None),
        P("level", "blk", None),
        P("level", "blk", None),
        P("level", "blk", None, None, None),
        P("level", "blk", None, None, None),
        P("level", "blk", None, None, None),
        P("level", None, None),
        P("level"),
    )
    out_specs = (
        P("level", None, "blk"),
        P("level", "blk", None, None, None),
        P("level", None, None),
    )

    return jax.shard_map(shards, mesh=mesh, in_specs=in_specs, out_specs=out_specs, check_vma=False)
```

```python
import functools

import jax
import jax.numpy as jnp
from jax import lax
from jax.experimental import pallas as pl
from jax.experimental.pallas import tpu as pltpu
from jax.sharding import PartitionSpec as P


f32 = jnp.float32
bf16 = jnp.bfloat16
VMEM_LIMIT = 12 << 20


def split(value):
    high = value.astype(bf16)
    return high, (value - high.astype(f32)).astype(bf16)


def wide_left(value):
    high, low = split(value)
    return jnp.concatenate([high, low, high], axis=1)


def wide_right(value):
    high, low = split(value)
    return jnp.concatenate([high, high, low], axis=0)


def wide_dot(left, right):
    return jnp.dot(left, right, preferred_element_type=f32)


def product(left, right):
    return wide_dot(wide_left(left), wide_right(right))


def call(kernel, out_shape, args, flops, in_specs=None, out_specs=None, scratch_shapes=()):
    size = lambda s: s.size * s.dtype.itemsize
    vmem = pl.BlockSpec(memory_space=pltpu.VMEM)
    moved = sum(size(a) for a in args) + sum(size(o) for o in jax.tree.leaves(out_shape))
    return pl.pallas_call(
        kernel,
        out_shape=out_shape,
        in_specs=in_specs or [vmem] * len(args),
        out_specs=out_specs or jax.tree.map(lambda _: vmem, out_shape),
        scratch_shapes=scratch_shapes,
        compiler_params=pltpu.CompilerParams(vmem_limit_bytes=VMEM_LIMIT),
        cost_estimate=pl.CostEstimate(flops=flops, bytes_accessed=moved, transcendentals=0),
    )(*args)


def span(index, length):
    return pl.ds(pl.multiple_of(index * length, 8), length)


def leaf_kernel(right, generator, inverse, lower, coupling, *refs):
    later, (away, solve_map, skeleton_map), refs = refs[:3], refs[3:6], refs[6:]
    (right_here, coupling_here, *later_here), refs = refs[:5], refs[5:]
    generator_here, inverse_here, lower_here, sems = refs
    core = lax.axis_index("blk") & 1
    half, k_half = right.shape[0] // 2, coupling.shape[0] // 2
    size = inverse.shape[0]
    copies = [
        pltpu.make_async_copy(source, target, sems.at[i])
        for i, (source, target) in enumerate(
            [
                (generator, generator_here),
                (inverse, inverse_here),
                (lower, lower_here),
                (right.at[span(1 - core, half)], right_here.at[0]),
                (coupling, coupling_here),
                (right.at[span(core, half)], right_here.at[1]),
                *((source.at[0], target) for source, target in zip(later, later_here)),
            ]
        )
    ]
    for copy in copies:
        copy.start()
    for copy in copies[:2]:
        copy.wait()
    solved = product(generator_here[:, :size], inverse_here[...])
    solve_map[...] = solved
    copies[2].wait()
    parts = wide_right(generator_here[:, size:] - product(solved, lower_here[...]))
    skeleton_map[...] = parts
    copies[3].wait()
    away[:half, :] = wide_dot(wide_left(right_here[0]), parts)
    copies[4].wait()
    away[half:, :] = wide_dot(wide_left(coupling_here[span(1 - core, k_half), :]), parts)
    for copy in copies[5:]:
        copy.wait()


def leaf_solve(child, right, coupling, solve_map, solved, leaf_map):
    parts = wide_right(solve_map[...])
    for part in range(2):
        solved[part] = wide_dot(wide_left(right[1 - part]), parts)
    on_target = lax.axis_index("blk") == child[0]
    leaf_map[...] = jnp.where(on_target, wide_dot(wide_left(coupling[...]), parts), 0.0)


def leaf_solve_kernel(bit, solved_early, map_early, *refs):
    solved, leaf_map = refs[-2:]
    early = (lax.axis_index("blk") >> bit) & 1

    @pl.when(early == 1)
    def _():
        solved[...] = solved_early[...]
        leaf_map[...] = map_early[...]

    @pl.when(early == 0)
    def _():
        leaf_solve(*refs)


def fold(tier, generator, inverse, lower, both):
    size = inverse.shape[0]
    solve_map = product(generator[:, :size], inverse)
    both[:, :size] = solve_map
    both[:, size:] = generator[:, size:] - product(solve_map, lower)
    upper = (lax.axis_index("blk") >> tier) & 1
    return wide_right(both[span(upper, size), :]), wide_right(both[span(1 - upper, size), :])


def first_fold_kernel(
    generator, inverse, lower, right, coupling, skeleton_map, mine_maps, other_maps, base, home, both
):
    core = lax.axis_index("blk") & 1
    k_half = home.shape[0]
    value = wide_dot(wide_left(right[1]), skeleton_map[...])
    home[...] = wide_dot(wide_left(coupling[span(core, k_half), :]), skeleton_map[...])
    mine_maps[0], other_maps[0] = fold(0, generator[...], inverse[...], lower[...], both)
    base[...] = wide_dot(wide_left(value), mine_maps[0])


def fold_kernel(first, generator, inverse, lower, *refs):
    mine_maps, other_maps, both = refs[-3:]
    for i in range(mine_maps.shape[0]):
        tier = first + i
        mine_maps[i], other_maps[i] = fold(tier, generator[tier], inverse[tier], lower[tier], both)


def base_kernel(index, home, mine_maps, base):
    base[...] = wide_dot(wide_left(home[...]), mine_maps[index])


def late_merge_kernel(index, bit, base, away, other_maps, child, right, coupling, solve_map, *refs):
    node, skeleton, solved, leaf_map = refs[-4:]
    merge_kernel(index, base, away, other_maps, node, skeleton)

    @pl.when((lax.axis_index("blk") >> bit) & 1 == 1)
    def _():
        leaf_solve(child, right, coupling, solve_map, solved, leaf_map)


def merge_kernel(index, base, away, other_maps, *refs):
    node, skeleton = refs[-2:]
    size = away.shape[1]
    both = base[...] + wide_dot(wide_left(away[...]), other_maps[index])
    skeleton[...] = both[:, size:]
    node[...] = both[:, :size]


def first_merge_kernel(base, away, other_maps, node, skeleton):
    half, size = node.shape
    both = base[...] + wide_dot(wide_left(away[:half, :]), other_maps[0])
    skeleton[...] = both[:, size:]
    node[...] = both[:, :size]


def carry_kernel(child, home, away, mine_maps, other_maps, next_maps, tail, carried, *climb):
    k_half, size = home.shape
    position = lax.axis_index("blk")
    mine = wide_dot(wide_left(home[...]), mine_maps[0])
    other = wide_dot(wide_left(away[away.shape[0] - k_half :, :]), other_maps[0])
    both = jnp.where(position == child[0], mine, 0.0) + jnp.where(position ^ 1 == child[0], other, 0.0)
    tail[...] = both[:, :size]
    carried[...] = both[:, size:]
    for out in climb:
        out[...] = wide_dot(wide_left(both[:, size:]), next_maps[0, :, size:])


def climb_kernel(index, carried, mine_maps, climb):
    size = carried.shape[1]
    climb[...] = wide_dot(wide_left(carried[...]), mine_maps[index, :, size:])


def relay_kernel(carried, far, out):
    out[0] = carried[...]
    out[1] = far[...]


def pair_kernel(index, home, away, mine_maps, other_maps, out):
    out[...] = wide_dot(wide_left(home[...]), mine_maps[index]) + wide_dot(
        wide_left(away[...]), other_maps[index]
    )


def top_kernel(index, tails, home, away, mine_maps, other_maps, top_mine, top_other, out):
    size = tails.shape[2]
    count = tails.shape[0]
    out[:count] = tails[...]
    both = wide_dot(wide_left(home[0]), mine_maps[index]) + wide_dot(
        wide_left(away[0]), other_maps[index]
    )
    out[count] = both[:, :size]
    both = wide_dot(wide_left(both[:, size:]), top_mine[0]) + wide_dot(
        wide_left(home[1] + away[1]), top_other[0]
    )
    out[count + 1] = both[:, :size]
    out[count + 2] = both[:, size:]


def last_merge_kernel(index, base, away, other_maps, tails, *refs):
    node, root = refs[-2:]
    half, size = away.shape
    both = base[...] + wide_dot(wide_left(away[...]), other_maps[index])
    root[:half, :] = both[:, size:]
    root[half:, :] = tails[tails.shape[0] - 1]
    node[...] = both[:, :size]


def maps_kernel(leaf_map, home, away, *refs):
    wide_maps, maps = refs[-2:]
    k_half, size = home.shape[1:]
    core = lax.axis_index("blk") & 1
    maps[:, :size] = leaf_map[...]
    for i in range(home.shape[0]):
        columns = slice((i + 1) * size, (i + 2) * size)
        maps[span(core, k_half), columns] = home[i]
        maps[span(1 - core, k_half), columns] = away[i]
    wide_maps[...] = wide_right(maps[...])


def final_kernel(fronts, height, solved, wide_maps, *refs):
    nodes, refs = refs[: 2 * height], refs[2 * height :]
    roots, refs = refs[: 2 * fronts], refs[2 * fronts :]
    leaf_out, node_out, root_out, root_maps, incoming, result, sems = refs
    core, level = lax.axis_index("blk") & 1, lax.axis_index("level")
    half, size = solved.shape[1:]
    k_half = root_maps.shape[1] // 2
    for front in range(1, fronts):
        root_maps[front, span(core, k_half), :] = roots[2 * front][half:, :]
        root_maps[front, span(1 - core, k_half), :] = roots[2 * front + 1][half:, :]

    def both_rows(mask):
        return jnp.concatenate([roots[2 * mask][:half, :], roots[2 * mask + 1][:half, :]], axis=0)

    @pl.when(level == 0)
    def _():
        incoming[...] = jnp.zeros_like(incoming)

    for here in range(1, fronts):

        @pl.when(level == here)
        def _():
            value = both_rows(here)
            for front in range(1, here):
                value = both_rows(here ^ front) + product(value, root_maps[here ^ front])
            incoming[...] = value

    copies = []
    step = half // 2
    for chunk in range(4):
        part, first = chunk // 2, chunk % 2 * step
        inner = slice(first, first + step)
        rows = pl.ds(pl.multiple_of((core if part == 0 else 1 - core) * half + first, 8), step)
        change = wide_dot(wide_left(incoming[chunk * step : (chunk + 1) * step, :]), wide_maps[...])
        bases = (
            [solved[part, inner, :]]
            + [nodes[2 * tier + part][inner, :] for tier in range(height)]
            + [roots[part][inner, :]]
        )
        targets = (
            [leaf_out.at[rows]] + [node_out.at[tier, rows] for tier in range(height)] + [root_out.at[rows]]
        )
        for i, (base, target) in enumerate(zip(bases, targets)):
            result[chunk, i] = base + change[:, i * size : (i + 1) * size]
            copies.append(pltpu.make_async_copy(result.at[chunk, i], target, sems.at[chunk, i]))
            copies[-1].start()
    for copy in copies:
        copy.wait()


def shards(
    right_sides,
    leaf_gen,
    leaf_inverse,
    leaf_lower,
    node_gen,
    node_inverse,
    node_lower,
    coupling,
    child_leaf,
):
    rows, leaf_size = right_sides.shape[1:]
    size = leaf_lower.shape[2]
    k_rows = coupling.shape[1]
    height = node_gen.shape[2]
    fronts = lax.axis_size("level")
    leaves = lax.axis_size("blk")
    half = rows // 2
    part = half + k_rows // 2
    smem = pl.BlockSpec(memory_space=pltpu.SMEM)
    vmem = pl.BlockSpec(memory_space=pltpu.VMEM)
    hbm = pl.BlockSpec(memory_space=pltpu.HBM)
    anywhere = pl.BlockSpec(memory_space=pl.ANY)
    array = lambda *shape: jax.ShapeDtypeStruct(shape, f32)

    def blk_swap(value, mask):
        return lax.ppermute(value, "blk", [(i, i ^ mask) for i in range(leaves)])

    def level_swap(value, mask):
        return lax.ppermute(value, "level", [(i, i ^ mask) for i in range(fronts)])

    k_half = k_rows // 2
    node_params = (node_gen[0, 0], node_inverse[0, 0], node_lower[0, 0])
    away, leaf_solve_map, leaf_skeleton, right_here, coupling_here, *first_params = call(
        leaf_kernel,
        (
            array(part, size),
            array(leaf_size, size),
            jax.ShapeDtypeStruct((3 * leaf_size, size), bf16),
            array(2, half, leaf_size),
            array(k_rows, leaf_size),
            *(array(*value.shape[1:]) for value in node_params),
        ),
        tuple(
            pltpu.with_memory_space_constraint(value, pltpu.HBM)
            for value in (
                right_sides[0],
                leaf_gen[0],
                leaf_inverse[0],
                leaf_lower[0],
                coupling[0],
                *node_params,
            )
        ),
        6 * (part + leaf_size) * leaf_size * size,
        in_specs=[hbm] * 8,
        scratch_shapes=[
            pltpu.VMEM((leaf_size, leaf_size), f32),
            pltpu.VMEM((size, size), f32),
            pltpu.VMEM((size, size), f32),
            pltpu.SemaphoreType.DMA((9,)),
        ],
    )
    merge_flops = 6 * half * 2 * size * size
    fold_flops = 6 * 4 * size * size * size
    wide = lambda count: jax.ShapeDtypeStruct((count, 3 * size, 2 * size), bf16)
    both = pltpu.VMEM((2 * size, 2 * size), f32)
    first_mine, first_other, base, home = call(
        first_fold_kernel,
        (wide(1), wide(1), array(half, 2 * size), array(k_half, size)),
        (*first_params, right_here, coupling_here, leaf_skeleton),
        fold_flops + 6 * part * (leaf_size + 2 * size) * size,
        scratch_shapes=[both],
    )
    *node_params, away = lax.optimization_barrier((*node_params, away))
    away = blk_swap(away, 1)
    node, skeleton = call(
        first_merge_kernel,
        (array(half, size), array(half, size)),
        (base, away, first_other),
        merge_flops,
    )
    nodes, away_first = [node], away

    def folds(first, last, *after):
        return call(
            functools.partial(fold_kernel, first),
            (wide(last - first),) * 2,
            (*node_params, *after),
            (last - first) * fold_flops,
            in_specs=[vmem] * 3 + [anywhere] * len(after),
            scratch_shapes=[both],
        )

    child_leaf, skeleton = lax.optimization_barrier((child_leaf, skeleton))
    for tier in range(1, height):
        away = blk_swap(skeleton, 1 << tier)
        after = ()
        if tier == 1:
            mine_maps, other_maps = folds(1, height - 1)
            tail, carried, *climb = call(
                carry_kernel,
                (array(k_half, size),) * (3 if height == 3 else 2),
                (child_leaf, home, away_first, first_mine, first_other, mine_maps),
                6 * k_half * 5 * size * size,
                in_specs=[smem] + [vmem] * 5,
            )
            tails = [tail]
        if tier < height - 2:
            pair = call(
                functools.partial(pair_kernel, tier - 1),
                array(k_half, 2 * size),
                (carried, blk_swap(carried, 1 << tier), mine_maps, other_maps),
                6 * k_half * 4 * size * size,
            )
            tails.append(pair[:, :size])
            carried = pair[:, size:]
        if tier == height - 2:
            if not climb:
                climb = [
                    call(
                        functools.partial(climb_kernel, tier - 1),
                        array(k_half, size),
                        (carried, mine_maps),
                        6 * k_half * size * size,
                    )
                ]
            far = blk_swap(climb[0], 2 << tier)
            after = (climb[0],)
        if tier == height - 1:
            top_mine, top_other = folds(height - 1, height)
            relay = call(relay_kernel, array(2, k_half, size), (carried, far), k_half * size)
            relayed = blk_swap(relay, 1 << (tier - 1))
            tails = call(
                functools.partial(top_kernel, tier - 2),
                array(height + 1, k_half, size),
                (jnp.stack(tails), relay, relayed, mine_maps, other_maps, top_mine, top_other),
                6 * k_half * 6 * size * size,
            )
            solved, leaf_map = call(
                functools.partial(leaf_solve_kernel, height - 2),
                (array(2, half, size), array(k_rows, size)),
                (*early, *leaf_args),
                6 * (rows + k_rows) * leaf_size * size,
                in_specs=[vmem] * 2 + [smem] + [vmem] * 3,
            )
            after = (solved,)
        last = tier == height - 1
        if last:
            mine_maps, other_maps = top_mine, top_other
        index = 0 if last else tier - 1
        base = call(
            functools.partial(base_kernel, index),
            array(half, 2 * size),
            (skeleton, mine_maps),
            merge_flops,
        )
        leaf_args = (child_leaf, right_here, coupling_here, leaf_solve_map)
        kernel = functools.partial(last_merge_kernel if last else merge_kernel, index)
        args, specs = (base, away, other_maps), [vmem] * 3
        shapes = (array(half, size), array(part if last else half, size))
        if last:
            args, specs = args + (tails,), specs + [vmem]
        if tier == height - 2:
            kernel = functools.partial(late_merge_kernel, index, height - 2)
            args, specs = args + leaf_args, specs + [smem] + [vmem] * 3
            shapes += (array(2, half, size), array(k_rows, size))
        node, skeleton, *early = call(
            kernel, shapes, args + after, merge_flops, in_specs=specs + [anywhere] * len(after)
        )
        nodes.append(node)
    received = [level_swap(skeleton, mask) for mask in range(1, fronts)]
    roots = [skeleton, blk_swap(skeleton, 1)]
    for value in received:
        roots += [value, blk_swap(value, 1)]
    pairs = []
    for value in nodes:
        pairs += [value, blk_swap(value, 1)]
    after = (*pairs[1::2], roots[1])
    wide_maps = call(
        maps_kernel,
        jax.ShapeDtypeStruct((3 * k_rows, size * (height + 2)), bf16),
        (leaf_map, tails, blk_swap(tails, 1), *after),
        k_rows * size * (height + 2) * 4,
        in_specs=[vmem] * 3 + [anywhere] * len(after),
        scratch_shapes=[pltpu.VMEM((k_rows, size * (height + 2)), f32)],
    )
    leaf_out, node_out, root_out = call(
        functools.partial(final_kernel, fronts, height),
        (array(rows, size), array(height, rows, size), array(rows, size)),
        (solved, wide_maps, *pairs, *roots),
        6 * rows * size * size * (height + 2),
        out_specs=(hbm,) * 3,
        scratch_shapes=[
            pltpu.VMEM((fronts, k_rows, size), f32),
            pltpu.VMEM((rows, size), f32),
            pltpu.VMEM((4, height + 2, rows // 4, size), f32),
            pltpu.SemaphoreType.DMA((4, height + 2)),
        ],
    )
    return (leaf_out[None], node_out[None, None], root_out[None])


def solution(mesh):
    in_specs = (
        P("level", None, "blk"),
        P("level", "blk", None),
        P("level", "blk", None),
        P("level", "blk", None),
        P("level", "blk", None, None, None),
        P("level", "blk", None, None, None),
        P("level", "blk", None, None, None),
        P("level", None, None),
        P("level"),
    )
    out_specs = (
        P("level", None, "blk"),
        P("level", "blk", None, None, None),
        P("level", None, None),
    )

    return jax.shard_map(shards, mesh=mesh, in_specs=in_specs, out_specs=out_specs, check_vma=False)
```

```python
import functools

import jax
import jax.numpy as jnp
from jax import lax
from jax.experimental import pallas as pl
from jax.experimental.pallas import tpu as pltpu
from jax.sharding import PartitionSpec as P


f32 = jnp.float32
bf16 = jnp.bfloat16
VMEM_LIMIT = 12 << 20


def split(value):
    high = value.astype(bf16)
    return high, (value - high.astype(f32)).astype(bf16)


def wide_left(value):
    high, low = split(value)
    return jnp.concatenate([high, low, high], axis=1)


def wide_right(value):
    high, low = split(value)
    return jnp.concatenate([high, high, low], axis=0)


def wide_dot(left, right):
    return jnp.dot(left, right, preferred_element_type=f32)


def product(left, right):
    return wide_dot(wide_left(left), wide_right(right))


def call(kernel, out_shape, args, flops, in_specs=None, out_specs=None, scratch_shapes=(), aliases={}):
    size = lambda s: s.size * s.dtype.itemsize
    vmem = pl.BlockSpec(memory_space=pltpu.VMEM)
    moved = sum(size(a) for a in args) + sum(size(o) for o in jax.tree.leaves(out_shape))
    return pl.pallas_call(
        kernel,
        out_shape=out_shape,
        in_specs=in_specs or [vmem] * len(args),
        out_specs=out_specs or jax.tree.map(lambda _: vmem, out_shape),
        scratch_shapes=scratch_shapes,
        input_output_aliases=aliases,
        compiler_params=pltpu.CompilerParams(vmem_limit_bytes=VMEM_LIMIT),
        cost_estimate=pl.CostEstimate(flops=flops, bytes_accessed=moved, transcendentals=0),
    )(*args)


def span(index, length):
    return pl.ds(pl.multiple_of(index * length, 8), length)


def leaf_kernel(right, generator, inverse, lower, coupling, *refs):
    later, (away, solve_map, skeleton_map), refs = refs[:3], refs[3:6], refs[6:]
    (right_here, coupling_here, *later_here), refs = refs[:5], refs[5:]
    generator_here, inverse_here, lower_here, sems = refs
    core = lax.axis_index("blk") & 1
    half, k_half = right.shape[0] // 2, coupling.shape[0] // 2
    size = inverse.shape[0]
    copies = [
        pltpu.make_async_copy(source, target, sems.at[i])
        for i, (source, target) in enumerate(
            [
                (generator, generator_here),
                (inverse, inverse_here),
                (lower, lower_here),
                (right.at[span(1 - core, half)], right_here.at[0]),
                (coupling, coupling_here),
                (right.at[span(core, half)], right_here.at[1]),
                *((source.at[0], target) for source, target in zip(later, later_here)),
            ]
        )
    ]
    for copy in copies:
        copy.start()
    for copy in copies[:2]:
        copy.wait()
    solved = product(generator_here[:, :size], inverse_here[...])
    solve_map[...] = solved
    copies[2].wait()
    parts = wide_right(generator_here[:, size:] - product(solved, lower_here[...]))
    skeleton_map[...] = parts
    copies[3].wait()
    away[:half, :] = wide_dot(wide_left(right_here[0]), parts)
    copies[4].wait()
    away[half:, :] = wide_dot(wide_left(coupling_here[span(1 - core, k_half), :]), parts)
    for copy in copies[5:]:
        copy.wait()


def leaf_solve(child, right, coupling, solve_map, solved, leaf_map):
    parts = wide_right(solve_map[...])
    for part in range(2):
        solved[part] = wide_dot(wide_left(right[1 - part]), parts)
    on_target = lax.axis_index("blk") == child[0]
    leaf_map[...] = jnp.where(on_target, wide_dot(wide_left(coupling[...]), parts), 0.0)


def leaf_solve_kernel(bit, solved_early, map_early, *refs):
    solved, leaf_map = refs[-2:]
    early = (lax.axis_index("blk") >> bit) & 1

    @pl.when(early == 1)
    def _():
        solved[...] = solved_early[...]
        leaf_map[...] = map_early[...]

    @pl.when(early == 0)
    def _():
        leaf_solve(*refs)


def fold(tier, generator, inverse, lower, both):
    size = inverse.shape[0]
    solve_map = product(generator[:, :size], inverse)
    both[:, :size] = solve_map
    both[:, size:] = generator[:, size:] - product(solve_map, lower)
    upper = (lax.axis_index("blk") >> tier) & 1
    return wide_right(both[span(upper, size), :]), wide_right(both[span(1 - upper, size), :])


def first_fold_kernel(
    generator, inverse, lower, right, coupling, skeleton_map, mine_maps, other_maps, base, home, both
):
    core = lax.axis_index("blk") & 1
    k_half = home.shape[0]
    value = wide_dot(wide_left(right[1]), skeleton_map[...])
    home[...] = wide_dot(wide_left(coupling[span(core, k_half), :]), skeleton_map[...])
    mine_maps[0], other_maps[0] = fold(0, generator[...], inverse[...], lower[...], both)
    base[...] = wide_dot(wide_left(value), mine_maps[0])


def fold_kernel(first, generator, inverse, lower, *refs):
    mine_maps, other_maps, both = refs[-3:]
    for i in range(mine_maps.shape[0]):
        tier = first + i
        mine_maps[i], other_maps[i] = fold(tier, generator[tier], inverse[tier], lower[tier], both)


def base_kernel(index, home, mine_maps, base):
    base[...] = wide_dot(wide_left(home[...]), mine_maps[index])


def late_merge_kernel(index, bit, base, away, other_maps, child, right, coupling, solve_map, *refs):
    node, skeleton, solved, leaf_map = refs[-4:]
    merge_kernel(index, base, away, other_maps, node, skeleton)

    @pl.when((lax.axis_index("blk") >> bit) & 1 == 1)
    def _():
        leaf_solve(child, right, coupling, solve_map, solved, leaf_map)


def merge_kernel(index, base, away, other_maps, *refs):
    node, skeleton = refs[-2:]
    size = away.shape[1]
    both = base[...] + wide_dot(wide_left(away[...]), other_maps[index])
    skeleton[...] = both[:, size:]
    node[...] = both[:, :size]


def first_merge_kernel(base, away, other_maps, node, skeleton):
    half, size = node.shape
    both = base[...] + wide_dot(wide_left(away[:half, :]), other_maps[0])
    skeleton[...] = both[:, size:]
    node[...] = both[:, :size]


def carry_kernel(child, home, away, mine_maps, other_maps, next_maps, tail, carried, *climb):
    k_half, size = home.shape
    position = lax.axis_index("blk")
    mine = wide_dot(wide_left(home[...]), mine_maps[0])
    other = wide_dot(wide_left(away[away.shape[0] - k_half :, :]), other_maps[0])
    both = jnp.where(position == child[0], mine, 0.0) + jnp.where(position ^ 1 == child[0], other, 0.0)
    tail[...] = both[:, :size]
    carried[...] = both[:, size:]
    for out in climb:
        out[...] = wide_dot(wide_left(both[:, size:]), next_maps[0, :, size:])


def climb_kernel(index, carried, mine_maps, climb):
    size = carried.shape[1]
    climb[...] = wide_dot(wide_left(carried[...]), mine_maps[index, :, size:])


def relay_kernel(carried, far, out):
    out[0] = carried[...]
    out[1] = far[...]


def pair_kernel(index, home, away, mine_maps, other_maps, out):
    out[...] = wide_dot(wide_left(home[...]), mine_maps[index]) + wide_dot(
        wide_left(away[...]), other_maps[index]
    )


def top_kernel(index, tails, home, away, mine_maps, other_maps, top_mine, top_other, out):
    size = tails.shape[2]
    count = tails.shape[0]
    out[:count] = tails[...]
    both = wide_dot(wide_left(home[0]), mine_maps[index]) + wide_dot(
        wide_left(away[0]), other_maps[index]
    )
    out[count] = both[:, :size]
    both = wide_dot(wide_left(both[:, size:]), top_mine[0]) + wide_dot(
        wide_left(home[1] + away[1]), top_other[0]
    )
    out[count + 1] = both[:, :size]
    out[count + 2] = both[:, size:]


def last_merge_kernel(index, base, away, other_maps, tails, *refs):
    node, root = refs[-2:]
    half, size = away.shape
    both = base[...] + wide_dot(wide_left(away[...]), other_maps[index])
    root[:half, :] = both[:, size:]
    root[half:, :] = tails[tails.shape[0] - 1]
    node[...] = both[:, :size]


def maps_kernel(leaf_map, home, away, *refs):
    wide_maps, maps = refs[-2:]
    k_half, size = home.shape[1:]
    core = lax.axis_index("blk") & 1
    maps[:, :size] = leaf_map[...]
    for i in range(home.shape[0]):
        columns = slice((i + 1) * size, (i + 2) * size)
        maps[span(core, k_half), columns] = home[i]
        maps[span(1 - core, k_half), columns] = away[i]
    wide_maps[...] = wide_right(maps[...])


def affected(child, height):
    position = lax.axis_index("blk")
    below = lax.axis_index("level") > 0
    shared = [position >> t == child[0] >> t for t in range(height)]
    return [jnp.logical_and(below, same) for same in shared] + [below, below]


def targets(leaf_out, node_out, root_out, rows):
    nodes = [node_out.at[tier, rows] for tier in range(node_out.shape[0])]
    return [leaf_out.at[rows]] + nodes + [root_out.at[rows]]


def part_rows(part, half):
    core = lax.axis_index("blk") & 1
    return pl.ds(pl.multiple_of((core if part == 0 else 1 - core) * half, 8), half)


def early_kernel(height, child, solved, *refs):
    nodes, roots, refs = refs[: 2 * height], refs[2 * height : 2 * height + 2], refs[-4:]
    leaf_out, node_out, root_out, sems = refs
    half, _ = solved.shape[1:]
    late = affected(child, height)
    copies = []
    for part in range(2):
        outs = targets(leaf_out, node_out, root_out, part_rows(part, half))
        bases = [solved.at[part]] + [nodes[2 * tier + part] for tier in range(height)]
        bases += [roots[part].at[pl.ds(0, half)]]
        copies += [
            (late[i], pltpu.make_async_copy(base, out, sems.at[part, i]))
            for i, (base, out) in enumerate(zip(bases, outs))
        ]
    for act in ("start", "wait"):
        for skip, copy in copies:
            pl.when(jnp.logical_not(skip))(getattr(copy, act))


def final_kernel(fronts, height, child, solved, wide_maps, *refs):
    nodes, refs = refs[: 2 * height], refs[2 * height :]
    roots, refs = refs[: 2 * fronts], refs[2 * fronts + 3 :]
    leaf_out, node_out, root_out, root_maps, incoming, result, sems = refs
    core, level = lax.axis_index("blk") & 1, lax.axis_index("level")
    half, size = solved.shape[1:]
    k_half = root_maps.shape[1] // 2
    count = height + 2
    late = affected(child, height)
    for front in range(1, fronts):
        root_maps[front, span(core, k_half), :] = roots[2 * front][half:, :]
        root_maps[front, span(1 - core, k_half), :] = roots[2 * front + 1][half:, :]

    def both_rows(mask):
        return jnp.concatenate([roots[2 * mask][:half, :], roots[2 * mask + 1][:half, :]], axis=0)

    for here in range(1, fronts):

        @pl.when(level == here)
        def _():
            value = both_rows(here)
            for front in range(1, here):
                value = both_rows(here ^ front) + product(value, root_maps[here ^ front])
            incoming[...] = wide_left(value)

    step = half // 2
    copies = []
    for chunk in range(4):
        first = (core if chunk < 2 else 1 - core) * half + chunk % 2 * step
        outs = targets(leaf_out, node_out, root_out, pl.ds(pl.multiple_of(first, 8), step))
        copies.append(
            [
                pltpu.make_async_copy(result.at[chunk, i], out, sems.at[chunk, i])
                for i, out in enumerate(outs)
            ]
        )

    def update(first, last):
        for chunk in range(4):
            part, inner = chunk // 2, slice(chunk % 2 * step, (chunk % 2 + 1) * step)
            change = wide_dot(
                incoming[chunk * step : (chunk + 1) * step, :], wide_maps[:, first * size : last * size]
            )
            for i in range(first, last):
                if i == 0:
                    base = solved[part, inner, :]
                elif i <= height:
                    base = nodes[2 * (i - 1) + part][inner, :]
                else:
                    base = roots[part][inner, :]
                result[chunk, i] = base + change[:, (i - first) * size : (i + 1 - first) * size]
                copies[chunk][i].start()

    pl.when(late[height])(functools.partial(update, height, count))
    for i in reversed(range(height)):
        pl.when(late[i])(functools.partial(update, i, i + 1))
    for i, flag in enumerate(late):
        for chunk in range(4):
            pl.when(flag)(copies[chunk][i].wait)


def shards(
    right_sides,
    leaf_gen,
    leaf_inverse,
    leaf_lower,
    node_gen,
    node_inverse,
    node_lower,
    coupling,
    child_leaf,
):
    rows, leaf_size = right_sides.shape[1:]
    size = leaf_lower.shape[2]
    k_rows = coupling.shape[1]
    height = node_gen.shape[2]
    fronts = lax.axis_size("level")
    leaves = lax.axis_size("blk")
    half = rows // 2
    part = half + k_rows // 2
    smem = pl.BlockSpec(memory_space=pltpu.SMEM)
    vmem = pl.BlockSpec(memory_space=pltpu.VMEM)
    hbm = pl.BlockSpec(memory_space=pltpu.HBM)
    anywhere = pl.BlockSpec(memory_space=pl.ANY)
    array = lambda *shape: jax.ShapeDtypeStruct(shape, f32)

    def blk_swap(value, mask):
        return lax.ppermute(value, "blk", [(i, i ^ mask) for i in range(leaves)])

    def level_swap(value, mask):
        return lax.ppermute(value, "level", [(i, i ^ mask) for i in range(fronts)])

    k_half = k_rows // 2
    node_params = (node_gen[0, 0], node_inverse[0, 0], node_lower[0, 0])
    away, leaf_solve_map, leaf_skeleton, right_here, coupling_here, *first_params = call(
        leaf_kernel,
        (
            array(part, size),
            array(leaf_size, size),
            jax.ShapeDtypeStruct((3 * leaf_size, size), bf16),
            array(2, half, leaf_size),
            array(k_rows, leaf_size),
            *(array(*value.shape[1:]) for value in node_params),
        ),
        tuple(
            pltpu.with_memory_space_constraint(value, pltpu.HBM)
            for value in (
                right_sides[0],
                leaf_gen[0],
                leaf_inverse[0],
                leaf_lower[0],
                coupling[0],
                *node_params,
            )
        ),
        6 * (part + leaf_size) * leaf_size * size,
        in_specs=[hbm] * 8,
        scratch_shapes=[
            pltpu.VMEM((leaf_size, leaf_size), f32),
            pltpu.VMEM((size, size), f32),
            pltpu.VMEM((size, size), f32),
            pltpu.SemaphoreType.DMA((9,)),
        ],
    )
    merge_flops = 6 * half * 2 * size * size
    fold_flops = 6 * 4 * size * size * size
    wide = lambda count: jax.ShapeDtypeStruct((count, 3 * size, 2 * size), bf16)
    both = pltpu.VMEM((2 * size, 2 * size), f32)
    first_mine, first_other, base, home = call(
        first_fold_kernel,
        (wide(1), wide(1), array(half, 2 * size), array(k_half, size)),
        (*first_params, right_here, coupling_here, leaf_skeleton),
        fold_flops + 6 * part * (leaf_size + 2 * size) * size,
        scratch_shapes=[both],
    )
    *node_params, away = lax.optimization_barrier((*node_params, away))
    away = blk_swap(away, 1)
    node, skeleton = call(
        first_merge_kernel,
        (array(half, size), array(half, size)),
        (base, away, first_other),
        merge_flops,
    )
    nodes, away_first = [node], away

    def folds(first, last, *after):
        return call(
            functools.partial(fold_kernel, first),
            (wide(last - first),) * 2,
            (*node_params, *after),
            (last - first) * fold_flops,
            in_specs=[vmem] * 3 + [anywhere] * len(after),
            scratch_shapes=[both],
        )

    child_leaf, skeleton = lax.optimization_barrier((child_leaf, skeleton))
    for tier in range(1, height):
        away = blk_swap(skeleton, 1 << tier)
        after = ()
        if tier == 1:
            mine_maps, other_maps = folds(1, height - 1)
            tail, carried, *climb = call(
                carry_kernel,
                (array(k_half, size),) * (3 if height == 3 else 2),
                (child_leaf, home, away_first, first_mine, first_other, mine_maps),
                6 * k_half * 5 * size * size,
                in_specs=[smem] + [vmem] * 5,
            )
            tails = [tail]
        if tier < height - 2:
            pair = call(
                functools.partial(pair_kernel, tier - 1),
                array(k_half, 2 * size),
                (carried, blk_swap(carried, 1 << tier), mine_maps, other_maps),
                6 * k_half * 4 * size * size,
            )
            tails.append(pair[:, :size])
            carried = pair[:, size:]
        if tier == height - 2:
            if not climb:
                climb = [
                    call(
                        functools.partial(climb_kernel, tier - 1),
                        array(k_half, size),
                        (carried, mine_maps),
                        6 * k_half * size * size,
                    )
                ]
            far = blk_swap(climb[0], 2 << tier)
            after = (climb[0],)
        if tier == height - 1:
            top_mine, top_other = folds(height - 1, height)
            relay = call(relay_kernel, array(2, k_half, size), (carried, far), k_half * size)
            relayed = blk_swap(relay, 1 << (tier - 1))
            tails = call(
                functools.partial(top_kernel, tier - 2),
                array(height + 1, k_half, size),
                (jnp.stack(tails), relay, relayed, mine_maps, other_maps, top_mine, top_other),
                6 * k_half * 6 * size * size,
            )
            solved, leaf_map = call(
                functools.partial(leaf_solve_kernel, height - 2),
                (array(2, half, size), array(k_rows, size)),
                (*early, *leaf_args),
                6 * (rows + k_rows) * leaf_size * size,
                in_specs=[vmem] * 2 + [smem] + [vmem] * 3,
            )
            after = (solved,)
        last = tier == height - 1
        if last:
            mine_maps, other_maps = top_mine, top_other
        index = 0 if last else tier - 1
        base = call(
            functools.partial(base_kernel, index),
            array(half, 2 * size),
            (skeleton, mine_maps),
            merge_flops,
        )
        leaf_args = (child_leaf, right_here, coupling_here, leaf_solve_map)
        kernel = functools.partial(last_merge_kernel if last else merge_kernel, index)
        args, specs = (base, away, other_maps), [vmem] * 3
        shapes = (array(half, size), array(part if last else half, size))
        if last:
            args, specs = args + (tails,), specs + [vmem]
        if tier == height - 2:
            kernel = functools.partial(late_merge_kernel, index, height - 2)
            args, specs = args + leaf_args, specs + [smem] + [vmem] * 3
            shapes += (array(2, half, size), array(k_rows, size))
        node, skeleton, *early = call(
            kernel, shapes, args + after, merge_flops, in_specs=specs + [anywhere] * len(after)
        )
        nodes.append(node)
    received = [level_swap(skeleton, mask) for mask in range(1, fronts)]
    roots = [skeleton, blk_swap(skeleton, 1)]
    for value in received:
        roots += [value, blk_swap(value, 1)]
    pairs = []
    for value in nodes:
        pairs += [value, blk_swap(value, 1)]
    shapes = (array(rows, size), array(height, rows, size), array(rows, size))
    early = call(
        functools.partial(early_kernel, height),
        shapes,
        (child_leaf, solved, *pairs, *roots[:2]),
        rows * size,
        in_specs=[smem] + [vmem] * (len(pairs) + 3),
        out_specs=(hbm,) * 3,
        scratch_shapes=[pltpu.SemaphoreType.DMA((2, height + 2))],
    )
    wide_maps = call(
        maps_kernel,
        jax.ShapeDtypeStruct((3 * k_rows, size * (height + 2)), bf16),
        (leaf_map, tails, blk_swap(tails, 1)),
        k_rows * size * (height + 2) * 4,
        scratch_shapes=[pltpu.VMEM((k_rows, size * (height + 2)), f32)],
    )
    args = (child_leaf, solved, wide_maps, *pairs, *roots)
    leaf_out, node_out, root_out = call(
        functools.partial(final_kernel, fronts, height),
        shapes,
        (*args, *early),
        6 * rows * size * size * (height + 2),
        in_specs=[smem] + [vmem] * (len(args) - 1) + [hbm] * 3,
        out_specs=(hbm,) * 3,
        aliases={len(args) + i: i for i in range(3)},
        scratch_shapes=[
            pltpu.VMEM((fronts, k_rows, size), f32),
            pltpu.VMEM((rows, 3 * size), bf16),
            pltpu.VMEM((4, height + 2, rows // 4, size), f32),
            pltpu.SemaphoreType.DMA((4, height + 2)),
        ],
    )
    return (leaf_out[None], node_out[None, None], root_out[None])


def solution(mesh):
    in_specs = (
        P("level", None, "blk"),
        P("level", "blk", None),
        P("level", "blk", None),
        P("level", "blk", None),
        P("level", "blk", None, None, None),
        P("level", "blk", None, None, None),
        P("level", "blk", None, None, None),
        P("level", None, None),
        P("level"),
    )
    out_specs = (
        P("level", None, "blk"),
        P("level", "blk", None, None, None),
        P("level", None, None),
    )

    return jax.shard_map(shards, mesh=mesh, in_specs=in_specs, out_specs=out_specs, check_vma=False)
```

```python
import functools

import jax
import jax.numpy as jnp
from jax import lax
from jax.experimental import pallas as pl
from jax.experimental.pallas import tpu as pltpu
from jax.sharding import PartitionSpec as P


f32 = jnp.float32
bf16 = jnp.bfloat16
VMEM_LIMIT = 12 << 20


def split(value):
    high = value.astype(bf16)
    return high, (value - high.astype(f32)).astype(bf16)


def wide_left(value):
    high, low = split(value)
    return jnp.concatenate([high, low, high], axis=1)


def wide_right(value):
    high, low = split(value)
    return jnp.concatenate([high, high, low], axis=0)


def wide_dot(left, right):
    return jnp.dot(left, right, preferred_element_type=f32)


def product(left, right):
    return wide_dot(wide_left(left), wide_right(right))


def call(kernel, out_shape, args, flops, in_specs=None, out_specs=None, scratch_shapes=(), aliases={}):
    size = lambda s: s.size * s.dtype.itemsize
    vmem = pl.BlockSpec(memory_space=pltpu.VMEM)
    moved = sum(size(a) for a in args) + sum(size(o) for o in jax.tree.leaves(out_shape))
    return pl.pallas_call(
        kernel,
        out_shape=out_shape,
        in_specs=in_specs or [vmem] * len(args),
        out_specs=out_specs or jax.tree.map(lambda _: vmem, out_shape),
        scratch_shapes=scratch_shapes,
        input_output_aliases=aliases,
        compiler_params=pltpu.CompilerParams(vmem_limit_bytes=VMEM_LIMIT),
        cost_estimate=pl.CostEstimate(flops=flops, bytes_accessed=moved, transcendentals=0),
    )(*args)


def span(index, length):
    return pl.ds(pl.multiple_of(index * length, 8), length)


def leaf_kernel(right, generator, inverse, lower, coupling, *refs):
    later, (away, solve_map, skeleton_map), refs = refs[:3], refs[3:6], refs[6:]
    (right_here, coupling_here, *later_here), refs = refs[:5], refs[5:]
    generator_here, inverse_here, lower_here, sems = refs
    core = lax.axis_index("blk") & 1
    half, k_half = right.shape[0] // 2, coupling.shape[0] // 2
    size = inverse.shape[0]
    copies = [
        pltpu.make_async_copy(source, target, sems.at[i])
        for i, (source, target) in enumerate(
            [
                (generator, generator_here),
                (inverse, inverse_here),
                (lower, lower_here),
                (right.at[span(1 - core, half)], right_here.at[0]),
                (coupling, coupling_here),
                (right.at[span(core, half)], right_here.at[1]),
                *((source.at[0], target) for source, target in zip(later, later_here)),
            ]
        )
    ]
    for copy in copies:
        copy.start()
    for copy in copies[:2]:
        copy.wait()
    solved = product(generator_here[:, :size], inverse_here[...])
    solve_map[...] = solved
    copies[2].wait()
    parts = wide_right(generator_here[:, size:] - product(solved, lower_here[...]))
    skeleton_map[...] = parts
    copies[3].wait()
    away[:half, :] = wide_dot(wide_left(right_here[0]), parts)
    copies[4].wait()
    away[half:, :] = wide_dot(wide_left(coupling_here[span(1 - core, k_half), :]), parts)
    for copy in copies[5:]:
        copy.wait()


def leaf_solve(child, right, coupling, solve_map, solved, leaf_map):
    parts = wide_right(solve_map[...])
    for part in range(2):
        solved[part] = wide_dot(wide_left(right[1 - part]), parts)
    on_target = lax.axis_index("blk") == child[0]
    leaf_map[...] = jnp.where(on_target, wide_dot(wide_left(coupling[...]), parts), 0.0)


def leaf_solve_kernel(bit, solved_early, map_early, *refs):
    solved, leaf_map = refs[-2:]
    early = (lax.axis_index("blk") >> bit) & 1

    @pl.when(early == 1)
    def _():
        solved[...] = solved_early[...]
        leaf_map[...] = map_early[...]

    @pl.when(early == 0)
    def _():
        leaf_solve(*refs)


def fold(tier, generator, inverse, lower, both):
    size = inverse.shape[0]
    solve_map = product(generator[:, :size], inverse)
    both[:, :size] = solve_map
    both[:, size:] = generator[:, size:] - product(solve_map, lower)
    upper = (lax.axis_index("blk") >> tier) & 1
    return wide_right(both[span(upper, size), :]), wide_right(both[span(1 - upper, size), :])


def first_fold_kernel(
    generator, inverse, lower, right, coupling, skeleton_map, mine_maps, other_maps, base, home, both
):
    core = lax.axis_index("blk") & 1
    k_half = home.shape[0]
    value = wide_dot(wide_left(right[1]), skeleton_map[...])
    home[...] = wide_dot(wide_left(coupling[span(core, k_half), :]), skeleton_map[...])
    mine_maps[0], other_maps[0] = fold(0, generator[...], inverse[...], lower[...], both)
    base[...] = wide_dot(wide_left(value), mine_maps[0])


def fold_kernel(first, generator, inverse, lower, *refs):
    mine_maps, other_maps, both = refs[-3:]
    for i in range(mine_maps.shape[0]):
        tier = first + i
        mine_maps[i], other_maps[i] = fold(tier, generator[tier], inverse[tier], lower[tier], both)


def base_kernel(index, home, mine_maps, base):
    base[...] = wide_dot(wide_left(home[...]), mine_maps[index])


def late_merge_kernel(index, bit, base, away, other_maps, child, right, coupling, solve_map, *refs):
    node, skeleton, solved, leaf_map = refs[-4:]
    merge_kernel(index, base, away, other_maps, node, skeleton)

    @pl.when((lax.axis_index("blk") >> bit) & 1 == 1)
    def _():
        leaf_solve(child, right, coupling, solve_map, solved, leaf_map)


def merge_kernel(index, base, away, other_maps, *refs):
    node, skeleton = refs[-2:]
    size = away.shape[1]
    both = base[...] + wide_dot(wide_left(away[...]), other_maps[index])
    skeleton[...] = both[:, size:]
    node[...] = both[:, :size]


def first_merge_kernel(base, away, other_maps, node, skeleton):
    half, size = node.shape
    both = base[...] + wide_dot(wide_left(away[:half, :]), other_maps[0])
    skeleton[...] = both[:, size:]
    node[...] = both[:, :size]


def carry_kernel(child, home, away, mine_maps, other_maps, next_maps, tail, carried, *climb):
    k_half, size = home.shape
    position = lax.axis_index("blk")
    mine = wide_dot(wide_left(home[...]), mine_maps[0])
    other = wide_dot(wide_left(away[away.shape[0] - k_half :, :]), other_maps[0])
    both = jnp.where(position == child[0], mine, 0.0) + jnp.where(position ^ 1 == child[0], other, 0.0)
    tail[...] = both[:, :size]
    carried[...] = both[:, size:]
    for out in climb:
        out[...] = wide_dot(wide_left(both[:, size:]), next_maps[0, :, size:])


def climb_kernel(index, carried, mine_maps, climb):
    size = carried.shape[1]
    climb[...] = wide_dot(wide_left(carried[...]), mine_maps[index, :, size:])


def relay_kernel(carried, far, out):
    out[0] = carried[...]
    out[1] = far[...]


def pair_kernel(index, home, away, mine_maps, other_maps, out):
    out[...] = wide_dot(wide_left(home[...]), mine_maps[index]) + wide_dot(
        wide_left(away[...]), other_maps[index]
    )


def top_kernel(index, tails, home, away, mine_maps, other_maps, top_mine, top_other, out):
    size = tails.shape[2]
    count = tails.shape[0]
    out[:count] = tails[...]
    both = wide_dot(wide_left(home[0]), mine_maps[index]) + wide_dot(
        wide_left(away[0]), other_maps[index]
    )
    out[count] = both[:, :size]
    both = wide_dot(wide_left(both[:, size:]), top_mine[0]) + wide_dot(
        wide_left(home[1] + away[1]), top_other[0]
    )
    out[count + 1] = both[:, :size]
    out[count + 2] = both[:, size:]


def last_merge_kernel(index, base, away, other_maps, tails, *refs):
    node, root = refs[-2:]
    half, size = away.shape
    both = base[...] + wide_dot(wide_left(away[...]), other_maps[index])
    root[:half, :] = both[:, size:]
    root[half:, :] = tails[tails.shape[0] - 1]
    node[...] = both[:, :size]


def maps_kernel(leaf_map, home, away, *refs):
    wide_maps, maps = refs[-2:]
    k_half, size = home.shape[1:]
    core = lax.axis_index("blk") & 1
    maps[:, :size] = leaf_map[...]
    for i in range(home.shape[0]):
        columns = slice((i + 1) * size, (i + 2) * size)
        maps[span(core, k_half), columns] = home[i]
        maps[span(1 - core, k_half), columns] = away[i]
    wide_maps[...] = wide_right(maps[...])


def affected(child, height):
    position = lax.axis_index("blk")
    below = lax.axis_index("level") > 0
    shared = [position >> t == child[0] >> t for t in range(height)]
    return [jnp.logical_and(below, same) for same in shared] + [below, below]


def targets(leaf_out, node_out, root_out, rows):
    nodes = [node_out.at[tier, rows] for tier in range(node_out.shape[0])]
    return [leaf_out.at[rows]] + nodes + [root_out.at[rows]]


def part_rows(part, half):
    core = lax.axis_index("blk") & 1
    return pl.ds(pl.multiple_of((core if part == 0 else 1 - core) * half, 8), half)


def early_kernel(height, child, solved, *refs):
    nodes, roots, refs = refs[: 2 * height], refs[2 * height : 2 * height + 2], refs[-4:]
    leaf_out, node_out, root_out, sems = refs
    half, _ = solved.shape[1:]
    late = affected(child, height)
    copies = []
    for part in range(2):
        outs = targets(leaf_out, node_out, root_out, part_rows(part, half))
        bases = [solved.at[part]] + [nodes[2 * tier + part] for tier in range(height)]
        bases += [roots[part].at[pl.ds(0, half)]]
        copies += [
            (late[i], pltpu.make_async_copy(base, out, sems.at[part, i]))
            for i, (base, out) in enumerate(zip(bases, outs))
        ]
    for act in ("start", "wait"):
        for skip, copy in copies:
            pl.when(jnp.logical_not(skip))(getattr(copy, act))


def final_kernel(fronts, height, child, solved, wide_maps, *refs):
    nodes, refs = refs[: 2 * height], refs[2 * height :]
    roots, refs = refs[: 2 * fronts], refs[2 * fronts + 3 :]
    leaf_out, node_out, root_out, root_maps, incoming, result, sems = refs
    core, level = lax.axis_index("blk") & 1, lax.axis_index("level")
    half, size = solved.shape[1:]
    k_half = root_maps.shape[1] // 2
    count = height + 2
    late = affected(child, height)
    for front in range(1, fronts):
        root_maps[front, span(core, k_half), :] = roots[2 * front][half:, :]
        root_maps[front, span(1 - core, k_half), :] = roots[2 * front + 1][half:, :]

    def both_rows(mask):
        return jnp.concatenate([roots[2 * mask][:half, :], roots[2 * mask + 1][:half, :]], axis=0)

    for here in range(1, fronts):

        @pl.when(level == here)
        def _():
            value = both_rows(here)
            for front in range(1, here):
                value = both_rows(here ^ front) + product(value, root_maps[here ^ front])
            incoming[...] = wide_left(value)

    step = half // 2
    copies = []
    for chunk in range(4):
        first = (core if chunk < 2 else 1 - core) * half + chunk % 2 * step
        outs = targets(leaf_out, node_out, root_out, pl.ds(pl.multiple_of(first, 8), step))
        copies.append(
            [
                pltpu.make_async_copy(result.at[chunk, i], out, sems.at[chunk, i])
                for i, out in enumerate(outs)
            ]
        )

    def update(first, last):
        for chunk in range(4):
            part, inner = chunk // 2, slice(chunk % 2 * step, (chunk % 2 + 1) * step)
            change = wide_dot(
                incoming[chunk * step : (chunk + 1) * step, :], wide_maps[:, first * size : last * size]
            )
            for i in range(first, last):
                if i == 0:
                    base = solved[part, inner, :]
                elif i <= height:
                    base = nodes[2 * (i - 1) + part][inner, :]
                else:
                    base = roots[part][inner, :]
                result[chunk, i] = base + change[:, (i - first) * size : (i + 1 - first) * size]
                copies[chunk][i].start()

    for i in range(height + 1):
        first = jnp.logical_and(late[i], jnp.logical_not(late[i - 1])) if i else late[0]
        pl.when(first)(functools.partial(update, i, count))
    for i, flag in enumerate(late):
        for chunk in range(4):
            pl.when(flag)(copies[chunk][i].wait)


def shards(
    right_sides,
    leaf_gen,
    leaf_inverse,
    leaf_lower,
    node_gen,
    node_inverse,
    node_lower,
    coupling,
    child_leaf,
):
    rows, leaf_size = right_sides.shape[1:]
    size = leaf_lower.shape[2]
    k_rows = coupling.shape[1]
    height = node_gen.shape[2]
    fronts = lax.axis_size("level")
    leaves = lax.axis_size("blk")
    half = rows // 2
    part = half + k_rows // 2
    smem = pl.BlockSpec(memory_space=pltpu.SMEM)
    vmem = pl.BlockSpec(memory_space=pltpu.VMEM)
    hbm = pl.BlockSpec(memory_space=pltpu.HBM)
    anywhere = pl.BlockSpec(memory_space=pl.ANY)
    array = lambda *shape: jax.ShapeDtypeStruct(shape, f32)

    def blk_swap(value, mask):
        return lax.ppermute(value, "blk", [(i, i ^ mask) for i in range(leaves)])

    def level_swap(value, mask):
        return lax.ppermute(value, "level", [(i, i ^ mask) for i in range(fronts)])

    k_half = k_rows // 2
    node_params = (node_gen[0, 0], node_inverse[0, 0], node_lower[0, 0])
    away, leaf_solve_map, leaf_skeleton, right_here, coupling_here, *first_params = call(
        leaf_kernel,
        (
            array(part, size),
            array(leaf_size, size),
            jax.ShapeDtypeStruct((3 * leaf_size, size), bf16),
            array(2, half, leaf_size),
            array(k_rows, leaf_size),
            *(array(*value.shape[1:]) for value in node_params),
        ),
        tuple(
            pltpu.with_memory_space_constraint(value, pltpu.HBM)
            for value in (
                right_sides[0],
                leaf_gen[0],
                leaf_inverse[0],
                leaf_lower[0],
                coupling[0],
                *node_params,
            )
        ),
        6 * (part + leaf_size) * leaf_size * size,
        in_specs=[hbm] * 8,
        scratch_shapes=[
            pltpu.VMEM((leaf_size, leaf_size), f32),
            pltpu.VMEM((size, size), f32),
            pltpu.VMEM((size, size), f32),
            pltpu.SemaphoreType.DMA((9,)),
        ],
    )
    merge_flops = 6 * half * 2 * size * size
    fold_flops = 6 * 4 * size * size * size
    wide = lambda count: jax.ShapeDtypeStruct((count, 3 * size, 2 * size), bf16)
    both = pltpu.VMEM((2 * size, 2 * size), f32)
    first_mine, first_other, base, home = call(
        first_fold_kernel,
        (wide(1), wide(1), array(half, 2 * size), array(k_half, size)),
        (*first_params, right_here, coupling_here, leaf_skeleton),
        fold_flops + 6 * part * (leaf_size + 2 * size) * size,
        scratch_shapes=[both],
    )
    *node_params, away = lax.optimization_barrier((*node_params, away))
    away = blk_swap(away, 1)
    node, skeleton = call(
        first_merge_kernel,
        (array(half, size), array(half, size)),
        (base, away, first_other),
        merge_flops,
    )
    nodes, away_first = [node], away

    def folds(first, last, *after):
        return call(
            functools.partial(fold_kernel, first),
            (wide(last - first),) * 2,
            (*node_params, *after),
            (last - first) * fold_flops,
            in_specs=[vmem] * 3 + [anywhere] * len(after),
            scratch_shapes=[both],
        )

    child_leaf, skeleton = lax.optimization_barrier((child_leaf, skeleton))
    for tier in range(1, height):
        away = blk_swap(skeleton, 1 << tier)
        after = ()
        if tier == 1:
            mine_maps, other_maps = folds(1, height - 1)
            tail, carried, *climb = call(
                carry_kernel,
                (array(k_half, size),) * (3 if height == 3 else 2),
                (child_leaf, home, away_first, first_mine, first_other, mine_maps),
                6 * k_half * 5 * size * size,
                in_specs=[smem] + [vmem] * 5,
            )
            tails = [tail]
        if tier < height - 2:
            pair = call(
                functools.partial(pair_kernel, tier - 1),
                array(k_half, 2 * size),
                (carried, blk_swap(carried, 1 << tier), mine_maps, other_maps),
                6 * k_half * 4 * size * size,
            )
            tails.append(pair[:, :size])
            carried = pair[:, size:]
        if tier == height - 2:
            if not climb:
                climb = [
                    call(
                        functools.partial(climb_kernel, tier - 1),
                        array(k_half, size),
                        (carried, mine_maps),
                        6 * k_half * size * size,
                    )
                ]
            far = blk_swap(climb[0], 2 << tier)
            after = (climb[0],)
        if tier == height - 1:
            top_mine, top_other = folds(height - 1, height)
            relay = call(relay_kernel, array(2, k_half, size), (carried, far), k_half * size)
            relayed = blk_swap(relay, 1 << (tier - 1))
            tails = call(
                functools.partial(top_kernel, tier - 2),
                array(height + 1, k_half, size),
                (jnp.stack(tails), relay, relayed, mine_maps, other_maps, top_mine, top_other),
                6 * k_half * 6 * size * size,
            )
            solved, leaf_map = call(
                functools.partial(leaf_solve_kernel, height - 2),
                (array(2, half, size), array(k_rows, size)),
                (*early, *leaf_args),
                6 * (rows + k_rows) * leaf_size * size,
                in_specs=[vmem] * 2 + [smem] + [vmem] * 3,
            )
            after = (solved,)
        last = tier == height - 1
        if last:
            mine_maps, other_maps = top_mine, top_other
        index = 0 if last else tier - 1
        base = call(
            functools.partial(base_kernel, index),
            array(half, 2 * size),
            (skeleton, mine_maps),
            merge_flops,
        )
        leaf_args = (child_leaf, right_here, coupling_here, leaf_solve_map)
        kernel = functools.partial(last_merge_kernel if last else merge_kernel, index)
        args, specs = (base, away, other_maps), [vmem] * 3
        shapes = (array(half, size), array(part if last else half, size))
        if last:
            args, specs = args + (tails,), specs + [vmem]
        if tier == height - 2:
            kernel = functools.partial(late_merge_kernel, index, height - 2)
            args, specs = args + leaf_args, specs + [smem] + [vmem] * 3
            shapes += (array(2, half, size), array(k_rows, size))
        node, skeleton, *early = call(
            kernel, shapes, args + after, merge_flops, in_specs=specs + [anywhere] * len(after)
        )
        nodes.append(node)
    received = []
    for mask in range(1, fronts):
        received.append(level_swap(skeleton, mask))
    roots = [skeleton, blk_swap(skeleton, 1)]
    for value in received:
        roots += [value, blk_swap(value, 1)]
    pairs = []
    for value in nodes:
        pairs += [value, blk_swap(value, 1)]
    shapes = (array(rows, size), array(height, rows, size), array(rows, size))
    early = call(
        functools.partial(early_kernel, height),
        shapes,
        (child_leaf, solved, *pairs, *roots[:2]),
        rows * size,
        in_specs=[smem] + [vmem] * (len(pairs) + 3),
        out_specs=(hbm,) * 3,
        scratch_shapes=[pltpu.SemaphoreType.DMA((2, height + 2))],
    )
    wide_maps = call(
        maps_kernel,
        jax.ShapeDtypeStruct((3 * k_rows, size * (height + 2)), bf16),
        (leaf_map, tails, blk_swap(tails, 1)),
        k_rows * size * (height + 2) * 4,
        scratch_shapes=[pltpu.VMEM((k_rows, size * (height + 2)), f32)],
    )
    args = (child_leaf, solved, wide_maps, *pairs, *roots)
    leaf_out, node_out, root_out = call(
        functools.partial(final_kernel, fronts, height),
        shapes,
        (*args, *early),
        6 * rows * size * size * (height + 2),
        in_specs=[smem] + [vmem] * (len(args) - 1) + [hbm] * 3,
        out_specs=(hbm,) * 3,
        aliases={len(args) + i: i for i in range(3)},
        scratch_shapes=[
            pltpu.VMEM((fronts, k_rows, size), f32),
            pltpu.VMEM((rows, 3 * size), bf16),
            pltpu.VMEM((4, height + 2, rows // 4, size), f32),
            pltpu.SemaphoreType.DMA((4, height + 2)),
        ],
    )
    return (leaf_out[None], node_out[None, None], root_out[None])


def solution(mesh):
    in_specs = (
        P("level", None, "blk"),
        P("level", "blk", None),
        P("level", "blk", None),
        P("level", "blk", None),
        P("level", "blk", None, None, None),
        P("level", "blk", None, None, None),
        P("level", "blk", None, None, None),
        P("level", None, None),
        P("level"),
    )
    out_specs = (
        P("level", None, "blk"),
        P("level", "blk", None, None, None),
        P("level", None, None),
    )

    return jax.shard_map(shards, mesh=mesh, in_specs=in_specs, out_specs=out_specs, check_vma=False)
```

```python
import functools

import jax
import jax.numpy as jnp
from jax import lax
from jax.experimental import pallas as pl
from jax.experimental.pallas import tpu as pltpu
from jax.sharding import PartitionSpec as P


f32 = jnp.float32
bf16 = jnp.bfloat16
VMEM_LIMIT = 12 << 20


def split(value):
    high = value.astype(bf16)
    return high, (value - high.astype(f32)).astype(bf16)


def wide_left(value):
    high, low = split(value)
    return jnp.concatenate([high, low, high], axis=1)


def wide_right(value):
    high, low = split(value)
    return jnp.concatenate([high, high, low], axis=0)


def wide_dot(left, right):
    return jnp.dot(left, right, preferred_element_type=f32)


def product(left, right):
    return wide_dot(wide_left(left), wide_right(right))


def call(kernel, out_shape, args, flops, in_specs=None, out_specs=None, scratch_shapes=(), aliases={}):
    size = lambda s: s.size * s.dtype.itemsize
    vmem = pl.BlockSpec(memory_space=pltpu.VMEM)
    moved = sum(size(a) for a in args) + sum(size(o) for o in jax.tree.leaves(out_shape))
    return pl.pallas_call(
        kernel,
        out_shape=out_shape,
        in_specs=in_specs or [vmem] * len(args),
        out_specs=out_specs or jax.tree.map(lambda _: vmem, out_shape),
        scratch_shapes=scratch_shapes,
        input_output_aliases=aliases,
        compiler_params=pltpu.CompilerParams(vmem_limit_bytes=VMEM_LIMIT),
        cost_estimate=pl.CostEstimate(flops=flops, bytes_accessed=moved, transcendentals=0),
    )(*args)


def span(index, length):
    return pl.ds(pl.multiple_of(index * length, 8), length)


def leaf_kernel(right, generator, inverse, lower, coupling, *refs):
    later, (away, solve_map, skeleton_map), refs = refs[:3], refs[3:6], refs[6:]
    (right_here, coupling_here, *later_here), refs = refs[:5], refs[5:]
    generator_here, inverse_here, lower_here, sems = refs
    core = lax.axis_index("blk") & 1
    half, k_half = right.shape[0] // 2, coupling.shape[0] // 2
    size = inverse.shape[0]
    copies = [
        pltpu.make_async_copy(source, target, sems.at[i])
        for i, (source, target) in enumerate(
            [
                (generator, generator_here),
                (inverse, inverse_here),
                (lower, lower_here),
                (right.at[span(1 - core, half)], right_here.at[0]),
                (coupling, coupling_here),
                (right.at[span(core, half)], right_here.at[1]),
                *((source.at[0], target) for source, target in zip(later, later_here)),
            ]
        )
    ]
    for copy in copies[:5]:
        copy.start()
    for copy in copies[:2]:
        copy.wait()
    for copy in copies[5:]:
        copy.start()
    solved = product(generator_here[:, :size], inverse_here[...])
    solve_map[...] = solved
    copies[2].wait()
    parts = wide_right(generator_here[:, size:] - product(solved, lower_here[...]))
    skeleton_map[...] = parts
    copies[3].wait()
    away[:half, :] = wide_dot(wide_left(right_here[0]), parts)
    copies[4].wait()
    away[half:, :] = wide_dot(wide_left(coupling_here[span(1 - core, k_half), :]), parts)
    for copy in copies[5:]:
        copy.wait()


def leaf_solve(child, right, coupling, solve_map, solved, leaf_map):
    parts = wide_right(solve_map[...])
    for part in range(2):
        solved[part] = wide_dot(wide_left(right[1 - part]), parts)
    on_target = lax.axis_index("blk") == child[0]
    leaf_map[...] = jnp.where(on_target, wide_dot(wide_left(coupling[...]), parts), 0.0)


def leaf_solve_kernel(bit, solved_early, map_early, *refs):
    solved, leaf_map = refs[-2:]
    early = (lax.axis_index("blk") >> bit) & 1

    @pl.when(early == 1)
    def _():
        solved[...] = solved_early[...]
        leaf_map[...] = map_early[...]

    @pl.when(early == 0)
    def _():
        leaf_solve(*refs)


def fold(tier, generator, inverse, lower, both):
    size = inverse.shape[0]
    solve_map = product(generator[:, :size], inverse)
    both[:, :size] = solve_map
    both[:, size:] = generator[:, size:] - product(solve_map, lower)
    upper = (lax.axis_index("blk") >> tier) & 1
    return wide_right(both[span(upper, size), :]), wide_right(both[span(1 - upper, size), :])


def first_fold_kernel(
    generator, inverse, lower, right, coupling, skeleton_map, mine_maps, other_maps, base, home, both
):
    core = lax.axis_index("blk") & 1
    k_half = home.shape[0]
    value = wide_dot(wide_left(right[1]), skeleton_map[...])
    home[...] = wide_dot(wide_left(coupling[span(core, k_half), :]), skeleton_map[...])
    mine_maps[0], other_maps[0] = fold(0, generator[...], inverse[...], lower[...], both)
    base[...] = wide_dot(wide_left(value), mine_maps[0])


def fold_kernel(first, generator, inverse, lower, *refs):
    mine_maps, other_maps, both = refs[-3:]
    for i in range(mine_maps.shape[0]):
        tier = first + i
        mine_maps[i], other_maps[i] = fold(tier, generator[tier], inverse[tier], lower[tier], both)


def base_kernel(index, home, mine_maps, base):
    base[...] = wide_dot(wide_left(home[...]), mine_maps[index])


def late_merge_kernel(index, bit, base, away, other_maps, child, right, coupling, solve_map, *refs):
    node, skeleton, solved, leaf_map = refs[-4:]
    merge_kernel(index, base, away, other_maps, node, skeleton)

    @pl.when((lax.axis_index("blk") >> bit) & 1 == 1)
    def _():
        leaf_solve(child, right, coupling, solve_map, solved, leaf_map)


def merge_kernel(index, base, away, other_maps, *refs):
    node, skeleton = refs[-2:]
    size = away.shape[1]
    both = base[...] + wide_dot(wide_left(away[...]), other_maps[index])
    skeleton[...] = both[:, size:]
    node[...] = both[:, :size]


def first_merge_kernel(base, away, other_maps, node, skeleton):
    half, size = node.shape
    both = base[...] + wide_dot(wide_left(away[:half, :]), other_maps[0])
    skeleton[...] = both[:, size:]
    node[...] = both[:, :size]


def carry_kernel(child, home, away, mine_maps, other_maps, next_maps, tail, carried, *climb):
    k_half, size = home.shape
    position = lax.axis_index("blk")
    mine = wide_dot(wide_left(home[...]), mine_maps[0])
    other = wide_dot(wide_left(away[away.shape[0] - k_half :, :]), other_maps[0])
    both = jnp.where(position == child[0], mine, 0.0) + jnp.where(position ^ 1 == child[0], other, 0.0)
    tail[...] = both[:, :size]
    carried[...] = both[:, size:]
    for out in climb:
        out[...] = wide_dot(wide_left(both[:, size:]), next_maps[0, :, size:])


def climb_kernel(index, carried, mine_maps, climb):
    size = carried.shape[1]
    climb[...] = wide_dot(wide_left(carried[...]), mine_maps[index, :, size:])


def relay_kernel(carried, far, out):
    out[0] = carried[...]
    out[1] = far[...]


def pair_kernel(index, home, away, mine_maps, other_maps, out):
    out[...] = wide_dot(wide_left(home[...]), mine_maps[index]) + wide_dot(
        wide_left(away[...]), other_maps[index]
    )


def top_kernel(index, tails, home, away, mine_maps, other_maps, top_mine, top_other, out):
    size = tails.shape[2]
    count = tails.shape[0]
    out[:count] = tails[...]
    both = wide_dot(wide_left(home[0]), mine_maps[index]) + wide_dot(
        wide_left(away[0]), other_maps[index]
    )
    out[count] = both[:, :size]
    both = wide_dot(wide_left(both[:, size:]), top_mine[0]) + wide_dot(
        wide_left(home[1] + away[1]), top_other[0]
    )
    out[count + 1] = both[:, :size]
    out[count + 2] = both[:, size:]


def last_merge_kernel(index, base, away, other_maps, tails, *refs):
    node, root = refs[-2:]
    half, size = away.shape
    both = base[...] + wide_dot(wide_left(away[...]), other_maps[index])
    root[:half, :] = both[:, size:]
    root[half:, :] = tails[tails.shape[0] - 1]
    node[...] = both[:, :size]


def maps_kernel(leaf_map, home, away, *refs):
    wide_maps, maps = refs[-2:]
    k_half, size = home.shape[1:]
    core = lax.axis_index("blk") & 1
    maps[:, :size] = leaf_map[...]
    for i in range(home.shape[0]):
        columns = slice((i + 1) * size, (i + 2) * size)
        maps[span(core, k_half), columns] = home[i]
        maps[span(1 - core, k_half), columns] = away[i]
    wide_maps[...] = wide_right(maps[...])


def affected(child, height):
    position = lax.axis_index("blk")
    below = lax.axis_index("level") > 0
    shared = [position >> t == child[0] >> t for t in range(height)]
    return [jnp.logical_and(below, same) for same in shared] + [below, below]


def targets(leaf_out, node_out, root_out, rows):
    nodes = [node_out.at[tier, rows] for tier in range(node_out.shape[0])]
    return [leaf_out.at[rows]] + nodes + [root_out.at[rows]]


def part_rows(part, half):
    core = lax.axis_index("blk") & 1
    return pl.ds(pl.multiple_of((core if part == 0 else 1 - core) * half, 8), half)


def early_kernel(height, child, solved, *refs):
    nodes, roots, refs = refs[: 2 * height], refs[2 * height : 2 * height + 2], refs[-4:]
    leaf_out, node_out, root_out, sems = refs
    half, _ = solved.shape[1:]
    late = affected(child, height)
    copies = []
    for part in range(2):
        outs = targets(leaf_out, node_out, root_out, part_rows(part, half))
        bases = [solved.at[part]] + [nodes[2 * tier + part] for tier in range(height)]
        bases += [roots[part].at[pl.ds(0, half)]]
        copies += [
            (late[i], pltpu.make_async_copy(base, out, sems.at[part, i]))
            for i, (base, out) in enumerate(zip(bases, outs))
        ]
    for act in ("start", "wait"):
        for skip, copy in copies:
            pl.when(jnp.logical_not(skip))(getattr(copy, act))


def final_kernel(fronts, height, child, solved, wide_maps, *refs):
    nodes, refs = refs[: 2 * height], refs[2 * height :]
    roots, refs = refs[: 2 * fronts], refs[2 * fronts + 3 :]
    leaf_out, node_out, root_out, root_maps, incoming, result, sems = refs
    core, level = lax.axis_index("blk") & 1, lax.axis_index("level")
    half, size = solved.shape[1:]
    k_half = root_maps.shape[1] // 2
    count = height + 2
    late = affected(child, height)
    for front in range(1, fronts):
        root_maps[front, span(core, k_half), :] = roots[2 * front][half:, :]
        root_maps[front, span(1 - core, k_half), :] = roots[2 * front + 1][half:, :]

    def both_rows(mask):
        return jnp.concatenate([roots[2 * mask][:half, :], roots[2 * mask + 1][:half, :]], axis=0)

    for here in range(1, fronts):

        @pl.when(level == here)
        def _():
            value = both_rows(here)
            for front in range(1, here):
                value = both_rows(here ^ front) + product(value, root_maps[here ^ front])
            incoming[...] = wide_left(value)

    step = half // 2
    copies = []
    for chunk in range(4):
        first = (core if chunk < 2 else 1 - core) * half + chunk % 2 * step
        outs = targets(leaf_out, node_out, root_out, pl.ds(pl.multiple_of(first, 8), step))
        copies.append(
            [
                pltpu.make_async_copy(result.at[chunk, i], out, sems.at[chunk, i])
                for i, out in enumerate(outs)
            ]
        )

    def update(first, last):
        for chunk in range(4):
            part, inner = chunk // 2, slice(chunk % 2 * step, (chunk % 2 + 1) * step)
            change = wide_dot(
                incoming[chunk * step : (chunk + 1) * step, :], wide_maps[:, first * size : last * size]
            )
            for i in range(first, last):
                if i == 0:
                    base = solved[part, inner, :]
                elif i <= height:
                    base = nodes[2 * (i - 1) + part][inner, :]
                else:
                    base = roots[part][inner, :]
                result[chunk, i] = base + change[:, (i - first) * size : (i + 1 - first) * size]
                copies[chunk][i].start()

    for i in range(height + 1):
        first = jnp.logical_and(late[i], jnp.logical_not(late[i - 1])) if i else late[0]
        pl.when(first)(functools.partial(update, i, count))
    for i, flag in enumerate(late):
        for chunk in range(4):
            pl.when(flag)(copies[chunk][i].wait)


def shards(
    right_sides,
    leaf_gen,
    leaf_inverse,
    leaf_lower,
    node_gen,
    node_inverse,
    node_lower,
    coupling,
    child_leaf,
):
    rows, leaf_size = right_sides.shape[1:]
    size = leaf_lower.shape[2]
    k_rows = coupling.shape[1]
    height = node_gen.shape[2]
    fronts = lax.axis_size("level")
    leaves = lax.axis_size("blk")
    half = rows // 2
    part = half + k_rows // 2
    smem = pl.BlockSpec(memory_space=pltpu.SMEM)
    vmem = pl.BlockSpec(memory_space=pltpu.VMEM)
    hbm = pl.BlockSpec(memory_space=pltpu.HBM)
    anywhere = pl.BlockSpec(memory_space=pl.ANY)
    array = lambda *shape: jax.ShapeDtypeStruct(shape, f32)

    def blk_swap(value, mask):
        return lax.ppermute(value, "blk", [(i, i ^ mask) for i in range(leaves)])

    def level_swap(value, mask):
        return lax.ppermute(value, "level", [(i, i ^ mask) for i in range(fronts)])

    k_half = k_rows // 2
    node_params = (node_gen[0, 0], node_inverse[0, 0], node_lower[0, 0])
    away, leaf_solve_map, leaf_skeleton, right_here, coupling_here, *first_params = call(
        leaf_kernel,
        (
            array(part, size),
            array(leaf_size, size),
            jax.ShapeDtypeStruct((3 * leaf_size, size), bf16),
            array(2, half, leaf_size),
            array(k_rows, leaf_size),
            *(array(*value.shape[1:]) for value in node_params),
        ),
        tuple(
            pltpu.with_memory_space_constraint(value, pltpu.HBM)
            for value in (
                right_sides[0],
                leaf_gen[0],
                leaf_inverse[0],
                leaf_lower[0],
                coupling[0],
                *node_params,
            )
        ),
        6 * (part + leaf_size) * leaf_size * size,
        in_specs=[hbm] * 8,
        scratch_shapes=[
            pltpu.VMEM((leaf_size, leaf_size), f32),
            pltpu.VMEM((size, size), f32),
            pltpu.VMEM((size, size), f32),
            pltpu.SemaphoreType.DMA((9,)),
        ],
    )
    merge_flops = 6 * half * 2 * size * size
    fold_flops = 6 * 4 * size * size * size
    wide = lambda count: jax.ShapeDtypeStruct((count, 3 * size, 2 * size), bf16)
    both = pltpu.VMEM((2 * size, 2 * size), f32)
    first_mine, first_other, base, home = call(
        first_fold_kernel,
        (wide(1), wide(1), array(half, 2 * size), array(k_half, size)),
        (*first_params, right_here, coupling_here, leaf_skeleton),
        fold_flops + 6 * part * (leaf_size + 2 * size) * size,
        scratch_shapes=[both],
    )
    *node_params, away = lax.optimization_barrier((*node_params, away))
    away = blk_swap(away, 1)
    node, skeleton = call(
        first_merge_kernel,
        (array(half, size), array(half, size)),
        (base, away, first_other),
        merge_flops,
    )
    nodes, away_first = [node], away

    def folds(first, last, *after):
        return call(
            functools.partial(fold_kernel, first),
            (wide(last - first),) * 2,
            (*node_params, *after),
            (last - first) * fold_flops,
            in_specs=[vmem] * 3 + [anywhere] * len(after),
            scratch_shapes=[both],
        )

    child_leaf, skeleton = lax.optimization_barrier((child_leaf, skeleton))
    for tier in range(1, height):
        away = blk_swap(skeleton, 1 << tier)
        after = ()
        if tier == 1:
            mine_maps, other_maps = folds(1, height - 1)
            tail, carried, *climb = call(
                carry_kernel,
                (array(k_half, size),) * (3 if height == 3 else 2),
                (child_leaf, home, away_first, first_mine, first_other, mine_maps),
                6 * k_half * 5 * size * size,
                in_specs=[smem] + [vmem] * 5,
            )
            tails = [tail]
        if tier < height - 2:
            pair = call(
                functools.partial(pair_kernel, tier - 1),
                array(k_half, 2 * size),
                (carried, blk_swap(carried, 1 << tier), mine_maps, other_maps),
                6 * k_half * 4 * size * size,
            )
            tails.append(pair[:, :size])
            carried = pair[:, size:]
        if tier == height - 2:
            if not climb:
                climb = [
                    call(
                        functools.partial(climb_kernel, tier - 1),
                        array(k_half, size),
                        (carried, mine_maps),
                        6 * k_half * size * size,
                    )
                ]
            far = blk_swap(climb[0], 2 << tier)
            after = (climb[0],)
        if tier == height - 1:
            top_mine, top_other = folds(height - 1, height)
            relay = call(relay_kernel, array(2, k_half, size), (carried, far), k_half * size)
            relayed = blk_swap(relay, 1 << (tier - 1))
            tails = call(
                functools.partial(top_kernel, tier - 2),
                array(height + 1, k_half, size),
                (jnp.stack(tails), relay, relayed, mine_maps, other_maps, top_mine, top_other),
                6 * k_half * 6 * size * size,
            )
            solved, leaf_map = call(
                functools.partial(leaf_solve_kernel, height - 2),
                (array(2, half, size), array(k_rows, size)),
                (*early, *leaf_args),
                6 * (rows + k_rows) * leaf_size * size,
                in_specs=[vmem] * 2 + [smem] + [vmem] * 3,
            )
            after = (solved,)
        last = tier == height - 1
        if last:
            mine_maps, other_maps = top_mine, top_other
        index = 0 if last else tier - 1
        base = call(
            functools.partial(base_kernel, index),
            array(half, 2 * size),
            (skeleton, mine_maps),
            merge_flops,
        )
        leaf_args = (child_leaf, right_here, coupling_here, leaf_solve_map)
        kernel = functools.partial(last_merge_kernel if last else merge_kernel, index)
        args, specs = (base, away, other_maps), [vmem] * 3
        shapes = (array(half, size), array(part if last else half, size))
        if last:
            args, specs = args + (tails,), specs + [vmem]
        if tier == height - 2:
            kernel = functools.partial(late_merge_kernel, index, height - 2)
            args, specs = args + leaf_args, specs + [smem] + [vmem] * 3
            shapes += (array(2, half, size), array(k_rows, size))
        node, skeleton, *early = call(
            kernel, shapes, args + after, merge_flops, in_specs=specs + [anywhere] * len(after)
        )
        nodes.append(node)
    received = [level_swap(skeleton, mask) for mask in range(1, fronts)]
    roots = [skeleton, blk_swap(skeleton, 1)]
    for value in received:
        roots += [value, blk_swap(value, 1)]
    pairs = []
    for value in nodes:
        pairs += [value, blk_swap(value, 1)]
    shapes = (array(rows, size), array(height, rows, size), array(rows, size))
    early = call(
        functools.partial(early_kernel, height),
        shapes,
        (child_leaf, solved, *pairs, *roots[:2]),
        rows * size,
        in_specs=[smem] + [vmem] * (len(pairs) + 3),
        out_specs=(hbm,) * 3,
        scratch_shapes=[pltpu.SemaphoreType.DMA((2, height + 2))],
    )
    wide_maps = call(
        maps_kernel,
        jax.ShapeDtypeStruct((3 * k_rows, size * (height + 2)), bf16),
        (leaf_map, tails, blk_swap(tails, 1)),
        k_rows * size * (height + 2) * 4,
        scratch_shapes=[pltpu.VMEM((k_rows, size * (height + 2)), f32)],
    )
    args = (child_leaf, solved, wide_maps, *pairs, *roots)
    leaf_out, node_out, root_out = call(
        functools.partial(final_kernel, fronts, height),
        shapes,
        (*args, *early),
        6 * rows * size * size * (height + 2),
        in_specs=[smem] + [vmem] * (len(args) - 1) + [hbm] * 3,
        out_specs=(hbm,) * 3,
        aliases={len(args) + i: i for i in range(3)},
        scratch_shapes=[
            pltpu.VMEM((fronts, k_rows, size), f32),
            pltpu.VMEM((rows, 3 * size), bf16),
            pltpu.VMEM((4, height + 2, rows // 4, size), f32),
            pltpu.SemaphoreType.DMA((4, height + 2)),
        ],
    )
    return (leaf_out[None], node_out[None, None], root_out[None])


def solution(mesh):
    in_specs = (
        P("level", None, "blk"),
        P("level", "blk", None),
        P("level", "blk", None),
        P("level", "blk", None),
        P("level", "blk", None, None, None),
        P("level", "blk", None, None, None),
        P("level", "blk", None, None, None),
        P("level", None, None),
        P("level"),
    )
    out_specs = (
        P("level", None, "blk"),
        P("level", "blk", None, None, None),
        P("level", None, None),
    )

    return jax.shard_map(shards, mesh=mesh, in_specs=in_specs, out_specs=out_specs, check_vma=False)
```

```python
import functools

import jax
import jax.numpy as jnp
from jax import lax
from jax.experimental import pallas as pl
from jax.experimental.pallas import tpu as pltpu
from jax.sharding import PartitionSpec as P


f32 = jnp.float32
bf16 = jnp.bfloat16
VMEM_LIMIT = 12 << 20


def split(value):
    high = value.astype(bf16)
    return high, (value - high.astype(f32)).astype(bf16)


def wide_left(value):
    high, low = split(value)
    return jnp.concatenate([high, low, high], axis=1)


def wide_right(value):
    high, low = split(value)
    return jnp.concatenate([high, high, low], axis=0)


def wide_dot(left, right):
    return jnp.dot(left, right, preferred_element_type=f32)


def product(left, right):
    return wide_dot(wide_left(left), wide_right(right))


def call(kernel, out_shape, args, flops, in_specs=None, out_specs=None, scratch_shapes=(), aliases={}):
    size = lambda s: s.size * s.dtype.itemsize
    vmem = pl.BlockSpec(memory_space=pltpu.VMEM)
    moved = sum(size(a) for a in args) + sum(size(o) for o in jax.tree.leaves(out_shape))
    return pl.pallas_call(
        kernel,
        out_shape=out_shape,
        in_specs=in_specs or [vmem] * len(args),
        out_specs=out_specs or jax.tree.map(lambda _: vmem, out_shape),
        scratch_shapes=scratch_shapes,
        input_output_aliases=aliases,
        compiler_params=pltpu.CompilerParams(vmem_limit_bytes=VMEM_LIMIT),
        cost_estimate=pl.CostEstimate(flops=flops, bytes_accessed=moved, transcendentals=0),
    )(*args)


def span(index, length):
    return pl.ds(pl.multiple_of(index * length, 8), length)


def leaf_kernel(right, generator, inverse, lower, coupling, *refs):
    later, (away, solve_map, skeleton_map), refs = refs[:3], refs[3:6], refs[6:]
    (right_here, coupling_here, *later_here), refs = refs[:5], refs[5:]
    generator_here, inverse_here, lower_here, sems = refs
    core = lax.axis_index("blk") & 1
    half, k_half = right.shape[0] // 2, coupling.shape[0] // 2
    size = inverse.shape[0]
    copies = [
        pltpu.make_async_copy(source, target, sems.at[i])
        for i, (source, target) in enumerate(
            [
                (generator, generator_here),
                (inverse, inverse_here),
                (lower, lower_here),
                (right.at[span(1 - core, half)], right_here.at[0]),
                (coupling, coupling_here),
                (right.at[span(core, half)], right_here.at[1]),
                *((source.at[0], target) for source, target in zip(later, later_here)),
            ]
        )
    ]
    for copy in copies:
        copy.start()
    for copy in copies[:2]:
        copy.wait()
    solved = product(generator_here[:, :size], inverse_here[...])
    solve_map[...] = solved
    copies[2].wait()
    parts = wide_right(generator_here[:, size:] - product(solved, lower_here[...]))
    skeleton_map[...] = parts
    copies[3].wait()
    away[:half, :] = wide_dot(wide_left(right_here[0]), parts)
    copies[4].wait()
    away[half:, :] = wide_dot(wide_left(coupling_here[span(1 - core, k_half), :]), parts)
    for copy in copies[5:]:
        copy.wait()


def leaf_solve(child, right, coupling, solve_map, solved, leaf_map):
    parts = wide_right(solve_map[...])
    for part in range(2):
        solved[part] = wide_dot(wide_left(right[1 - part]), parts)
    on_target = lax.axis_index("blk") == child[0]
    leaf_map[...] = jnp.where(on_target, wide_dot(wide_left(coupling[...]), parts), 0.0)


def leaf_solve_kernel(bit, solved_early, map_early, *refs):
    solved, leaf_map = refs[-2:]
    early = ((lax.axis_index("blk") >> bit) & 3) == 3

    @pl.when(early)
    def _():
        solved[...] = solved_early[...]
        leaf_map[...] = map_early[...]

    @pl.when(jnp.logical_not(early))
    def _():
        leaf_solve(*refs)


def fold(tier, generator, inverse, lower, both):
    size = inverse.shape[0]
    solve_map = product(generator[:, :size], inverse)
    both[:, :size] = solve_map
    both[:, size:] = generator[:, size:] - product(solve_map, lower)
    upper = (lax.axis_index("blk") >> tier) & 1
    return wide_right(both[span(upper, size), :]), wide_right(both[span(1 - upper, size), :])


def first_fold_kernel(
    generator, inverse, lower, right, coupling, skeleton_map, mine_maps, other_maps, base, home, both
):
    core = lax.axis_index("blk") & 1
    k_half = home.shape[0]
    value = wide_dot(wide_left(right[1]), skeleton_map[...])
    home[...] = wide_dot(wide_left(coupling[span(core, k_half), :]), skeleton_map[...])
    mine_maps[0], other_maps[0] = fold(0, generator[...], inverse[...], lower[...], both)
    base[...] = wide_dot(wide_left(value), mine_maps[0])


def fold_kernel(first, generator, inverse, lower, *refs):
    mine_maps, other_maps, both = refs[-3:]
    for i in range(mine_maps.shape[0]):
        tier = first + i
        mine_maps[i], other_maps[i] = fold(tier, generator[tier], inverse[tier], lower[tier], both)


def base_kernel(index, home, mine_maps, base):
    base[...] = wide_dot(wide_left(home[...]), mine_maps[index])


def late_merge_kernel(index, bit, base, away, other_maps, child, right, coupling, solve_map, *refs):
    node, skeleton, solved, leaf_map = refs[-4:]
    merge_kernel(index, base, away, other_maps, node, skeleton)

    @pl.when(((lax.axis_index("blk") >> bit) & 3) == 3)
    def _():
        leaf_solve(child, right, coupling, solve_map, solved, leaf_map)


def merge_kernel(index, base, away, other_maps, *refs):
    node, skeleton = refs[-2:]
    size = away.shape[1]
    both = base[...] + wide_dot(wide_left(away[...]), other_maps[index])
    skeleton[...] = both[:, size:]
    node[...] = both[:, :size]


def first_merge_kernel(base, away, other_maps, node, skeleton):
    half, size = node.shape
    both = base[...] + wide_dot(wide_left(away[:half, :]), other_maps[0])
    skeleton[...] = both[:, size:]
    node[...] = both[:, :size]


def carry_kernel(child, home, away, mine_maps, other_maps, next_maps, tail, carried, *climb):
    k_half, size = home.shape
    position = lax.axis_index("blk")
    mine = wide_dot(wide_left(home[...]), mine_maps[0])
    other = wide_dot(wide_left(away[away.shape[0] - k_half :, :]), other_maps[0])
    both = jnp.where(position == child[0], mine, 0.0) + jnp.where(position ^ 1 == child[0], other, 0.0)
    tail[...] = both[:, :size]
    carried[...] = both[:, size:]
    for out in climb:
        out[...] = wide_dot(wide_left(both[:, size:]), next_maps[0, :, size:])


def climb_kernel(index, carried, mine_maps, climb):
    size = carried.shape[1]
    climb[...] = wide_dot(wide_left(carried[...]), mine_maps[index, :, size:])


def relay_kernel(carried, far, out):
    out[0] = carried[...]
    out[1] = far[...]


def pair_kernel(index, home, away, mine_maps, other_maps, out):
    out[...] = wide_dot(wide_left(home[...]), mine_maps[index]) + wide_dot(
        wide_left(away[...]), other_maps[index]
    )


def top_kernel(index, tails, home, away, mine_maps, other_maps, top_mine, top_other, out):
    size = tails.shape[2]
    count = tails.shape[0]
    out[:count] = tails[...]
    both = wide_dot(wide_left(home[0]), mine_maps[index]) + wide_dot(
        wide_left(away[0]), other_maps[index]
    )
    out[count] = both[:, :size]
    both = wide_dot(wide_left(both[:, size:]), top_mine[0]) + wide_dot(
        wide_left(home[1] + away[1]), top_other[0]
    )
    out[count + 1] = both[:, :size]
    out[count + 2] = both[:, size:]


def last_merge_kernel(index, base, away, other_maps, tails, *refs):
    node, root = refs[-2:]
    half, size = away.shape
    both = base[...] + wide_dot(wide_left(away[...]), other_maps[index])
    root[:half, :] = both[:, size:]
    root[half:, :] = tails[tails.shape[0] - 1]
    node[...] = both[:, :size]


def maps_kernel(leaf_map, home, away, *refs):
    wide_maps, maps = refs[-2:]
    k_half, size = home.shape[1:]
    core = lax.axis_index("blk") & 1
    maps[:, :size] = leaf_map[...]
    for i in range(home.shape[0]):
        columns = slice((i + 1) * size, (i + 2) * size)
        maps[span(core, k_half), columns] = home[i]
        maps[span(1 - core, k_half), columns] = away[i]
    wide_maps[...] = wide_right(maps[...])


def affected(child, height):
    position = lax.axis_index("blk")
    below = lax.axis_index("level") > 0
    shared = [position >> t == child[0] >> t for t in range(height)]
    return [jnp.logical_and(below, same) for same in shared] + [below, below]


def targets(leaf_out, node_out, root_out, rows):
    nodes = [node_out.at[tier, rows] for tier in range(node_out.shape[0])]
    return [leaf_out.at[rows]] + nodes + [root_out.at[rows]]


def part_rows(part, half):
    core = lax.axis_index("blk") & 1
    return pl.ds(pl.multiple_of((core if part == 0 else 1 - core) * half, 8), half)


def early_kernel(height, child, solved, *refs):
    nodes, roots, refs = refs[: 2 * height], refs[2 * height : 2 * height + 2], refs[-4:]
    leaf_out, node_out, root_out, sems = refs
    half, _ = solved.shape[1:]
    late = affected(child, height)
    copies = []
    for part in range(2):
        outs = targets(leaf_out, node_out, root_out, part_rows(part, half))
        bases = [solved.at[part]] + [nodes[2 * tier + part] for tier in range(height)]
        bases += [roots[part].at[pl.ds(0, half)]]
        copies += [
            (late[i], pltpu.make_async_copy(base, out, sems.at[part, i]))
            for i, (base, out) in enumerate(zip(bases, outs))
        ]
    for act in ("start", "wait"):
        for skip, copy in copies:
            pl.when(jnp.logical_not(skip))(getattr(copy, act))


def final_kernel(fronts, height, child, solved, wide_maps, *refs):
    nodes, refs = refs[: 2 * height], refs[2 * height :]
    roots, refs = refs[: 2 * fronts], refs[2 * fronts + 3 :]
    leaf_out, node_out, root_out, root_maps, incoming, result, sems = refs
    core, level = lax.axis_index("blk") & 1, lax.axis_index("level")
    half, size = solved.shape[1:]
    k_half = root_maps.shape[1] // 2
    count = height + 2
    late = affected(child, height)
    for front in range(1, fronts):
        root_maps[front, span(core, k_half), :] = roots[2 * front][half:, :]
        root_maps[front, span(1 - core, k_half), :] = roots[2 * front + 1][half:, :]

    def both_rows(mask):
        return jnp.concatenate([roots[2 * mask][:half, :], roots[2 * mask + 1][:half, :]], axis=0)

    for here in range(1, fronts):

        @pl.when(level == here)
        def _():
            value = both_rows(here)
            for front in range(1, here):
                value = both_rows(here ^ front) + product(value, root_maps[here ^ front])
            incoming[...] = wide_left(value)

    step = half // 2
    copies = []
    for chunk in range(4):
        first = (core if chunk < 2 else 1 - core) * half + chunk % 2 * step
        outs = targets(leaf_out, node_out, root_out, pl.ds(pl.multiple_of(first, 8), step))
        copies.append(
            [
                pltpu.make_async_copy(result.at[chunk, i], out, sems.at[chunk, i])
                for i, out in enumerate(outs)
            ]
        )

    def update(first, last):
        for chunk in range(4):
            part, inner = chunk // 2, slice(chunk % 2 * step, (chunk % 2 + 1) * step)
            change = wide_dot(
                incoming[chunk * step : (chunk + 1) * step, :], wide_maps[:, first * size : last * size]
            )
            for i in range(first, last):
                if i == 0:
                    base = solved[part, inner, :]
                elif i <= height:
                    base = nodes[2 * (i - 1) + part][inner, :]
                else:
                    base = roots[part][inner, :]
                result[chunk, i] = base + change[:, (i - first) * size : (i + 1 - first) * size]
                copies[chunk][i].start()

    for i in range(height + 1):
        first = jnp.logical_and(late[i], jnp.logical_not(late[i - 1])) if i else late[0]
        pl.when(first)(functools.partial(update, i, count))
    for i, flag in enumerate(late):
        for chunk in range(4):
            pl.when(flag)(copies[chunk][i].wait)


def shards(
    right_sides,
    leaf_gen,
    leaf_inverse,
    leaf_lower,
    node_gen,
    node_inverse,
    node_lower,
    coupling,
    child_leaf,
):
    rows, leaf_size = right_sides.shape[1:]
    size = leaf_lower.shape[2]
    k_rows = coupling.shape[1]
    height = node_gen.shape[2]
    fronts = lax.axis_size("level")
    leaves = lax.axis_size("blk")
    half = rows // 2
    part = half + k_rows // 2
    smem = pl.BlockSpec(memory_space=pltpu.SMEM)
    vmem = pl.BlockSpec(memory_space=pltpu.VMEM)
    hbm = pl.BlockSpec(memory_space=pltpu.HBM)
    anywhere = pl.BlockSpec(memory_space=pl.ANY)
    array = lambda *shape: jax.ShapeDtypeStruct(shape, f32)

    def blk_swap(value, mask):
        return lax.ppermute(value, "blk", [(i, i ^ mask) for i in range(leaves)])

    def level_swap(value, mask):
        return lax.ppermute(value, "level", [(i, i ^ mask) for i in range(fronts)])

    k_half = k_rows // 2
    node_params = (node_gen[0, 0], node_inverse[0, 0], node_lower[0, 0])
    away, leaf_solve_map, leaf_skeleton, right_here, coupling_here, *first_params = call(
        leaf_kernel,
        (
            array(part, size),
            array(leaf_size, size),
            jax.ShapeDtypeStruct((3 * leaf_size, size), bf16),
            array(2, half, leaf_size),
            array(k_rows, leaf_size),
            *(array(*value.shape[1:]) for value in node_params),
        ),
        tuple(
            pltpu.with_memory_space_constraint(value, pltpu.HBM)
            for value in (
                right_sides[0],
                leaf_gen[0],
                leaf_inverse[0],
                leaf_lower[0],
                coupling[0],
                *node_params,
            )
        ),
        6 * (part + leaf_size) * leaf_size * size,
        in_specs=[hbm] * 8,
        scratch_shapes=[
            pltpu.VMEM((leaf_size, leaf_size), f32),
            pltpu.VMEM((size, size), f32),
            pltpu.VMEM((size, size), f32),
            pltpu.SemaphoreType.DMA((9,)),
        ],
    )
    merge_flops = 6 * half * 2 * size * size
    fold_flops = 6 * 4 * size * size * size
    wide = lambda count: jax.ShapeDtypeStruct((count, 3 * size, 2 * size), bf16)
    both = pltpu.VMEM((2 * size, 2 * size), f32)
    first_mine, first_other, base, home = call(
        first_fold_kernel,
        (wide(1), wide(1), array(half, 2 * size), array(k_half, size)),
        (*first_params, right_here, coupling_here, leaf_skeleton),
        fold_flops + 6 * part * (leaf_size + 2 * size) * size,
        scratch_shapes=[both],
    )
    *node_params, away = lax.optimization_barrier((*node_params, away))
    away = blk_swap(away, 1)
    node, skeleton = call(
        first_merge_kernel,
        (array(half, size), array(half, size)),
        (base, away, first_other),
        merge_flops,
    )
    nodes, away_first = [node], away

    def folds(first, last, *after):
        return call(
            functools.partial(fold_kernel, first),
            (wide(last - first),) * 2,
            (*node_params, *after),
            (last - first) * fold_flops,
            in_specs=[vmem] * 3 + [anywhere] * len(after),
            scratch_shapes=[both],
        )

    child_leaf, skeleton = lax.optimization_barrier((child_leaf, skeleton))
    for tier in range(1, height):
        away = blk_swap(skeleton, 1 << tier)
        after = ()
        if tier == 1:
            mine_maps, other_maps = folds(1, height - 1)
            tail, carried, *climb = call(
                carry_kernel,
                (array(k_half, size),) * (3 if height == 3 else 2),
                (child_leaf, home, away_first, first_mine, first_other, mine_maps),
                6 * k_half * 5 * size * size,
                in_specs=[smem] + [vmem] * 5,
            )
            tails = [tail]
        if tier < height - 2:
            pair = call(
                functools.partial(pair_kernel, tier - 1),
                array(k_half, 2 * size),
                (carried, blk_swap(carried, 1 << tier), mine_maps, other_maps),
                6 * k_half * 4 * size * size,
            )
            tails.append(pair[:, :size])
            carried = pair[:, size:]
        if tier == height - 2:
            if not climb:
                climb = [
                    call(
                        functools.partial(climb_kernel, tier - 1),
                        array(k_half, size),
                        (carried, mine_maps),
                        6 * k_half * size * size,
                    )
                ]
            far = blk_swap(climb[0], 2 << tier)
            after = (climb[0],)
        if tier == height - 1:
            top_mine, top_other = folds(height - 1, height)
            relay = call(relay_kernel, array(2, k_half, size), (carried, far), k_half * size)
            relayed = blk_swap(relay, 1 << (tier - 1))
            tails = call(
                functools.partial(top_kernel, tier - 2),
                array(height + 1, k_half, size),
                (jnp.stack(tails), relay, relayed, mine_maps, other_maps, top_mine, top_other),
                6 * k_half * 6 * size * size,
            )
            solved, leaf_map = call(
                functools.partial(leaf_solve_kernel, height - 2),
                (array(2, half, size), array(k_rows, size)),
                (*early, *leaf_args),
                6 * (rows + k_rows) * leaf_size * size,
                in_specs=[vmem] * 2 + [smem] + [vmem] * 3,
            )
            after = (solved,)
        last = tier == height - 1
        if last:
            mine_maps, other_maps = top_mine, top_other
        index = 0 if last else tier - 1
        base = call(
            functools.partial(base_kernel, index),
            array(half, 2 * size),
            (skeleton, mine_maps),
            merge_flops,
        )
        leaf_args = (child_leaf, right_here, coupling_here, leaf_solve_map)
        kernel = functools.partial(last_merge_kernel if last else merge_kernel, index)
        args, specs = (base, away, other_maps), [vmem] * 3
        shapes = (array(half, size), array(part if last else half, size))
        if last:
            args, specs = args + (tails,), specs + [vmem]
        if tier == height - 2:
            kernel = functools.partial(late_merge_kernel, index, height - 2)
            args, specs = args + leaf_args, specs + [smem] + [vmem] * 3
            shapes += (array(2, half, size), array(k_rows, size))
        node, skeleton, *early = call(
            kernel, shapes, args + after, merge_flops, in_specs=specs + [anywhere] * len(after)
        )
        nodes.append(node)
    received = [level_swap(skeleton, mask) for mask in range(1, fronts)]
    roots = [skeleton, blk_swap(skeleton, 1)]
    for value in received:
        roots += [value, blk_swap(value, 1)]
    pairs = []
    for value in nodes:
        pairs += [value, blk_swap(value, 1)]
    shapes = (array(rows, size), array(height, rows, size), array(rows, size))
    early = call(
        functools.partial(early_kernel, height),
        shapes,
        (child_leaf, solved, *pairs, *roots[:2]),
        rows * size,
        in_specs=[smem] + [vmem] * (len(pairs) + 3),
        out_specs=(hbm,) * 3,
        scratch_shapes=[pltpu.SemaphoreType.DMA((2, height + 2))],
    )
    wide_maps = call(
        maps_kernel,
        jax.ShapeDtypeStruct((3 * k_rows, size * (height + 2)), bf16),
        (leaf_map, tails, blk_swap(tails, 1)),
        k_rows * size * (height + 2) * 4,
        scratch_shapes=[pltpu.VMEM((k_rows, size * (height + 2)), f32)],
    )
    args = (child_leaf, solved, wide_maps, *pairs, *roots)
    leaf_out, node_out, root_out = call(
        functools.partial(final_kernel, fronts, height),
        shapes,
        (*args, *early),
        6 * rows * size * size * (height + 2),
        in_specs=[smem] + [vmem] * (len(args) - 1) + [hbm] * 3,
        out_specs=(hbm,) * 3,
        aliases={len(args) + i: i for i in range(3)},
        scratch_shapes=[
            pltpu.VMEM((fronts, k_rows, size), f32),
            pltpu.VMEM((rows, 3 * size), bf16),
            pltpu.VMEM((4, height + 2, rows // 4, size), f32),
            pltpu.SemaphoreType.DMA((4, height + 2)),
        ],
    )
    return (leaf_out[None], node_out[None, None], root_out[None])


def solution(mesh):
    in_specs = (
        P("level", None, "blk"),
        P("level", "blk", None),
        P("level", "blk", None),
        P("level", "blk", None),
        P("level", "blk", None, None, None),
        P("level", "blk", None, None, None),
        P("level", "blk", None, None, None),
        P("level", None, None),
        P("level"),
    )
    out_specs = (
        P("level", None, "blk"),
        P("level", "blk", None, None, None),
        P("level", None, None),
    )

    return jax.shard_map(shards, mesh=mesh, in_specs=in_specs, out_specs=out_specs, check_vma=False)
```

```python
import functools

import jax
import jax.numpy as jnp
from jax import lax
from jax.experimental import pallas as pl
from jax.experimental.pallas import tpu as pltpu
from jax.sharding import PartitionSpec as P


f32 = jnp.float32
bf16 = jnp.bfloat16
VMEM_LIMIT = 12 << 20


def split(value):
    high = value.astype(bf16)
    return high, (value - high.astype(f32)).astype(bf16)


def wide_left(value):
    high, low = split(value)
    return jnp.concatenate([high, low, high], axis=1)


def wide_right(value):
    high, low = split(value)
    return jnp.concatenate([high, high, low], axis=0)


def wide_dot(left, right):
    return jnp.dot(left, right, preferred_element_type=f32)


def product(left, right):
    return wide_dot(wide_left(left), wide_right(right))


def call(kernel, out_shape, args, flops, in_specs=None, out_specs=None, scratch_shapes=(), aliases={}):
    size = lambda s: s.size * s.dtype.itemsize
    vmem = pl.BlockSpec(memory_space=pltpu.VMEM)
    moved = sum(size(a) for a in args) + sum(size(o) for o in jax.tree.leaves(out_shape))
    return pl.pallas_call(
        kernel,
        out_shape=out_shape,
        in_specs=in_specs or [vmem] * len(args),
        out_specs=out_specs or jax.tree.map(lambda _: vmem, out_shape),
        scratch_shapes=scratch_shapes,
        input_output_aliases=aliases,
        compiler_params=pltpu.CompilerParams(vmem_limit_bytes=VMEM_LIMIT),
        cost_estimate=pl.CostEstimate(flops=flops, bytes_accessed=moved, transcendentals=0),
    )(*args)


def span(index, length):
    return pl.ds(pl.multiple_of(index * length, 8), length)


def leaf_kernel(right, generator, inverse, lower, coupling, *refs):
    later, (away, solve_map, skeleton_map), refs = refs[:3], refs[3:6], refs[6:]
    (right_here, coupling_here, *later_here), refs = refs[:5], refs[5:]
    generator_here, inverse_here, lower_here, sems = refs
    core = lax.axis_index("blk") & 1
    half, k_half = right.shape[0] // 2, coupling.shape[0] // 2
    size = inverse.shape[0]
    copies = [
        pltpu.make_async_copy(source, target, sems.at[i])
        for i, (source, target) in enumerate(
            [
                (generator, generator_here),
                (inverse, inverse_here),
                (lower, lower_here),
                (right.at[span(1 - core, half)], right_here.at[0]),
                (coupling, coupling_here),
                (right.at[span(core, half)], right_here.at[1]),
                *((source.at[0], target) for source, target in zip(later, later_here)),
            ]
        )
    ]
    for copy in copies:
        copy.start()
    for copy in copies[:2]:
        copy.wait()
    solved = product(generator_here[:, :size], inverse_here[...])
    solve_map[...] = solved
    copies[2].wait()
    parts = wide_right(generator_here[:, size:] - product(solved, lower_here[...]))
    skeleton_map[...] = parts
    copies[3].wait()
    away[:half, :] = wide_dot(wide_left(right_here[0]), parts)
    copies[4].wait()
    away[half:, :] = wide_dot(wide_left(coupling_here[span(1 - core, k_half), :]), parts)
    for copy in copies[5:]:
        copy.wait()


def leaf_solve(child, right, coupling, solve_map, solved, leaf_map):
    parts = wide_right(solve_map[...])
    for part in range(2):
        solved[part] = wide_dot(wide_left(right[1 - part]), parts)
    on_target = lax.axis_index("blk") == child[0]
    leaf_map[...] = jnp.where(on_target, wide_dot(wide_left(coupling[...]), parts), 0.0)


def leaf_solve_kernel(bit, solved_early, map_early, *refs):
    solved, leaf_map = refs[-2:]
    early = (lax.axis_index("blk") >> bit) & 1

    @pl.when(early == 1)
    def _():
        solved[...] = solved_early[...]
        leaf_map[...] = map_early[...]

    @pl.when(early == 0)
    def _():
        leaf_solve(*refs)


def fold(tier, generator, inverse, lower, both):
    size = inverse.shape[0]
    solve_map = product(generator[:, :size], inverse)
    both[:, :size] = solve_map
    both[:, size:] = generator[:, size:] - product(solve_map, lower)
    upper = (lax.axis_index("blk") >> tier) & 1
    return wide_right(both[span(upper, size), :]), wide_right(both[span(1 - upper, size), :])


def first_fold_kernel(
    generator, inverse, lower, right, coupling, skeleton_map, mine_maps, other_maps, base, home, both
):
    core = lax.axis_index("blk") & 1
    k_half = home.shape[0]
    value = wide_dot(wide_left(right[1]), skeleton_map[...])
    home[...] = wide_dot(wide_left(coupling[span(core, k_half), :]), skeleton_map[...])
    mine_maps[0], other_maps[0] = fold(0, generator[...], inverse[...], lower[...], both)
    base[...] = wide_dot(wide_left(value), mine_maps[0])


def fold_kernel(first, generator, inverse, lower, *refs):
    mine_maps, other_maps, both = refs[-3:]
    for i in range(mine_maps.shape[0]):
        tier = first + i
        mine_maps[i], other_maps[i] = fold(tier, generator[tier], inverse[tier], lower[tier], both)


def base_kernel(index, home, mine_maps, base):
    base[...] = wide_dot(wide_left(home[...]), mine_maps[index])


def late_merge_kernel(index, bit, base, away, other_maps, child, right, coupling, solve_map, *refs):
    node, skeleton, solved, leaf_map = refs[-4:]
    merge_kernel(index, base, away, other_maps, node, skeleton)

    @pl.when((lax.axis_index("blk") >> bit) & 1 == 1)
    def _():
        leaf_solve(child, right, coupling, solve_map, solved, leaf_map)


def merge_kernel(index, base, away, other_maps, *refs):
    node, skeleton = refs[-2:]
    size = away.shape[1]
    both = base[...] + wide_dot(wide_left(away[...]), other_maps[index])
    skeleton[...] = both[:, size:]
    node[...] = both[:, :size]


def first_merge_kernel(base, away, other_maps, node, skeleton):
    half, size = node.shape
    both = base[...] + wide_dot(wide_left(away[:half, :]), other_maps[0])
    skeleton[...] = both[:, size:]
    node[...] = both[:, :size]


def carry_kernel(child, home, away, mine_maps, other_maps, next_maps, tail, carried, *climb):
    k_half, size = home.shape
    position = lax.axis_index("blk")
    mine = wide_dot(wide_left(home[...]), mine_maps[0])
    other = wide_dot(wide_left(away[away.shape[0] - k_half :, :]), other_maps[0])
    both = jnp.where(position == child[0], mine, 0.0) + jnp.where(position ^ 1 == child[0], other, 0.0)
    tail[...] = both[:, :size]
    carried[...] = both[:, size:]
    for out in climb:
        out[...] = wide_dot(wide_left(both[:, size:]), next_maps[0, :, size:])


def climb_kernel(index, carried, mine_maps, climb):
    size = carried.shape[1]
    climb[...] = wide_dot(wide_left(carried[...]), mine_maps[index, :, size:])


def relay_kernel(carried, far, out):
    out[0] = carried[...]
    out[1] = far[...]


def pair_kernel(index, home, away, mine_maps, other_maps, out):
    out[...] = wide_dot(wide_left(home[...]), mine_maps[index]) + wide_dot(
        wide_left(away[...]), other_maps[index]
    )


def top_kernel(index, tails, home, away, mine_maps, other_maps, top_mine, top_other, out):
    size = tails.shape[2]
    count = tails.shape[0]
    out[:count] = tails[...]
    both = wide_dot(wide_left(home[0]), mine_maps[index]) + wide_dot(
        wide_left(away[0]), other_maps[index]
    )
    out[count] = both[:, :size]
    both = wide_dot(wide_left(both[:, size:]), top_mine[0]) + wide_dot(
        wide_left(home[1] + away[1]), top_other[0]
    )
    out[count + 1] = both[:, :size]
    out[count + 2] = both[:, size:]


def last_merge_kernel(index, base, away, other_maps, tails, *refs):
    node, root = refs[-2:]
    half, size = away.shape
    both = base[...] + wide_dot(wide_left(away[...]), other_maps[index])
    root[:half, :] = both[:, size:]
    root[half:, :] = tails[tails.shape[0] - 1]
    node[...] = both[:, :size]


def maps_kernel(leaf_map, home, away, *refs):
    wide_maps, maps = refs[-2:]
    k_half, size = home.shape[1:]
    core = lax.axis_index("blk") & 1
    maps[:, :size] = leaf_map[...]
    for i in range(home.shape[0]):
        columns = slice((i + 1) * size, (i + 2) * size)
        maps[span(core, k_half), columns] = home[i]
        maps[span(1 - core, k_half), columns] = away[i]
    wide_maps[...] = wide_right(maps[...])


def affected(child, height):
    position = lax.axis_index("blk")
    below = lax.axis_index("level") > 0
    shared = [position >> t == child[0] >> t for t in range(height)]
    return [jnp.logical_and(below, same) for same in shared] + [below, below]


def targets(leaf_out, node_out, root_out, rows):
    nodes = [node_out.at[tier, rows] for tier in range(node_out.shape[0])]
    return [leaf_out.at[rows]] + nodes + [root_out.at[rows]]


def part_rows(part, half):
    core = lax.axis_index("blk") & 1
    return pl.ds(pl.multiple_of((core if part == 0 else 1 - core) * half, 8), half)


def early_kernel(height, child, solved, *refs):
    nodes, roots, refs = refs[: 2 * height], refs[2 * height : 2 * height + 2], refs[-4:]
    leaf_out, node_out, root_out, sems = refs
    half, _ = solved.shape[1:]
    late = affected(child, height)
    copies = []
    for part in range(2):
        outs = targets(leaf_out, node_out, root_out, part_rows(part, half))
        bases = [solved.at[part]] + [nodes[2 * tier + part] for tier in range(height)]
        bases += [roots[part].at[pl.ds(0, half)]]
        copies += [
            (late[i], pltpu.make_async_copy(base, out, sems.at[part, i]))
            for i, (base, out) in enumerate(zip(bases, outs))
        ]
    for act in ("start", "wait"):
        for skip, copy in copies:
            pl.when(jnp.logical_not(skip))(getattr(copy, act))


def final_kernel(fronts, height, child, solved, wide_maps, *refs):
    nodes, refs = refs[: 2 * height], refs[2 * height :]
    roots, refs = refs[: 2 * fronts], refs[2 * fronts + 3 :]
    leaf_out, node_out, root_out, root_maps, incoming, result, sems = refs
    core, level = lax.axis_index("blk") & 1, lax.axis_index("level")
    half, size = solved.shape[1:]
    k_half = root_maps.shape[1] // 2
    count = height + 2
    late = affected(child, height)
    for front in range(1, fronts):
        root_maps[front, span(core, k_half), :] = roots[2 * front][half:, :]
        root_maps[front, span(1 - core, k_half), :] = roots[2 * front + 1][half:, :]

    def both_rows(mask):
        return jnp.concatenate([roots[2 * mask][:half, :], roots[2 * mask + 1][:half, :]], axis=0)

    for here in range(1, fronts):

        @pl.when(level == here)
        def _():
            value = both_rows(here)
            for front in range(1, here):
                value = both_rows(here ^ front) + product(value, root_maps[here ^ front])
            incoming[...] = wide_left(value)

    copies = []
    for part in range(2):
        outs = targets(leaf_out, node_out, root_out, part_rows(part, half))
        copies.append(
            [
                pltpu.make_async_copy(result.at[part, i], out, sems.at[part, i])
                for i, out in enumerate(outs)
            ]
        )

    def update(first, last):
        for part in range(2):
            change = wide_dot(
                incoming[part * half : (part + 1) * half, :], wide_maps[:, first * size : last * size]
            )
            for i in range(first, last):
                if i == 0:
                    base = solved[part]
                elif i <= height:
                    base = nodes[2 * (i - 1) + part][...]
                else:
                    base = roots[part][:half, :]
                result[part, i] = base + change[:, (i - first) * size : (i + 1 - first) * size]
                copies[part][i].start()

    for i in range(height + 1):
        first = jnp.logical_and(late[i], jnp.logical_not(late[i - 1])) if i else late[0]
        pl.when(first)(functools.partial(update, i, count))
    for i, flag in enumerate(late):
        for part in range(2):
            pl.when(flag)(copies[part][i].wait)


def shards(
    right_sides,
    leaf_gen,
    leaf_inverse,
    leaf_lower,
    node_gen,
    node_inverse,
    node_lower,
    coupling,
    child_leaf,
):
    rows, leaf_size = right_sides.shape[1:]
    size = leaf_lower.shape[2]
    k_rows = coupling.shape[1]
    height = node_gen.shape[2]
    fronts = lax.axis_size("level")
    leaves = lax.axis_size("blk")
    half = rows // 2
    part = half + k_rows // 2
    smem = pl.BlockSpec(memory_space=pltpu.SMEM)
    vmem = pl.BlockSpec(memory_space=pltpu.VMEM)
    hbm = pl.BlockSpec(memory_space=pltpu.HBM)
    anywhere = pl.BlockSpec(memory_space=pl.ANY)
    array = lambda *shape: jax.ShapeDtypeStruct(shape, f32)

    def blk_swap(value, mask):
        return lax.ppermute(value, "blk", [(i, i ^ mask) for i in range(leaves)])

    def level_swap(value, mask):
        return lax.ppermute(value, "level", [(i, i ^ mask) for i in range(fronts)])

    k_half = k_rows // 2
    node_params = (node_gen[0, 0], node_inverse[0, 0], node_lower[0, 0])
    away, leaf_solve_map, leaf_skeleton, right_here, coupling_here, *first_params = call(
        leaf_kernel,
        (
            array(part, size),
            array(leaf_size, size),
            jax.ShapeDtypeStruct((3 * leaf_size, size), bf16),
            array(2, half, leaf_size),
            array(k_rows, leaf_size),
            *(array(*value.shape[1:]) for value in node_params),
        ),
        tuple(
            pltpu.with_memory_space_constraint(value, pltpu.HBM)
            for value in (
                right_sides[0],
                leaf_gen[0],
                leaf_inverse[0],
                leaf_lower[0],
                coupling[0],
                *node_params,
            )
        ),
        6 * (part + leaf_size) * leaf_size * size,
        in_specs=[hbm] * 8,
        scratch_shapes=[
            pltpu.VMEM((leaf_size, leaf_size), f32),
            pltpu.VMEM((size, size), f32),
            pltpu.VMEM((size, size), f32),
            pltpu.SemaphoreType.DMA((9,)),
        ],
    )
    merge_flops = 6 * half * 2 * size * size
    fold_flops = 6 * 4 * size * size * size
    wide = lambda count: jax.ShapeDtypeStruct((count, 3 * size, 2 * size), bf16)
    both = pltpu.VMEM((2 * size, 2 * size), f32)
    first_mine, first_other, base, home = call(
        first_fold_kernel,
        (wide(1), wide(1), array(half, 2 * size), array(k_half, size)),
        (*first_params, right_here, coupling_here, leaf_skeleton),
        fold_flops + 6 * part * (leaf_size + 2 * size) * size,
        scratch_shapes=[both],
    )
    *node_params, away = lax.optimization_barrier((*node_params, away))
    away = blk_swap(away, 1)
    node, skeleton = call(
        first_merge_kernel,
        (array(half, size), array(half, size)),
        (base, away, first_other),
        merge_flops,
    )
    nodes, away_first = [node], away

    def folds(first, last, *after):
        return call(
            functools.partial(fold_kernel, first),
            (wide(last - first),) * 2,
            (*node_params, *after),
            (last - first) * fold_flops,
            in_specs=[vmem] * 3 + [anywhere] * len(after),
            scratch_shapes=[both],
        )

    child_leaf, skeleton = lax.optimization_barrier((child_leaf, skeleton))
    for tier in range(1, height):
        away = blk_swap(skeleton, 1 << tier)
        after = ()
        if tier == 1:
            mine_maps, other_maps = folds(1, height - 1)
            tail, carried, *climb = call(
                carry_kernel,
                (array(k_half, size),) * (3 if height == 3 else 2),
                (child_leaf, home, away_first, first_mine, first_other, mine_maps),
                6 * k_half * 5 * size * size,
                in_specs=[smem] + [vmem] * 5,
            )
            tails = [tail]
        if tier < height - 2:
            pair = call(
                functools.partial(pair_kernel, tier - 1),
                array(k_half, 2 * size),
                (carried, blk_swap(carried, 1 << tier), mine_maps, other_maps),
                6 * k_half * 4 * size * size,
            )
            tails.append(pair[:, :size])
            carried = pair[:, size:]
        if tier == height - 2:
            if not climb:
                climb = [
                    call(
                        functools.partial(climb_kernel, tier - 1),
                        array(k_half, size),
                        (carried, mine_maps),
                        6 * k_half * size * size,
                    )
                ]
            far = blk_swap(climb[0], 2 << tier)
            after = (climb[0],)
        if tier == height - 1:
            top_mine, top_other = folds(height - 1, height)
            relay = call(relay_kernel, array(2, k_half, size), (carried, far), k_half * size)
            relayed = blk_swap(relay, 1 << (tier - 1))
            tails = call(
                functools.partial(top_kernel, tier - 2),
                array(height + 1, k_half, size),
                (jnp.stack(tails), relay, relayed, mine_maps, other_maps, top_mine, top_other),
                6 * k_half * 6 * size * size,
            )
            solved, leaf_map = call(
                functools.partial(leaf_solve_kernel, height - 2),
                (array(2, half, size), array(k_rows, size)),
                (*early, *leaf_args),
                6 * (rows + k_rows) * leaf_size * size,
                in_specs=[vmem] * 2 + [smem] + [vmem] * 3,
            )
            after = (solved,)
        last = tier == height - 1
        if last:
            mine_maps, other_maps = top_mine, top_other
        index = 0 if last else tier - 1
        base = call(
            functools.partial(base_kernel, index),
            array(half, 2 * size),
            (skeleton, mine_maps),
            merge_flops,
        )
        leaf_args = (child_leaf, right_here, coupling_here, leaf_solve_map)
        kernel = functools.partial(last_merge_kernel if last else merge_kernel, index)
        args, specs = (base, away, other_maps), [vmem] * 3
        shapes = (array(half, size), array(part if last else half, size))
        if last:
            args, specs = args + (tails,), specs + [vmem]
        if tier == height - 2:
            kernel = functools.partial(late_merge_kernel, index, height - 2)
            args, specs = args + leaf_args, specs + [smem] + [vmem] * 3
            shapes += (array(2, half, size), array(k_rows, size))
        node, skeleton, *early = call(
            kernel, shapes, args + after, merge_flops, in_specs=specs + [anywhere] * len(after)
        )
        nodes.append(node)
    received = [level_swap(skeleton, mask) for mask in range(1, fronts)]
    roots = [skeleton, blk_swap(skeleton, 1)]
    for value in received:
        roots += [value, blk_swap(value, 1)]
    pairs = []
    for value in nodes:
        pairs += [value, blk_swap(value, 1)]
    shapes = (array(rows, size), array(height, rows, size), array(rows, size))
    early = call(
        functools.partial(early_kernel, height),
        shapes,
        (child_leaf, solved, *pairs, *roots[:2]),
        rows * size,
        in_specs=[smem] + [vmem] * (len(pairs) + 3),
        out_specs=(hbm,) * 3,
        scratch_shapes=[pltpu.SemaphoreType.DMA((2, height + 2))],
    )
    wide_maps = call(
        maps_kernel,
        jax.ShapeDtypeStruct((3 * k_rows, size * (height + 2)), bf16),
        (leaf_map, tails, blk_swap(tails, 1)),
        k_rows * size * (height + 2) * 4,
        scratch_shapes=[pltpu.VMEM((k_rows, size * (height + 2)), f32)],
    )
    args = (child_leaf, solved, wide_maps, *pairs, *roots)
    leaf_out, node_out, root_out = call(
        functools.partial(final_kernel, fronts, height),
        shapes,
        (*args, *early),
        6 * rows * size * size * (height + 2),
        in_specs=[smem] + [vmem] * (len(args) - 1) + [hbm] * 3,
        out_specs=(hbm,) * 3,
        aliases={len(args) + i: i for i in range(3)},
        scratch_shapes=[
            pltpu.VMEM((fronts, k_rows, size), f32),
            pltpu.VMEM((rows, 3 * size), bf16),
            pltpu.VMEM((2, height + 2, half, size), f32),
            pltpu.SemaphoreType.DMA((2, height + 2)),
        ],
    )
    return (leaf_out[None], node_out[None, None], root_out[None])


def solution(mesh):
    in_specs = (
        P("level", None, "blk"),
        P("level", "blk", None),
        P("level", "blk", None),
        P("level", "blk", None),
        P("level", "blk", None, None, None),
        P("level", "blk", None, None, None),
        P("level", "blk", None, None, None),
        P("level", None, None),
        P("level"),
    )
    out_specs = (
        P("level", None, "blk"),
        P("level", "blk", None, None, None),
        P("level", None, None),
    )

    return jax.shard_map(shards, mesh=mesh, in_specs=in_specs, out_specs=out_specs, check_vma=False)
```

```python
import functools

import jax
import jax.numpy as jnp
from jax import lax
from jax.experimental import pallas as pl
from jax.experimental.pallas import tpu as pltpu
from jax.sharding import PartitionSpec as P


f32 = jnp.float32
bf16 = jnp.bfloat16
VMEM_LIMIT = 12 << 20


def split(value):
    high = value.astype(bf16)
    return high, (value - high.astype(f32)).astype(bf16)


def wide_left(value):
    high, low = split(value)
    return jnp.concatenate([high, low, high], axis=1)


def wide_right(value):
    high, low = split(value)
    return jnp.concatenate([high, high, low], axis=0)


def wide_dot(left, right):
    return jnp.dot(left, right, preferred_element_type=f32)


def product(left, right):
    return wide_dot(wide_left(left), wide_right(right))


def call(kernel, out_shape, args, flops, in_specs=None, out_specs=None, scratch_shapes=(), aliases={}):
    size = lambda s: s.size * s.dtype.itemsize
    vmem = pl.BlockSpec(memory_space=pltpu.VMEM)
    moved = sum(size(a) for a in args) + sum(size(o) for o in jax.tree.leaves(out_shape))
    return pl.pallas_call(
        kernel,
        out_shape=out_shape,
        in_specs=in_specs or [vmem] * len(args),
        out_specs=out_specs or jax.tree.map(lambda _: vmem, out_shape),
        scratch_shapes=scratch_shapes,
        input_output_aliases=aliases,
        compiler_params=pltpu.CompilerParams(vmem_limit_bytes=VMEM_LIMIT),
        cost_estimate=pl.CostEstimate(flops=flops, bytes_accessed=moved, transcendentals=0),
    )(*args)


def span(index, length):
    return pl.ds(pl.multiple_of(index * length, 8), length)


def leaf_kernel(right, generator, inverse, lower, coupling, *refs):
    later, (away, solve_map, skeleton_map), refs = refs[:3], refs[3:6], refs[6:]
    (right_here, coupling_here, *later_here), refs = refs[:5], refs[5:]
    generator_here, inverse_here, lower_here, sems = refs
    core = lax.axis_index("blk") & 1
    half, k_half = right.shape[0] // 2, coupling.shape[0] // 2
    size = inverse.shape[0]
    copies = [
        pltpu.make_async_copy(source, target, sems.at[i])
        for i, (source, target) in enumerate(
            [
                (generator, generator_here),
                (inverse, inverse_here),
                (lower, lower_here),
                (right.at[span(1 - core, half)], right_here.at[0]),
                (coupling, coupling_here),
                (right.at[span(core, half)], right_here.at[1]),
                *((source.at[0], target) for source, target in zip(later, later_here)),
            ]
        )
    ]
    for copy in copies:
        copy.start()
    for copy in copies[:2]:
        copy.wait()
    solved = product(generator_here[:, :size], inverse_here[...])
    solve_map[...] = solved
    copies[2].wait()
    parts = wide_right(generator_here[:, size:] - product(solved, lower_here[...]))
    skeleton_map[...] = parts
    copies[3].wait()
    away[:half, :] = wide_dot(wide_left(right_here[0]), parts)
    copies[4].wait()
    away[half:, :] = wide_dot(wide_left(coupling_here[span(1 - core, k_half), :]), parts)
    for copy in copies[5:]:
        copy.wait()


def leaf_solve(child, right, coupling, solve_map, solved, leaf_map):
    parts = wide_right(solve_map[...])
    for part in range(2):
        solved[part] = wide_dot(wide_left(right[1 - part]), parts)
    on_target = lax.axis_index("blk") == child[0]
    leaf_map[...] = jnp.where(on_target, wide_dot(wide_left(coupling[...]), parts), 0.0)


def leaf_solve_kernel(bit, solved_early, map_early, *refs):
    solved, leaf_map = refs[-2:]
    early = (lax.axis_index("blk") >> bit) & 1

    @pl.when(early == 1)
    def _():
        solved[...] = solved_early[...]
        leaf_map[...] = map_early[...]

    @pl.when(early == 0)
    def _():
        leaf_solve(*refs)


def fold(tier, generator, inverse, lower, both):
    size = inverse.shape[0]
    solve_map = product(generator[:, :size], inverse)
    both[:, :size] = solve_map
    both[:, size:] = generator[:, size:] - product(solve_map, lower)
    upper = (lax.axis_index("blk") >> tier) & 1
    return wide_right(both[span(upper, size), :]), wide_right(both[span(1 - upper, size), :])


def first_fold_kernel(
    generator, inverse, lower, right, coupling, skeleton_map, mine_maps, other_maps, base, home, both
):
    core = lax.axis_index("blk") & 1
    k_half = home.shape[0]
    value = wide_dot(wide_left(right[1]), skeleton_map[...])
    home[...] = wide_dot(wide_left(coupling[span(core, k_half), :]), skeleton_map[...])
    mine_maps[0], other_maps[0] = fold(0, generator[...], inverse[...], lower[...], both)
    base[...] = wide_dot(wide_left(value), mine_maps[0])


def fold_kernel(first, generator, inverse, lower, *refs):
    mine_maps, other_maps, both = refs[-3:]
    for i in range(mine_maps.shape[0]):
        tier = first + i
        mine_maps[i], other_maps[i] = fold(tier, generator[tier], inverse[tier], lower[tier], both)


def base_kernel(index, home, mine_maps, base):
    base[...] = wide_dot(wide_left(home[...]), mine_maps[index])


def late_merge_kernel(index, bit, base, away, other_maps, child, right, coupling, solve_map, *refs):
    node, skeleton, solved, leaf_map = refs[-4:]
    merge_kernel(index, base, away, other_maps, node, skeleton)

    @pl.when((lax.axis_index("blk") >> bit) & 1 == 1)
    def _():
        leaf_solve(child, right, coupling, solve_map, solved, leaf_map)


def merge_kernel(index, base, away, other_maps, *refs):
    node, skeleton = refs[-2:]
    size = away.shape[1]
    both = base[...] + wide_dot(wide_left(away[...]), other_maps[index])
    skeleton[...] = both[:, size:]
    node[...] = both[:, :size]


def first_merge_kernel(base, away, other_maps, _, node, skeleton):
    half, size = node.shape
    both = base[...] + wide_dot(wide_left(away[:half, :]), other_maps[0])
    skeleton[...] = both[:, size:]
    node[...] = both[:, :size]


def carry_kernel(child, home, away, mine_maps, other_maps, next_maps, tail, carried, *climb):
    k_half, size = home.shape
    position = lax.axis_index("blk")
    mine = wide_dot(wide_left(home[...]), mine_maps[0])
    other = wide_dot(wide_left(away[away.shape[0] - k_half :, :]), other_maps[0])
    both = jnp.where(position == child[0], mine, 0.0) + jnp.where(position ^ 1 == child[0], other, 0.0)
    tail[...] = both[:, :size]
    carried[...] = both[:, size:]
    for out in climb:
        out[...] = wide_dot(wide_left(both[:, size:]), next_maps[0, :, size:])


def climb_kernel(index, carried, mine_maps, climb):
    size = carried.shape[1]
    climb[...] = wide_dot(wide_left(carried[...]), mine_maps[index, :, size:])


def relay_kernel(carried, far, out):
    out[0] = carried[...]
    out[1] = far[...]


def pair_kernel(index, home, away, mine_maps, other_maps, out):
    out[...] = wide_dot(wide_left(home[...]), mine_maps[index]) + wide_dot(
        wide_left(away[...]), other_maps[index]
    )


def top_kernel(index, tails, home, away, mine_maps, other_maps, top_mine, top_other, out):
    size = tails.shape[2]
    count = tails.shape[0]
    out[:count] = tails[...]
    both = wide_dot(wide_left(home[0]), mine_maps[index]) + wide_dot(
        wide_left(away[0]), other_maps[index]
    )
    out[count] = both[:, :size]
    both = wide_dot(wide_left(both[:, size:]), top_mine[0]) + wide_dot(
        wide_left(home[1] + away[1]), top_other[0]
    )
    out[count + 1] = both[:, :size]
    out[count + 2] = both[:, size:]


def last_merge_kernel(index, base, away, other_maps, tails, *refs):
    node, root = refs[-2:]
    half, size = away.shape
    both = base[...] + wide_dot(wide_left(away[...]), other_maps[index])
    root[:half, :] = both[:, size:]
    root[half:, :] = tails[tails.shape[0] - 1]
    node[...] = both[:, :size]


def maps_kernel(leaf_map, home, away, *refs):
    wide_maps, maps = refs[-2:]
    k_half, size = home.shape[1:]
    core = lax.axis_index("blk") & 1
    maps[:, :size] = leaf_map[...]
    for i in range(home.shape[0]):
        columns = slice((i + 1) * size, (i + 2) * size)
        maps[span(core, k_half), columns] = home[i]
        maps[span(1 - core, k_half), columns] = away[i]
    wide_maps[...] = wide_right(maps[...])


def affected(child, height):
    position = lax.axis_index("blk")
    below = lax.axis_index("level") > 0
    shared = [position >> t == child[0] >> t for t in range(height)]
    return [jnp.logical_and(below, same) for same in shared] + [below, below]


def targets(leaf_out, node_out, root_out, rows):
    nodes = [node_out.at[tier, rows] for tier in range(node_out.shape[0])]
    return [leaf_out.at[rows]] + nodes + [root_out.at[rows]]


def part_rows(part, half):
    core = lax.axis_index("blk") & 1
    return pl.ds(pl.multiple_of((core if part == 0 else 1 - core) * half, 8), half)


def early_kernel(height, child, solved, *refs):
    nodes, roots, refs = refs[: 2 * height], refs[2 * height : 2 * height + 2], refs[-4:]
    leaf_out, node_out, root_out, sems = refs
    half, _ = solved.shape[1:]
    late = affected(child, height)
    copies = []
    for part in range(2):
        outs = targets(leaf_out, node_out, root_out, part_rows(part, half))
        bases = [solved.at[part]] + [nodes[2 * tier + part] for tier in range(height)]
        bases += [roots[part].at[pl.ds(0, half)]]
        copies += [
            (late[i], pltpu.make_async_copy(base, out, sems.at[part, i]))
            for i, (base, out) in enumerate(zip(bases, outs))
        ]
    for act in ("start", "wait"):
        for skip, copy in copies:
            pl.when(jnp.logical_not(skip))(getattr(copy, act))


def final_kernel(fronts, height, child, solved, wide_maps, *refs):
    nodes, refs = refs[: 2 * height], refs[2 * height :]
    roots, refs = refs[: 2 * fronts], refs[2 * fronts + 3 :]
    leaf_out, node_out, root_out, root_maps, incoming, result, sems = refs
    core, level = lax.axis_index("blk") & 1, lax.axis_index("level")
    half, size = solved.shape[1:]
    k_half = root_maps.shape[1] // 2
    count = height + 2
    late = affected(child, height)
    for front in range(1, fronts):
        root_maps[front, span(core, k_half), :] = roots[2 * front][half:, :]
        root_maps[front, span(1 - core, k_half), :] = roots[2 * front + 1][half:, :]

    def both_rows(mask):
        return jnp.concatenate([roots[2 * mask][:half, :], roots[2 * mask + 1][:half, :]], axis=0)

    for here in range(1, fronts):

        @pl.when(level == here)
        def _():
            value = both_rows(here)
            for front in range(1, here):
                value = both_rows(here ^ front) + product(value, root_maps[here ^ front])
            incoming[...] = wide_left(value)

    step = half // 2
    copies = []
    for chunk in range(4):
        first = (core if chunk < 2 else 1 - core) * half + chunk % 2 * step
        outs = targets(leaf_out, node_out, root_out, pl.ds(pl.multiple_of(first, 8), step))
        copies.append(
            [
                pltpu.make_async_copy(result.at[chunk, i], out, sems.at[chunk, i])
                for i, out in enumerate(outs)
            ]
        )

    def update(first, last):
        for chunk in range(4):
            part, inner = chunk // 2, slice(chunk % 2 * step, (chunk % 2 + 1) * step)
            change = wide_dot(
                incoming[chunk * step : (chunk + 1) * step, :], wide_maps[:, first * size : last * size]
            )
            for i in range(first, last):
                if i == 0:
                    base = solved[part, inner, :]
                elif i <= height:
                    base = nodes[2 * (i - 1) + part][inner, :]
                else:
                    base = roots[part][inner, :]
                result[chunk, i] = base + change[:, (i - first) * size : (i + 1 - first) * size]
                copies[chunk][i].start()

    for i in range(height + 1):
        first = jnp.logical_and(late[i], jnp.logical_not(late[i - 1])) if i else late[0]
        pl.when(first)(functools.partial(update, i, count))
    for i, flag in enumerate(late):
        for chunk in range(4):
            pl.when(flag)(copies[chunk][i].wait)


def shards(
    right_sides,
    leaf_gen,
    leaf_inverse,
    leaf_lower,
    node_gen,
    node_inverse,
    node_lower,
    coupling,
    child_leaf,
):
    rows, leaf_size = right_sides.shape[1:]
    size = leaf_lower.shape[2]
    k_rows = coupling.shape[1]
    height = node_gen.shape[2]
    fronts = lax.axis_size("level")
    leaves = lax.axis_size("blk")
    half = rows // 2
    part = half + k_rows // 2
    smem = pl.BlockSpec(memory_space=pltpu.SMEM)
    vmem = pl.BlockSpec(memory_space=pltpu.VMEM)
    hbm = pl.BlockSpec(memory_space=pltpu.HBM)
    anywhere = pl.BlockSpec(memory_space=pl.ANY)
    array = lambda *shape: jax.ShapeDtypeStruct(shape, f32)

    def blk_swap(value, mask):
        return lax.ppermute(value, "blk", [(i, i ^ mask) for i in range(leaves)])

    def level_swap(value, mask):
        return lax.ppermute(value, "level", [(i, i ^ mask) for i in range(fronts)])

    k_half = k_rows // 2
    node_params = (node_gen[0, 0], node_inverse[0, 0], node_lower[0, 0])
    away, leaf_solve_map, leaf_skeleton, right_here, coupling_here, *first_params = call(
        leaf_kernel,
        (
            array(part, size),
            array(leaf_size, size),
            jax.ShapeDtypeStruct((3 * leaf_size, size), bf16),
            array(2, half, leaf_size),
            array(k_rows, leaf_size),
            *(array(*value.shape[1:]) for value in node_params),
        ),
        tuple(
            pltpu.with_memory_space_constraint(value, pltpu.HBM)
            for value in (
                right_sides[0],
                leaf_gen[0],
                leaf_inverse[0],
                leaf_lower[0],
                coupling[0],
                *node_params,
            )
        ),
        6 * (part + leaf_size) * leaf_size * size,
        in_specs=[hbm] * 8,
        scratch_shapes=[
            pltpu.VMEM((leaf_size, leaf_size), f32),
            pltpu.VMEM((size, size), f32),
            pltpu.VMEM((size, size), f32),
            pltpu.SemaphoreType.DMA((9,)),
        ],
    )
    merge_flops = 6 * half * 2 * size * size
    fold_flops = 6 * 4 * size * size * size
    wide = lambda count: jax.ShapeDtypeStruct((count, 3 * size, 2 * size), bf16)
    both = pltpu.VMEM((2 * size, 2 * size), f32)
    first_mine, first_other, base, home = call(
        first_fold_kernel,
        (wide(1), wide(1), array(half, 2 * size), array(k_half, size)),
        (*first_params, right_here, coupling_here, leaf_skeleton),
        fold_flops + 6 * part * (leaf_size + 2 * size) * size,
        scratch_shapes=[both],
    )
    *node_params, child_leaf, away = lax.optimization_barrier((*node_params, child_leaf, away))
    away = blk_swap(away, 1)
    node, skeleton = call(
        first_merge_kernel,
        (array(half, size), array(half, size)),
        (base, away, first_other, child_leaf),
        merge_flops,
        in_specs=[vmem] * 3 + [smem],
    )
    nodes, away_first = [node], away

    def folds(first, last, *after):
        return call(
            functools.partial(fold_kernel, first),
            (wide(last - first),) * 2,
            (*node_params, *after),
            (last - first) * fold_flops,
            in_specs=[vmem] * 3 + [anywhere] * len(after),
            scratch_shapes=[both],
        )

    for tier in range(1, height):
        away = blk_swap(skeleton, 1 << tier)
        after = ()
        if tier == 1:
            mine_maps, other_maps = folds(1, height - 1)
            tail, carried, *climb = call(
                carry_kernel,
                (array(k_half, size),) * (3 if height == 3 else 2),
                (child_leaf, home, away_first, first_mine, first_other, mine_maps),
                6 * k_half * 5 * size * size,
                in_specs=[smem] + [vmem] * 5,
            )
            tails = [tail]
        if tier < height - 2:
            pair = call(
                functools.partial(pair_kernel, tier - 1),
                array(k_half, 2 * size),
                (carried, blk_swap(carried, 1 << tier), mine_maps, other_maps),
                6 * k_half * 4 * size * size,
            )
            tails.append(pair[:, :size])
            carried = pair[:, size:]
        if tier == height - 2:
            if not climb:
                climb = [
                    call(
                        functools.partial(climb_kernel, tier - 1),
                        array(k_half, size),
                        (carried, mine_maps),
                        6 * k_half * size * size,
                    )
                ]
            far = blk_swap(climb[0], 2 << tier)
            after = (climb[0],)
        if tier == height - 1:
            top_mine, top_other = folds(height - 1, height)
            relay = call(relay_kernel, array(2, k_half, size), (carried, far), k_half * size)
            relayed = blk_swap(relay, 1 << (tier - 1))
            tails = call(
                functools.partial(top_kernel, tier - 2),
                array(height + 1, k_half, size),
                (jnp.stack(tails), relay, relayed, mine_maps, other_maps, top_mine, top_other),
                6 * k_half * 6 * size * size,
            )
            solved, leaf_map = call(
                functools.partial(leaf_solve_kernel, height - 2),
                (array(2, half, size), array(k_rows, size)),
                (*early, *leaf_args),
                6 * (rows + k_rows) * leaf_size * size,
                in_specs=[vmem] * 2 + [smem] + [vmem] * 3,
            )
            after = (solved,)
        last = tier == height - 1
        if last:
            mine_maps, other_maps = top_mine, top_other
        index = 0 if last else tier - 1
        base = call(
            functools.partial(base_kernel, index),
            array(half, 2 * size),
            (skeleton, mine_maps),
            merge_flops,
        )
        leaf_args = (child_leaf, right_here, coupling_here, leaf_solve_map)
        kernel = functools.partial(last_merge_kernel if last else merge_kernel, index)
        args, specs = (base, away, other_maps), [vmem] * 3
        shapes = (array(half, size), array(part if last else half, size))
        if last:
            args, specs = args + (tails,), specs + [vmem]
        if tier == height - 2:
            kernel = functools.partial(late_merge_kernel, index, height - 2)
            args, specs = args + leaf_args, specs + [smem] + [vmem] * 3
            shapes += (array(2, half, size), array(k_rows, size))
        node, skeleton, *early = call(
            kernel, shapes, args + after, merge_flops, in_specs=specs + [anywhere] * len(after)
        )
        nodes.append(node)
    received = [level_swap(skeleton, mask) for mask in range(1, fronts)]
    roots = [skeleton, blk_swap(skeleton, 1)]
    for value in received:
        roots += [value, blk_swap(value, 1)]
    pairs = []
    for value in nodes:
        pairs += [value, blk_swap(value, 1)]
    shapes = (array(rows, size), array(height, rows, size), array(rows, size))
    early = call(
        functools.partial(early_kernel, height),
        shapes,
        (child_leaf, solved, *pairs, *roots[:2]),
        rows * size,
        in_specs=[smem] + [vmem] * (len(pairs) + 3),
        out_specs=(hbm,) * 3,
        scratch_shapes=[pltpu.SemaphoreType.DMA((2, height + 2))],
    )
    wide_maps = call(
        maps_kernel,
        jax.ShapeDtypeStruct((3 * k_rows, size * (height + 2)), bf16),
        (leaf_map, tails, blk_swap(tails, 1)),
        k_rows * size * (height + 2) * 4,
        scratch_shapes=[pltpu.VMEM((k_rows, size * (height + 2)), f32)],
    )
    args = (child_leaf, solved, wide_maps, *pairs, *roots)
    leaf_out, node_out, root_out = call(
        functools.partial(final_kernel, fronts, height),
        shapes,
        (*args, *early),
        6 * rows * size * size * (height + 2),
        in_specs=[smem] + [vmem] * (len(args) - 1) + [hbm] * 3,
        out_specs=(hbm,) * 3,
        aliases={len(args) + i: i for i in range(3)},
        scratch_shapes=[
            pltpu.VMEM((fronts, k_rows, size), f32),
            pltpu.VMEM((rows, 3 * size), bf16),
            pltpu.VMEM((4, height + 2, rows // 4, size), f32),
            pltpu.SemaphoreType.DMA((4, height + 2)),
        ],
    )
    return (leaf_out[None], node_out[None, None], root_out[None])


def solution(mesh):
    in_specs = (
        P("level", None, "blk"),
        P("level", "blk", None),
        P("level", "blk", None),
        P("level", "blk", None),
        P("level", "blk", None, None, None),
        P("level", "blk", None, None, None),
        P("level", "blk", None, None, None),
        P("level", None, None),
        P("level"),
    )
    out_specs = (
        P("level", None, "blk"),
        P("level", "blk", None, None, None),
        P("level", None, None),
    )

    return jax.shard_map(shards, mesh=mesh, in_specs=in_specs, out_specs=out_specs, check_vma=False)
```
